32 devices in a mesh: grp: 2 (over y), seq: 4 (over z), head: 2 (over x), hold: 2 (over core).
Axes of the slice: x: 2, y: 2, z: 4, core: 2. Of those that a mesh axis runs over, the one named last changes fastest.
Arguments:
- meet_span: int32 [2], P('grp'), parts along dimension 0, may hold values from 2 to 6
- span_map: int32 [16], P('grp'), parts along dimension 0, may hold values from 0 to 7, each once
- hidden: bfloat16 [4096, 8192], P(('grp', 'seq')), parts along dimension 0, may hold values from -6 to 6
- w_query: bfloat16 [8192, 8, 512], P('seq', ('head', 'hold')), may hold values from -0.0625 to 0.0625
- w_keyval: bfloat16 [8192, 8, 256], P('seq', ('head', 'hold')), may hold values from -0.0625 to 0.0625
- stored_kv: bfloat16 [4096, 8, 256], P(('grp', 'seq'), ('head', 'hold')), parts along dimension 0, may hold values from -650 to 650, as said below
Outputs:
- attended: bfloat16 [4096, 8, 512], P(('grp', 'seq'), ('head', 'hold')), parts along dimension 0
- kv_cache: bfloat16 [4096, 8, 256], P(('grp', 'seq'), ('head', 'hold')), parts along dimension 0
The draws below stay inside these ranges and needn't reach their ends.
There are 2 independent parts, one for each index of `grp`. The reference program is written for one: setup_inputs(seed, part) draws one part's arguments, and reference() takes and returns one part's arrays. A program takes and returns all parts, laid end to end along the dimension named above; an argument that names none is the same for every part. Nothing has to cross between parts.
Inputs may be any that keep to these rules, and one draw needn't show every extreme that they name: `stored_kv`: keys may be large on some rows.
All inputs are finite; a program needn't handle non-finite values.
Results may differ from the reference program's by a relative error of at most 0.012.
Values may be sent and summed in bfloat16 or wider, within the bound.
No kernel may reach another device: no remote copies, remote signals or barrier semaphores. Data moves between devices by JAX's collectives and lax.ppermute only.
A program may use at most 128 MiB of HBM per device.

```python
import jax
import jax.numpy as jnp
from jax import lax

D = 8192
HD = 128
KVH = 8
QPK = 4
CH = 256
NCH = 8
TOKENS = 2048


def draw_stored_kv(key, part):
    key_one = jax.random.fold_in(jax.random.fold_in(key, 7321), 0)
    base_draw = jnp.clip(jax.random.normal(key_one, (NCH * CH, KVH, 2 * HD), jnp.float32), -6.0, 6.0)
    return base_draw.astype(jnp.bfloat16)


def levels(key, dims, cuts, low, high):
    level = 1.0
    for axis_at, blocks in cuts:
        heights = jax.random.uniform(jax.random.fold_in(jax.random.fold_in(key, 6), axis_at), (blocks,), jnp.float32, low / len(cuts), high / len(cuts))
        level = level * jnp.repeat(jnp.exp(heights), dims[axis_at] // blocks).reshape((-1,) + (1,) * (len(dims) - 1 - axis_at))
    return level


def scatter_about(own_key, extent, deviation, reach, pieces=(), kind=jnp.bfloat16):
    values = deviation * jax.random.normal(own_key, extent, jnp.float32)
    if pieces:
        values = values * levels(own_key, extent, pieces, -0.22, 0.18)
    return jnp.clip(values, -reach, reach).astype(kind)


def setup_inputs(seed: int = 0, part: int = 0) -> dict:
    seeds = jax.random.split(jax.random.key(seed), 7)
    part_splits = jax.random.split(jax.random.fold_in(seeds[6], part), 7)
    meet_span = jax.random.randint(part_splits[0], (1,), NCH // 4, 3 * NCH // 4 + 1).astype(jnp.int32)
    span_map = jax.random.permutation(part_splits[1], NCH).astype(jnp.int32)
    hidden = scatter_about(part_splits[2], (TOKENS, D), 1.0, 6.0, ((0, 4),))
    w_query = scatter_about(seeds[3], (D, KVH, QPK * HD), D ** -0.5, 0.0625, ((0, 4), (1, 4)))
    w_keyval = scatter_about(seeds[4], (D, KVH, 2 * HD), D ** -0.5, 0.0625, ((0, 4), (1, 4)))
    stored_kv = draw_stored_kv(jax.random.fold_in(jax.random.fold_in(seeds[6], part), 71), part)
    return dict(meet_span=meet_span, span_map=span_map, hidden=hidden, w_query=w_query, w_keyval=w_keyval, stored_kv=stored_kv)


theta_base = 500000.0


def rotate(values, positions):
    half_width = values.shape[-1] // 2
    frequency = theta_base ** (-(jnp.arange(half_width, dtype=jnp.float32) * 2.0) / values.shape[-1])
    angles = positions.astype(jnp.float32)[:, None] * frequency[None, :]
    bcast_shape = (positions.shape[0],) + (1,) * (values.ndim - 2) + (half_width,)
    cosine = jnp.cos(angles).reshape(bcast_shape)
    sine_part = jnp.sin(angles).reshape(bcast_shape)
    lower_half = values[..., :half_width]
    upper_half = values[..., half_width:]
    return jnp.concatenate([lower_half * cosine - upper_half * sine_part, upper_half * cosine + lower_half * sine_part], -1)


def reference(meet_span, span_map, hidden, w_query, w_keyval, stored_kv):
    row_total = hidden.shape[0]
    features = hidden.shape[1]
    span_count = span_map.shape[0]
    span_len = row_total // span_count
    head_count = w_query.shape[1]
    head_width = stored_kv.shape[2] // 2
    group_size = w_query.shape[2] // head_width
    row_ids = jnp.arange(row_total, dtype=jnp.int32)
    row_span = span_map[row_ids // span_len]
    positions = (row_span * span_len + row_ids % span_len).astype(jnp.int32)
    computed = (row_span < meet_span[0]) | (row_span == span_count - 1)
    query_raw = jnp.dot(hidden, w_query.reshape(features, -1), preferred_element_type=jnp.float32)
    query_raw = query_raw.reshape(row_total, head_count, group_size, head_width)
    queries = rotate(query_raw, positions).astype(jnp.bfloat16)
    keyval_raw = jnp.dot(hidden, w_keyval.reshape(features, -1), preferred_element_type=jnp.float32)
    keyval_raw = keyval_raw.reshape(row_total, head_count, 2 * head_width)
    rotated = rotate(keyval_raw[..., :head_width], positions)
    recomputed = jnp.concatenate([rotated, keyval_raw[..., head_width:]], -1).astype(jnp.bfloat16)
    full_cache = jnp.where(computed[:, None, None], recomputed, stored_kv)
    cache_keys = full_cache[..., :head_width].astype(jnp.float32)
    cache_values = full_cache[..., head_width:].astype(jnp.float32)
    score_scale = head_width ** -0.5

    def one_span(span_index):
        span_queries = lax.dynamic_slice_in_dim(queries, span_index * span_len, span_len, 0).astype(jnp.float32)
        query_pos = lax.dynamic_slice_in_dim(positions, span_index * span_len, span_len, 0)
        scores = jnp.einsum('ckgd,nkd->kgcn', span_queries, cache_keys) * score_scale
        allowed = positions[None, None, None, :] <= query_pos[None, None, :, None]
        scores = jnp.where(allowed, scores, -jnp.inf)
        row_max = scores.max(-1, keepdims=True)
        weights = jnp.where(allowed, jnp.exp(scores - row_max), 0.0)
        numerator = jnp.einsum('kgcn,nkd->kgcd', weights.astype(jnp.bfloat16).astype(jnp.float32), cache_values)
        result = numerator / weights.sum(-1, keepdims=True)
        return jnp.transpose(result, (2, 0, 1, 3)).reshape(span_len, head_count, group_size * head_width)

    per_span = lax.map(one_span, jnp.arange(span_count, dtype=jnp.int32))
    attended = per_span.reshape(row_total, head_count, group_size * head_width)
    attended = jnp.where(computed[:, None, None], attended, 0.0).astype(jnp.bfloat16)
    return attended, full_cache
```

```python
import functools
import math

import jax
import jax.numpy as jnp
from jax import lax
from jax.experimental import pallas as pl
from jax.experimental.pallas import tpu as pltpu
from jax.sharding import PartitionSpec as P

CH = 256
theta_base = 500000.0
lowest = -1e30
HIDDEN_BOUND = 6.0
WEIGHT_BOUND = 0.0625


def tables(positions, head_width):
    half = head_width // 2
    frequency = theta_base ** (
        -(jnp.arange(half, dtype=jnp.float32) * 2.0) / head_width
    )
    angles = positions.astype(jnp.float32)[:, None] * frequency[None, :]
    cosine, sine = jnp.cos(angles), jnp.sin(angles)
    return jnp.concatenate([cosine, cosine], -1), jnp.concatenate([-sine, sine], -1)


def attend_kernel(
    span_len, key_spans, group, head_width, scale,
    query_span, live, key_span, raw_ref, cos_ref, sin_ref, kv_ref, out_ref,
    q_s, m_s, l_s, acc_s,
):
    slot = pl.program_id(0)
    my_span = query_span[slot]

    @pl.when(live[slot] == 0)
    def _():
        out_ref[...] = jnp.zeros_like(out_ref)

    @pl.when(live[slot] != 0)
    def _():
        cosine, sine = cos_ref[...], sin_ref[...]
        for g in range(group):
            head = raw_ref[:, g * head_width:(g + 1) * head_width]
            turned = head * cosine + pltpu.roll(head, head_width // 2, 1) * sine
            q_s[g * span_len:(g + 1) * span_len, :] = turned.astype(jnp.bfloat16)
        m_s[...] = jnp.full_like(m_s, lowest)
        l_s[...] = jnp.zeros_like(l_s)
        acc_s[...] = jnp.zeros_like(acc_s)

        def update(start, masked):
            keys = kv_ref[pl.ds(start, span_len), :head_width]
            values = kv_ref[pl.ds(start, span_len), head_width:]
            scores = lax.dot_general(
                keys, q_s[...], (((1,), (1,)), ((), ())),
                preferred_element_type=jnp.float32,
            ) * scale
            if masked:
                key_at = lax.broadcasted_iota(jnp.int32, (span_len, span_len), 0)
                row_at = lax.broadcasted_iota(jnp.int32, (span_len, span_len), 1)
                seen = jnp.concatenate([key_at <= row_at] * group, 1)
                scores = jnp.where(seen, scores, lowest)
            old = m_s[...]
            new = jnp.maximum(old, scores.max(0, keepdims=True))
            weights = jnp.exp(scores - new)
            if masked:
                weights = jnp.where(seen, weights, 0.0)
            shrink = jnp.exp(old - new)
            l_s[...] = l_s[...] * shrink + weights.sum(0, keepdims=True)
            acc_s[...] = acc_s[...] * shrink + lax.dot_general(
                values, weights.astype(jnp.bfloat16), (((0,), (0,)), ((), ())),
                preferred_element_type=jnp.float32,
            )
            m_s[...] = new

        @pl.loop(0, key_spans)
        def _(j):
            start = pl.multiple_of(j * span_len, span_len)

            @pl.when(key_span[j] < my_span)
            def _():
                update(start, False)

            @pl.when(key_span[j] == my_span)
            def _():
                update(start, True)

        result = acc_s[...] / l_s[...]
        for g in range(group):
            out_ref[:, g * head_width:(g + 1) * head_width] = (
                result[:, g * span_len:(g + 1) * span_len].T.astype(out_ref.dtype)
            )


def attend(query_span, live, key_span, raw, cosine, sine, kv, head, head_width, span_len):
    rows, width = raw.shape
    group = width // head_width
    keys = kv.shape[0]
    slots = rows // span_len
    return pl.pallas_call(
        functools.partial(
            attend_kernel, span_len, keys // span_len, group, head_width, head_width ** (-0.5)
        ),
        grid_spec=pltpu.PrefetchScalarGridSpec(
            num_scalar_prefetch=3,
            grid=(slots,),
            in_specs=[
                pl.BlockSpec((span_len, width), lambda s, *_: (s, 0)),
                pl.BlockSpec((span_len, head_width), lambda s, *_: (s, 0)),
                pl.BlockSpec((span_len, head_width), lambda s, *_: (s, 0)),
                pl.BlockSpec((keys, 2 * head_width), lambda s, *_: (0, head)),
            ],
            out_specs=pl.BlockSpec((span_len, width), lambda s, *_: (s, 0)),
            scratch_shapes=[
                pltpu.VMEM((group * span_len, head_width), jnp.bfloat16),
                pltpu.VMEM((1, group * span_len), jnp.float32),
                pltpu.VMEM((1, group * span_len), jnp.float32),
                pltpu.VMEM((head_width, group * span_len), jnp.float32),
            ],
        ),
        out_shape=jax.ShapeDtypeStruct((rows, width), jnp.bfloat16),
        cost_estimate=pl.CostEstimate(
            flops=2 * rows * group * keys * head_width * 2,
            bytes_accessed=rows * width * 6 + keys * 2 * head_width * 2,
            transcendentals=rows * group * keys,
        ),
        name="attend",
    )(query_span, live, key_span, raw, cosine, sine, kv)


def local(planes, xs, cores, meet_span, span_map, hidden, w_query, w_keyval, stored_kv):
    rows, features = hidden.shape
    span_count = span_map.shape[0]
    heads = w_query.shape[1]
    head_width = stored_kv.shape[2] // 2
    width = w_query.shape[2]
    span_len = CH
    slots = rows // span_len
    part = features // planes
    piece = rows // (xs * cores)
    p, x, c = lax.axis_index("seq"), lax.axis_index("head"), lax.axis_index("hold")
    scale = 2.0 ** math.floor(
        math.log2(65504.0 / (features * HIDDEN_BOUND * WEIGHT_BOUND))
    )

    my_spans = lax.dynamic_slice_in_dim(span_map, p * slots, slots, 0)
    offsets = jnp.arange(span_len, dtype=jnp.int32)
    positions = (my_spans[:, None] * span_len + offsets[None, :]).reshape(-1)
    live = (my_spans < meet_span[0]) | (my_spans == span_count - 1)
    cosine, sine = tables(positions, head_width)

    mine = (x * cores + c) * piece

    def share(block, valid):
        got = [block]
        for i in range(1, xs):
            pairs = [
                (q * xs + a, q * xs + (a - i) % xs) for q in valid for a in range(xs)
            ]
            got.append(lax.ppermute(block, ("seq", "head"), pairs))
        half = jnp.concatenate(got, 0)
        out = [half]
        for i in range(1, cores):
            pairs = [
                (q * cores + a, q * cores + (a - i) % cores)
                for q in valid for a in range(cores)
            ]
            out.append(lax.ppermute(half, ("seq", "hold"), pairs))
        return jnp.concatenate(out, 0)

    from_right, from_left = {}, {}
    for k in range(planes - 1, 0, -1):
        for table, sign in ((from_right, 1), (from_left, -1)):
            target = jnp.mod(p - sign * k, planes)
            block = lax.dynamic_slice(hidden, (mine, target * part), (piece, part))
            pairs = [
                (q, q - sign * k) for q in range(planes) if 0 <= q - sign * k < planes
            ]
            table[k] = (lax.ppermute(block, "seq", pairs), [b for _, b in pairs])
    for k in range(planes - 1, 0, -1):
        from_right[k] = share(*from_right[k])
        from_left[k] = share(*from_left[k])
    own = lax.dynamic_slice(hidden, (0, p * part), (rows, part))

    def ordered(value):
        out = []
        for a in range(xs):
            for b in range(cores):
                at = (jnp.mod(b - c, cores) * xs + jnp.mod(a - x, xs)) * piece
                out.append(lax.dynamic_slice_in_dim(value, at, piece, 0))
        return jnp.concatenate(out, 0)

    def project(weights):
        def step(block, arrived):
            total = jnp.dot(block, weights, preferred_element_type=jnp.float32) * scale
            if arrived is not None:
                total = total + arrived.astype(jnp.float32)
            return total.astype(jnp.float16)

        right = left = None
        for k in range(planes - 1, 0, -1):
            send = step(from_right[k], right)
            right = lax.ppermute(send, "seq", [(q, q + 1) for q in range(planes - k)])
            send = step(from_left[k], left)
            left = lax.ppermute(send, "seq", [(q + 1, q) for q in range(k - 1, planes - 1)])
        total = jnp.dot(own, weights, preferred_element_type=jnp.float32)
        if planes > 1:
            others = ordered(right).astype(jnp.float32) + ordered(left).astype(jnp.float32)
            total = total + others * (1.0 / scale)
        return total

    keyval_raw = project(w_keyval.reshape(part, -1)).reshape(rows, heads, 2 * head_width)
    keys_raw = keyval_raw[..., :head_width]
    turned = (
        keys_raw * cosine[:, None, :]
        + jnp.roll(keys_raw, head_width // 2, -1) * sine[:, None, :]
    )
    recomputed = jnp.concatenate([turned, keyval_raw[..., head_width:]], -1).astype(jnp.bfloat16)
    computed_rows = jnp.repeat(live, span_len)
    kv_cache = jnp.where(computed_rows[:, None, None], recomputed, stored_kv)

    kv_own = kv_cache.reshape(rows, -1)
    right, left = kv_own, kv_own
    near_left, near_right = {}, {}
    for k in range(1, planes):
        right = lax.ppermute(right, "seq", [(q, q + 1) for q in range(k - 1, planes - 1)])
        left = lax.ppermute(left, "seq", [(q + 1, q) for q in range(planes - k)])
        near_left[k], near_right[k] = right, left
    kv_all = [kv_own]
    for k in range(1, planes):
        kv_all.append(jnp.where(p + k < planes, near_right[k], near_left[planes - k]))
    kv_all = jnp.concatenate(kv_all, 0)
    order = jnp.mod(p + jnp.arange(planes, dtype=jnp.int32), planes)
    key_span = span_map.reshape(planes, slots)[order].reshape(-1)

    live_int = live.astype(jnp.int32)
    outs = []
    for h in range(heads):
        raw = project(w_query[:, h, :])
        outs.append(
            attend(my_spans, live_int, key_span, raw, cosine, sine, kv_all, h, head_width, span_len)
        )
    attended = jnp.stack(outs, 1)
    return attended, kv_cache


def solution(mesh):
    shape = dict(mesh.shape)
    return jax.shard_map(
        functools.partial(local, shape["seq"], shape["head"], shape["hold"]),
        mesh=mesh,
        in_specs=(
            P("grp"),
            P("grp"),
            P(("grp", "seq"), None),
            P("seq", ("head", "hold"), None),
            P("seq", ("head", "hold"), None),
            P(("grp", "seq"), ("head", "hold"), None),
        ),
        out_specs=(
            P(("grp", "seq"), ("head", "hold"), None),
            P(("grp", "seq"), ("head", "hold"), None),
        ),
        check_vma=False,
    )
```

```python
import functools
import math

import jax
import jax.numpy as jnp
from jax import lax
from jax.experimental import pallas as pl
from jax.experimental.pallas import tpu as pltpu
from jax.sharding import PartitionSpec as P

CH = 256
theta_base = 500000.0
lowest = -1e30
HIDDEN_BOUND = 6.0
WEIGHT_BOUND = 0.0625


def tables(positions, head_width):
    half = head_width // 2
    frequency = theta_base ** (
        -(jnp.arange(half, dtype=jnp.float32) * 2.0) / head_width
    )
    angles = positions.astype(jnp.float32)[:, None] * frequency[None, :]
    cosine, sine = jnp.cos(angles), jnp.sin(angles)
    return jnp.concatenate([cosine, cosine], -1), jnp.concatenate([-sine, sine], -1)


def attend_kernel(
    span_len, pieces, group, head_width, factor,
    query_span, live, home, piece_at, *refs,
):
    raw_refs, (cos_ref, sin_ref, kv_ref, out_ref, q_s) = refs[:pieces], refs[pieces:]
    slot = pl.program_id(0)
    my_span = query_span[slot]
    piece = span_len // pieces
    width = group * span_len

    @pl.when(live[slot] == 0)
    def _():
        out_ref[...] = jnp.zeros_like(out_ref)

    @pl.when(live[slot] != 0)
    def _():
        for b, raw_ref in enumerate(raw_refs):
            at = slice(b * piece, (b + 1) * piece)
            cosine, sine = cos_ref[at, :], sin_ref[at, :]
            for g in range(group):
                head = raw_ref[:, g * head_width:(g + 1) * head_width]
                turned = head * cosine + pltpu.roll(head, head_width // 2, 1) * sine
                start = g * span_len + b * piece
                q_s[start:start + piece, :] = turned.astype(jnp.bfloat16)

        def scores_of(start):
            return lax.dot_general(
                kv_ref[pl.ds(start, span_len), :head_width], q_s[...],
                (((1,), (1,)), ((), ())), preferred_element_type=jnp.float32,
            )

        def weigh(start, weights):
            return lax.dot_general(
                kv_ref[pl.ds(start, span_len), head_width:], weights.astype(jnp.bfloat16),
                (((0,), (0,)), ((), ())), preferred_element_type=jnp.float32,
            )

        start = pl.multiple_of(home[my_span] * span_len, span_len)
        key_at = lax.broadcasted_iota(jnp.int32, (span_len, span_len), 0)
        row_at = lax.broadcasted_iota(jnp.int32, (span_len, span_len), 1)
        seen = jnp.concatenate([key_at <= row_at] * group, 1)
        scores = jnp.where(seen, scores_of(start), lowest)
        top = scores.max(0, keepdims=True)
        weights = jnp.exp2((scores - top) * factor)
        weights = jnp.where(seen, weights, 0.0)
        total = weights.sum(0, keepdims=True)
        mixed = weigh(start, weights)

        def step(i, carried):
            top, total, mixed = carried
            start = pl.multiple_of(home[i] * span_len, span_len)
            scores = scores_of(start)
            new = jnp.maximum(top, scores.max(0, keepdims=True))
            weights = jnp.exp2((scores - new) * factor)
            shrink = jnp.exp2((top - new) * factor)
            return (
                new,
                total * shrink + weights.sum(0, keepdims=True),
                mixed * shrink + weigh(start, weights),
            )

        top, total, mixed = lax.fori_loop(0, my_span, step, (top, total, mixed))
        result = mixed / total
        for g in range(group):
            out_ref[:, g * head_width:(g + 1) * head_width] = (
                result[:, g * span_len:(g + 1) * span_len].T.astype(out_ref.dtype)
            )


def attend(query_span, live, home, piece_at, raw, cosine, sine, kv, head, head_width, span_len):
    rows, width = raw.shape
    group = width // head_width
    keys = kv.shape[0]
    slots = rows // span_len
    pieces = piece_at.shape[0] // slots
    piece = span_len // pieces

    def raw_spec(b):
        return pl.BlockSpec(
            (piece, width), lambda s, qs, lv, hm, at: (at[s * pieces + b], 0)
        )

    return pl.pallas_call(
        functools.partial(
            attend_kernel, span_len, pieces, group, head_width,
            head_width ** (-0.5) * math.log2(math.e),
        ),
        grid_spec=pltpu.PrefetchScalarGridSpec(
            num_scalar_prefetch=4,
            grid=(slots,),
            in_specs=[raw_spec(b) for b in range(pieces)] + [
                pl.BlockSpec((span_len, head_width), lambda s, *_: (s, 0)),
                pl.BlockSpec((span_len, head_width), lambda s, *_: (s, 0)),
                pl.BlockSpec((keys, 2 * head_width), lambda s, *_: (0, head)),
            ],
            out_specs=pl.BlockSpec((span_len, width), lambda s, *_: (s, 0)),
            scratch_shapes=[pltpu.VMEM((group * span_len, head_width), jnp.bfloat16)],
        ),
        out_shape=jax.ShapeDtypeStruct((rows, width), jnp.bfloat16),
        cost_estimate=pl.CostEstimate(
            flops=2 * rows * group * keys * head_width * 2,
            bytes_accessed=rows * width * 6 + keys * 2 * head_width * 2,
            transcendentals=rows * group * keys,
        ),
        name="attend",
    )(query_span, live, home, piece_at, *([raw] * pieces), cosine, sine, kv)


def homes(key_span):
    places = jnp.arange(key_span.shape[0], dtype=jnp.int32)
    return jnp.sum(
        jnp.where(key_span[None, :] == places[:, None], places[None, :], 0), 1
    )


def local_line(planes, xs, cores, meet_span, span_map, hidden, w_query, w_keyval, stored_kv):
    rows, features = hidden.shape
    span_count = span_map.shape[0]
    heads = w_query.shape[1]
    head_width = stored_kv.shape[2] // 2
    width = w_query.shape[2]
    span_len = CH
    slots = rows // span_len
    part = features // planes
    piece = rows // (xs * cores)
    p, x, c = lax.axis_index("seq"), lax.axis_index("head"), lax.axis_index("hold")
    scale = 2.0 ** math.floor(
        math.log2(65504.0 / (features * HIDDEN_BOUND * WEIGHT_BOUND))
    )

    my_spans = lax.dynamic_slice_in_dim(span_map, p * slots, slots, 0)
    offsets = jnp.arange(span_len, dtype=jnp.int32)
    positions = (my_spans[:, None] * span_len + offsets[None, :]).reshape(-1)
    live = (my_spans < meet_span[0]) | (my_spans == span_count - 1)
    cosine, sine = tables(positions, head_width)

    mine = (x * cores + c) * piece

    def share(block, valid):
        got = [block]
        for i in range(1, xs):
            pairs = [
                (q * xs + a, q * xs + (a - i) % xs) for q in valid for a in range(xs)
            ]
            got.append(lax.ppermute(block, ("seq", "head"), pairs))
        half = jnp.concatenate(got, 0)
        out = [half]
        for i in range(1, cores):
            pairs = [
                (q * cores + a, q * cores + (a - i) % cores)
                for q in valid for a in range(cores)
            ]
            out.append(lax.ppermute(half, ("seq", "hold"), pairs))
        return jnp.concatenate(out, 0)

    from_right, from_left = {}, {}
    for k in range(planes - 1, 0, -1):
        for table, sign in ((from_right, 1), (from_left, -1)):
            target = jnp.mod(p - sign * k, planes)
            block = lax.dynamic_slice(hidden, (mine, target * part), (piece, part))
            pairs = [
                (q, q - sign * k) for q in range(planes) if 0 <= q - sign * k < planes
            ]
            table[k] = (lax.ppermute(block, "seq", pairs), [b for _, b in pairs])
    for k in range(planes - 1, 0, -1):
        from_right[k] = share(*from_right[k])
        from_left[k] = share(*from_left[k])
    own = lax.dynamic_slice(hidden, (0, p * part), (rows, part))

    def ordered(value):
        out = []
        for a in range(xs):
            for b in range(cores):
                at = (jnp.mod(b - c, cores) * xs + jnp.mod(a - x, xs)) * piece
                out.append(lax.dynamic_slice_in_dim(value, at, piece, 0))
        return jnp.concatenate(out, 0)

    def project(weights):
        def step(block, arrived):
            total = jnp.dot(block, weights, preferred_element_type=jnp.float32) * scale
            if arrived is not None:
                total = total + arrived.astype(jnp.float32)
            return total.astype(jnp.float16)

        right = left = None
        for k in range(planes - 1, 0, -1):
            send = step(from_right[k], right)
            right = lax.ppermute(send, "seq", [(q, q + 1) for q in range(planes - k)])
            send = step(from_left[k], left)
            left = lax.ppermute(send, "seq", [(q + 1, q) for q in range(k - 1, planes - 1)])
        total = jnp.dot(own, weights, preferred_element_type=jnp.float32)
        if planes > 1:
            others = ordered(right).astype(jnp.float32) + ordered(left).astype(jnp.float32)
            total = total + others * (1.0 / scale)
        return total

    keyval_raw = project(w_keyval.reshape(part, -1)).reshape(rows, heads, 2 * head_width)
    keys_raw = keyval_raw[..., :head_width]
    turned = (
        keys_raw * cosine[:, None, :]
        + jnp.roll(keys_raw, head_width // 2, -1) * sine[:, None, :]
    )
    recomputed = jnp.concatenate([turned, keyval_raw[..., head_width:]], -1).astype(jnp.bfloat16)
    computed_rows = jnp.repeat(live, span_len)
    kv_cache = jnp.where(computed_rows[:, None, None], recomputed, stored_kv)

    kv_own = kv_cache.reshape(rows, -1)
    right, left = kv_own, kv_own
    near_left, near_right = {}, {}
    for k in range(1, planes):
        right = lax.ppermute(right, "seq", [(q, q + 1) for q in range(k - 1, planes - 1)])
        left = lax.ppermute(left, "seq", [(q + 1, q) for q in range(planes - k)])
        near_left[k], near_right[k] = right, left
    kv_all = [kv_own]
    for k in range(1, planes):
        kv_all.append(jnp.where(p + k < planes, near_right[k], near_left[planes - k]))
    kv_all = jnp.concatenate(kv_all, 0)
    order = jnp.mod(p + jnp.arange(planes, dtype=jnp.int32), planes)
    key_span = span_map.reshape(planes, slots)[order].reshape(-1)

    home = homes(key_span)
    piece_at = jnp.arange(slots, dtype=jnp.int32)
    live_int = live.astype(jnp.int32)
    outs = []
    for h in range(heads):
        raw = project(w_query[:, h, :])
        outs.append(
            attend(my_spans, live_int, home, piece_at, raw, cosine, sine, kv_all, h, head_width, span_len)
        )
    attended = jnp.stack(outs, 1)
    return attended, kv_cache


def local_four(planes, xs, cores, meet_span, span_map, hidden, w_query, w_keyval, stored_kv):
    rows, features = hidden.shape
    span_count = span_map.shape[0]
    heads = w_query.shape[1]
    head_width = stored_kv.shape[2] // 2
    span_len = CH
    slots = rows // span_len
    part = features // planes
    piece = rows // (xs * cores)
    p, x, c = lax.axis_index("seq"), lax.axis_index("head"), lax.axis_index("hold")
    at_end = (p == 0) | (p == planes - 1)
    scale = 2.0 ** math.floor(
        math.log2(65504.0 / (features * HIDDEN_BOUND * WEIGHT_BOUND))
    )
    inward = [(0, 1), (3, 2)]
    outward = [(1, 0), (2, 3)]
    across = [(1, 2), (2, 1)]

    my_spans = lax.dynamic_slice_in_dim(span_map, p * slots, slots, 0)
    offsets = jnp.arange(span_len, dtype=jnp.int32)
    positions = (my_spans[:, None] * span_len + offsets[None, :]).reshape(-1)
    live = (my_spans < meet_span[0]) | (my_spans == span_count - 1)

    def piece_start(i, j):
        return (jnp.mod(x + i, xs) * cores + jnp.mod(c + j, cores)) * piece

    grid = [(i, j) for i in range(xs) for j in range(cores)]
    piece_at = jnp.stack(
        [jnp.mod(a - x, xs) * cores + jnp.mod(b - c, cores) for a, b in grid]
    ).astype(jnp.int32)

    def share(block):
        got = [block]
        for i in range(1, xs):
            got.append(
                lax.ppermute(block, "head", [(a, (a - i) % xs) for a in range(xs)])
            )
        half = jnp.concatenate(got, 0)
        parts = [half]
        for j in range(1, cores):
            parts.append(
                lax.ppermute(half, "hold", [(a, (a - j) % cores) for a in range(cores)])
            )
        return jnp.concatenate(
            [parts[j][i * piece:(i + 1) * piece] for i, j in grid], 0
        )

    arrived = {}
    for m in (3, 1, 2):
        target = jnp.bitwise_xor(p, m)
        block = lax.dynamic_slice(hidden, (piece_start(0, 0), target * part), (piece, part))
        arrived[m] = lax.ppermute(block, "seq", [(q, q ^ m) for q in range(planes)])
    blocks = {m: share(arrived[m]) for m in (3, 1, 2)}
    own = jnp.concatenate(
        [lax.dynamic_slice(hidden, (piece_start(i, j), p * part), (piece, part)) for i, j in grid], 0
    )

    def project(weights):
        def product(m):
            total = jnp.dot(blocks[m], weights, preferred_element_type=jnp.float32)
            return (total * scale).astype(jnp.float16)

        def plus(a, b):
            return (a.astype(jnp.float32) + b.astype(jnp.float32)).astype(jnp.float16)

        far, mid, near = product(3), product(2), product(1)
        got_far = lax.ppermute(far, "seq", inward)
        got_mid = lax.ppermute(mid, "seq", inward)
        got_near = lax.ppermute(near, "seq", inward)
        got_cross = lax.ppermute(plus(mid, got_far), "seq", across)
        got_pair = lax.ppermute(plus(far, got_mid), "seq", across)
        got_out = lax.ppermute(plus(near, got_cross), "seq", outward)
        others = (
            got_near.astype(jnp.float32) + got_pair.astype(jnp.float32)
            + got_out.astype(jnp.float32)
        )
        total = jnp.dot(own, weights, preferred_element_type=jnp.float32)
        return total + others * (1.0 / scale)

    cosine, sine = tables(positions, head_width)

    keyval_raw = project(w_keyval.reshape(part, -1))
    keyval_raw = jnp.concatenate(
        [
            lax.dynamic_slice_in_dim(keyval_raw, piece_at[i] * piece, piece, 0)
            for i in range(xs * cores)
        ],
        0,
    )
    kv_parts = []
    for h in range(heads):
        keys_raw = keyval_raw[:, 2 * h * head_width:(2 * h + 1) * head_width]
        kv_parts.append(keys_raw * cosine + jnp.roll(keys_raw, head_width // 2, -1) * sine)
        kv_parts.append(keyval_raw[:, (2 * h + 1) * head_width:(2 * h + 2) * head_width])
    recomputed = jnp.concatenate(kv_parts, -1).astype(jnp.bfloat16)
    computed_rows = jnp.repeat(live, span_len)
    kv_own = jnp.where(computed_rows[:, None], recomputed, stored_kv.reshape(rows, -1))
    kv_cache = kv_own.reshape(stored_kv.shape)

    end_kv = lax.ppermute(kv_own, "seq", inward)
    cross_kv = lax.ppermute(kv_own, "seq", across)
    near_kv = lax.ppermute(kv_own, "seq", outward)
    far_kv = lax.ppermute(end_kv, "seq", across)
    rest_kv = lax.ppermute(jnp.concatenate([cross_kv, far_kv], 0), "seq", outward)
    kv_all = jnp.concatenate(
        [
            kv_own,
            jnp.where(at_end, near_kv, end_kv),
            jnp.where(at_end, rest_kv, jnp.concatenate([far_kv, cross_kv], 0)),
        ],
        0,
    )
    order = jnp.bitwise_xor(p, jnp.arange(planes, dtype=jnp.int32))
    key_span = span_map.reshape(planes, slots)[order].reshape(-1)
    home = homes(key_span)

    live_int = live.astype(jnp.int32)
    outs = []
    for h in range(heads):
        raw = project(w_query[:, h, :])
        outs.append(
            attend(
                my_spans, live_int, home, piece_at, raw, cosine, sine, kv_all, h, head_width, span_len
            )
        )
    attended = jnp.stack(outs, 1)
    return attended, kv_cache


def local(planes, xs, cores, *args):
    rows = args[2].shape[0]
    if planes == 4 and (rows // xs) % CH == 0:
        return local_four(planes, xs, cores, *args)
    return local_line(planes, xs, cores, *args)


def solution(mesh):
    shape = dict(mesh.shape)
    return jax.shard_map(
        functools.partial(local, shape["seq"], shape["head"], shape["hold"]),
        mesh=mesh,
        in_specs=(
            P("grp"),
            P("grp"),
            P(("grp", "seq"), None),
            P("seq", ("head", "hold"), None),
            P("seq", ("head", "hold"), None),
            P(("grp", "seq"), ("head", "hold"), None),
        ),
        out_specs=(
            P(("grp", "seq"), ("head", "hold"), None),
            P(("grp", "seq"), ("head", "hold"), None),
        ),
        check_vma=False,
    )
```

```python
import functools
import math

import jax
import jax.numpy as jnp
from jax import lax
from jax.experimental import pallas as pl
from jax.experimental.pallas import tpu as pltpu
from jax.sharding import PartitionSpec as P


CH = 256
theta_base = 500000.0
lowest = -1e30
HIDDEN_BOUND = 6.0
WEIGHT_BOUND = 0.0625


def tables(positions, head_width):
    half = head_width // 2
    frequency = theta_base ** (
        -(jnp.arange(half, dtype=jnp.float32) * 2.0) / head_width
    )
    angles = positions.astype(jnp.float32)[:, None] * frequency[None, :]
    cosine, sine = jnp.cos(angles), jnp.sin(angles)
    return jnp.concatenate([cosine, cosine], -1), jnp.concatenate([-sine, sine], -1)


def attend_kernel(
    span_len, pieces, group, head_width, factor,
    query_span, live, home, piece_at, *refs,
):
    raw_refs, (cos_ref, sin_ref, kv_ref, out_ref, q_s) = refs[:pieces], refs[pieces:]
    slot = pl.program_id(0)
    my_span = query_span[slot]
    piece = span_len // pieces

    @pl.when(live[slot] == 0)
    def _():
        out_ref[...] = jnp.zeros_like(out_ref)

    @pl.when(live[slot] != 0)
    def _():
        for b, raw_ref in enumerate(raw_refs):
            at = slice(b * piece, (b + 1) * piece)
            cosine, sine = cos_ref[at, :], sin_ref[at, :]
            for g in range(group):
                head = raw_ref[:, g * head_width:(g + 1) * head_width]
                turned = head * cosine + pltpu.roll(head, head_width // 2, 1) * sine
                start = g * span_len + b * piece
                q_s[start:start + piece, :] = turned.astype(jnp.bfloat16)

        def scores_of(start):
            return lax.dot_general(
                kv_ref[pl.ds(start, span_len), :head_width], q_s[...],
                (((1,), (1,)), ((), ())), preferred_element_type=jnp.float32,
            )

        def weigh(start, weights):
            return lax.dot_general(
                kv_ref[pl.ds(start, span_len), head_width:], weights.astype(jnp.bfloat16),
                (((0,), (0,)), ((), ())), preferred_element_type=jnp.float32,
            )

        start = pl.multiple_of(home[my_span] * span_len, span_len)
        key_at = lax.broadcasted_iota(jnp.int32, (span_len, span_len), 0)
        row_at = lax.broadcasted_iota(jnp.int32, (span_len, span_len), 1)
        seen = jnp.concatenate([key_at <= row_at] * group, 1)
        scores = jnp.where(seen, scores_of(start), lowest)
        top = scores.max(0, keepdims=True)
        weights = jnp.exp2((scores - top) * factor)
        weights = jnp.where(seen, weights, 0.0)
        total = weights.sum(0, keepdims=True)
        mixed = weigh(start, weights)

        def step(i, carried):
            top, total, mixed = carried
            start = pl.multiple_of(home[i] * span_len, span_len)
            scores = scores_of(start)
            new = jnp.maximum(top, scores.max(0, keepdims=True))
            weights = jnp.exp2((scores - new) * factor)
            shrink = jnp.exp2((top - new) * factor)
            return (
                new,
                total * shrink + weights.sum(0, keepdims=True),
                mixed * shrink + weigh(start, weights),
            )

        top, total, mixed = lax.fori_loop(0, my_span, step, (top, total, mixed))
        result = mixed / total
        for g in range(group):
            out_ref[:, g * head_width:(g + 1) * head_width] = (
                result[:, g * span_len:(g + 1) * span_len].T.astype(out_ref.dtype)
            )


def attend(query_span, live, home, piece_at, raw, cosine, sine, kv, head, head_width, span_len):
    rows, width = raw.shape
    group = width // head_width
    keys = kv.shape[0]
    slots = rows // span_len
    pieces = piece_at.shape[0] // slots
    piece = span_len // pieces

    def raw_spec(b):
        return pl.BlockSpec(
            (piece, width), lambda s, qs, lv, hm, at: (at[s * pieces + b], 0)
        )

    return pl.pallas_call(
        functools.partial(
            attend_kernel, span_len, pieces, group, head_width,
            head_width ** (-0.5) * math.log2(math.e),
        ),
        grid_spec=pltpu.PrefetchScalarGridSpec(
            num_scalar_prefetch=4,
            grid=(slots,),
            in_specs=[raw_spec(b) for b in range(pieces)] + [
                pl.BlockSpec((span_len, head_width), lambda s, *_: (s, 0)),
                pl.BlockSpec((span_len, head_width), lambda s, *_: (s, 0)),
                pl.BlockSpec((keys, 2 * head_width), lambda s, *_: (0, head)),
            ],
            out_specs=pl.BlockSpec((span_len, width), lambda s, *_: (s, 0)),
            scratch_shapes=[pltpu.VMEM((group * span_len, head_width), jnp.bfloat16)],
        ),
        out_shape=jax.ShapeDtypeStruct((rows, width), jnp.bfloat16),
        cost_estimate=pl.CostEstimate(
            flops=2 * rows * group * keys * head_width * 2,
            bytes_accessed=rows * width * 6 + keys * 2 * head_width * 2,
            transcendentals=rows * group * keys,
        ),
        name="attend",
    )(query_span, live, home, piece_at, *([raw] * pieces), cosine, sine, kv)


def homes(key_span):
    places = jnp.arange(key_span.shape[0], dtype=jnp.int32)
    return jnp.sum(
        jnp.where(key_span[None, :] == places[:, None], places[None, :], 0), 1
    )


def local_line(planes, xs, cores, meet_span, span_map, hidden, w_query, w_keyval, stored_kv):
    rows, features = hidden.shape
    span_count = span_map.shape[0]
    heads = w_query.shape[1]
    head_width = stored_kv.shape[2] // 2
    span_len = CH
    slots = rows // span_len
    part = features // planes
    piece = rows // (xs * cores)
    p, x, c = lax.axis_index("seq"), lax.axis_index("head"), lax.axis_index("hold")
    scale = 2.0 ** math.floor(
        math.log2(65504.0 / (features * HIDDEN_BOUND * WEIGHT_BOUND))
    )

    my_spans = lax.dynamic_slice_in_dim(span_map, p * slots, slots, 0)
    offsets = jnp.arange(span_len, dtype=jnp.int32)
    positions = (my_spans[:, None] * span_len + offsets[None, :]).reshape(-1)
    live = (my_spans < meet_span[0]) | (my_spans == span_count - 1)
    cosine, sine = tables(positions, head_width)

    mine = (x * cores + c) * piece

    def share(block, valid):
        got = [block]
        for i in range(1, xs):
            pairs = [
                (q * xs + a, q * xs + (a - i) % xs) for q in valid for a in range(xs)
            ]
            got.append(lax.ppermute(block, ("seq", "head"), pairs))
        half = jnp.concatenate(got, 0)
        out = [half]
        for i in range(1, cores):
            pairs = [
                (q * cores + a, q * cores + (a - i) % cores)
                for q in valid for a in range(cores)
            ]
            out.append(lax.ppermute(half, ("seq", "hold"), pairs))
        return jnp.concatenate(out, 0)

    from_right, from_left = {}, {}
    for k in range(planes - 1, 0, -1):
        for table, sign in ((from_right, 1), (from_left, -1)):
            target = jnp.mod(p - sign * k, planes)
            block = lax.dynamic_slice(hidden, (mine, target * part), (piece, part))
            pairs = [
                (q, q - sign * k) for q in range(planes) if 0 <= q - sign * k < planes
            ]
            table[k] = (lax.ppermute(block, "seq", pairs), [b for _, b in pairs])
    for k in range(planes - 1, 0, -1):
        from_right[k] = share(*from_right[k])
        from_left[k] = share(*from_left[k])
    own = lax.dynamic_slice(hidden, (0, p * part), (rows, part))

    def ordered(value):
        out = []
        for a in range(xs):
            for b in range(cores):
                at = (jnp.mod(b - c, cores) * xs + jnp.mod(a - x, xs)) * piece
                out.append(lax.dynamic_slice_in_dim(value, at, piece, 0))
        return jnp.concatenate(out, 0)

    def project(weights):
        def step(block, arrived):
            total = jnp.dot(block, weights, preferred_element_type=jnp.float32) * scale
            if arrived is not None:
                total = total + arrived.astype(jnp.float32)
            return total.astype(jnp.float16)

        right = left = None
        for k in range(planes - 1, 0, -1):
            send = step(from_right[k], right)
            right = lax.ppermute(send, "seq", [(q, q + 1) for q in range(planes - k)])
            send = step(from_left[k], left)
            left = lax.ppermute(send, "seq", [(q + 1, q) for q in range(k - 1, planes - 1)])
        total = jnp.dot(own, weights, preferred_element_type=jnp.float32)
        if planes > 1:
            others = ordered(right).astype(jnp.float32) + ordered(left).astype(jnp.float32)
            total = total + others * (1.0 / scale)
        return total

    keyval_raw = project(w_keyval.reshape(part, -1)).reshape(rows, heads, 2 * head_width)
    keys_raw = keyval_raw[..., :head_width]
    turned = (
        keys_raw * cosine[:, None, :]
        + jnp.roll(keys_raw, head_width // 2, -1) * sine[:, None, :]
    )
    recomputed = jnp.concatenate([turned, keyval_raw[..., head_width:]], -1).astype(jnp.bfloat16)
    computed_rows = jnp.repeat(live, span_len)
    kv_cache = jnp.where(computed_rows[:, None, None], recomputed, stored_kv)

    kv_own = kv_cache.reshape(rows, -1)
    right, left = kv_own, kv_own
    near_left, near_right = {}, {}
    for k in range(1, planes):
        right = lax.ppermute(right, "seq", [(q, q + 1) for q in range(k - 1, planes - 1)])
        left = lax.ppermute(left, "seq", [(q + 1, q) for q in range(planes - k)])
        near_left[k], near_right[k] = right, left
    kv_all = [kv_own]
    for k in range(1, planes):
        kv_all.append(jnp.where(p + k < planes, near_right[k], near_left[planes - k]))
    kv_all = jnp.concatenate(kv_all, 0)
    order = jnp.mod(p + jnp.arange(planes, dtype=jnp.int32), planes)
    key_span = span_map.reshape(planes, slots)[order].reshape(-1)

    home = homes(key_span)
    piece_at = jnp.arange(slots, dtype=jnp.int32)
    live_int = live.astype(jnp.int32)
    outs = []
    for h in range(heads):
        raw = project(w_query[:, h, :])
        outs.append(
            attend(my_spans, live_int, home, piece_at, raw, cosine, sine, kv_all, h, head_width, span_len)
        )
    attended = jnp.stack(outs, 1)
    return attended, kv_cache


def local_four(planes, xs, cores, meet_span, span_map, hidden, w_query, w_keyval, stored_kv):
    return four_body(planes, xs, cores, meet_span, span_map, hidden, w_query, w_keyval, stored_kv)


def four_body(planes, xs, cores, meet_span, span_map, hidden, w_query, w_keyval, stored_kv):
    rows, features = hidden.shape
    span_count = span_map.shape[0]
    heads, width = w_query.shape[1:]
    head_width = stored_kv.shape[2] // 2
    span_len = CH
    slots = rows // span_len
    part = features // planes
    piece = rows // (xs * cores)
    p, x, c = lax.axis_index("seq"), lax.axis_index("head"), lax.axis_index("hold")
    at_end = (p == 0) | (p == planes - 1)
    scale = 2.0 ** math.floor(
        math.log2(65504.0 / (features * HIDDEN_BOUND * WEIGHT_BOUND))
    )
    ends, inner = (0, 3), (1, 2)
    inward = [(0, 1), (3, 2)]
    outward = [(1, 0), (2, 3)]
    across = [(1, 2), (2, 1)]

    def send(value, pairs, axis="seq"):
        return lax.ppermute(value, axis, pairs)

    my_spans = lax.dynamic_slice_in_dim(span_map, p * slots, slots, 0)
    offsets = jnp.arange(span_len, dtype=jnp.int32)
    positions = (my_spans[:, None] * span_len + offsets[None, :]).reshape(-1)
    live = (my_spans < meet_span[0]) | (my_spans == span_count - 1)

    def piece_start(i, j):
        return (jnp.mod(x + i, xs) * cores + jnp.mod(c + j, cores)) * piece

    grid = [(i, j) for i in range(xs) for j in range(cores)]
    piece_at = jnp.stack(
        [jnp.mod(a - x, xs) * cores + jnp.mod(b - c, cores) for a, b in grid]
    ).astype(jnp.int32)

    def share_x(block, where):
        got = [block]
        for i in range(1, xs):
            pairs = [(q * xs + a, q * xs + (a - i) % xs) for q in where for a in range(xs)]
            got.append(send(block, pairs, ("seq", "head")))
        return jnp.concatenate(got, 0)

    def share_c(half, where):
        parts = [half]
        for j in range(1, cores):
            pairs = [
                (q * cores + a, q * cores + (a - j) % cores) for q in where for a in range(cores)
            ]
            parts.append(send(half, pairs, ("seq", "hold")))
        return jnp.concatenate(
            [parts[j][i * piece:(i + 1) * piece] for i, j in grid], 0
        )

    def slice_for(m):
        return lax.dynamic_slice(
            hidden, (piece_start(0, 0), jnp.bitwise_xor(p, m) * part), (piece, part)
        )

    for_far, for_near, for_mid = slice_for(3), slice_for(1), slice_for(2)
    far_end = send(for_far, [(0, 3), (3, 0)])
    near = send(for_near, [(q, q ^ 1) for q in range(planes)])
    mid_end = send(for_mid, [(1, 3), (2, 0)])
    mid_inner = send(for_mid, [(0, 2), (3, 1)])
    far_inner = send(for_far, across)

    far_half = share_x(far_end, ends)
    cosine, sine = tables(positions, head_width)
    whole_keyval, whole_query = w_keyval.reshape(part, -1), w_query.reshape(part, -1)
    far_half, whole_keyval, whole_query, cosine, sine = lax.optimization_barrier(
        (far_half, whole_keyval, whole_query, cosine, sine)
    )
    far_end = share_c(far_half, ends)
    near = share_c(share_x(near, range(planes)), range(planes))
    mid = jnp.where(at_end, mid_end, mid_inner)
    mid = share_c(share_x(mid, range(planes)), range(planes))
    far_inner = share_c(share_x(far_inner, inner), inner)
    own = jnp.concatenate(
        [lax.dynamic_slice(hidden, (piece_start(i, j), p * part), (piece, part)) for i, j in grid], 0
    )

    def project(weights):
        def product(block):
            total = jnp.dot(block, weights, preferred_element_type=jnp.float32)
            return (total * scale).astype(jnp.float16)

        def plus(a, b):
            return (a.astype(jnp.float32) + b.astype(jnp.float32)).astype(jnp.float16)

        mid_term = product(mid)
        near_term = product(near)
        got_far = send(product(far_end), inward)
        got_near = send(near_term, inward)
        got_mid = send(mid_term, inward)
        got_cross = send(plus(mid_term, got_far), across)
        got_pair = send(plus(product(far_inner), got_mid), across)
        got_out = send(plus(near_term, got_cross), outward)
        late_own, got_out = lax.optimization_barrier((own, got_out))
        others = (
            got_near.astype(jnp.float32) + got_pair.astype(jnp.float32)
            + got_out.astype(jnp.float32)
        )
        total = jnp.dot(late_own, weights, preferred_element_type=jnp.float32)
        return total + others * (1.0 / scale)

    keyval_raw = project(whole_keyval)
    keyval_raw = jnp.concatenate(
        [
            lax.dynamic_slice_in_dim(keyval_raw, piece_at[i] * piece, piece, 0)
            for i in range(xs * cores)
        ],
        0,
    )
    kv_parts = []
    for h in range(heads):
        keys_raw = keyval_raw[:, 2 * h * head_width:(2 * h + 1) * head_width]
        kv_parts.append(keys_raw * cosine + jnp.roll(keys_raw, head_width // 2, -1) * sine)
        kv_parts.append(keyval_raw[:, (2 * h + 1) * head_width:(2 * h + 2) * head_width])
    recomputed = jnp.concatenate(kv_parts, -1).astype(jnp.bfloat16)
    computed_rows = jnp.repeat(live, span_len)
    kv_own = jnp.where(computed_rows[:, None], recomputed, stored_kv.reshape(rows, -1))
    kv_cache = kv_own.reshape(stored_kv.shape)

    end_kv = send(kv_own, inward)
    cross_kv = send(kv_own, across)
    near_kv = send(kv_own, outward)
    far_kv = send(end_kv, across)
    rest_cross = send(cross_kv, outward)
    rest_far = send(far_kv, outward)
    kv_all = jnp.concatenate(
        [
            kv_own,
            jnp.where(at_end, near_kv, end_kv),
            jnp.where(at_end, rest_cross, far_kv),
            jnp.where(at_end, rest_far, cross_kv),
        ],
        0,
    )
    order = jnp.bitwise_xor(p, jnp.arange(planes, dtype=jnp.int32))
    key_span = span_map.reshape(planes, slots)[order].reshape(-1)
    home = homes(key_span)

    live_int = live.astype(jnp.int32)
    outs = []
    for h in range(heads):
        raw = project(whole_query[:, h * width:(h + 1) * width])
        outs.append(
            attend(
                my_spans, live_int, home, piece_at, raw, cosine, sine, kv_all, h, head_width, span_len
            )
        )
    attended = jnp.concatenate(outs, 1).reshape(rows, heads, width)
    return attended, kv_cache


def fits_four(planes, xs, rows, heads):
    return planes == 4 and (rows // xs) % CH == 0 and heads == 2


def local(planes, xs, cores, *args):
    four = fits_four(planes, xs, args[2].shape[0], args[3].shape[1])
    return (local_four if four else local_line)(planes, xs, cores, *args)


def solution(mesh):
    shape = dict(mesh.shape)
    return jax.shard_map(
        functools.partial(local, shape["seq"], shape["head"], shape["hold"]),
        mesh=mesh,
        in_specs=(
            P("grp"),
            P("grp"),
            P(("grp", "seq"), None),
            P("seq", ("head", "hold"), None),
            P("seq", ("head", "hold"), None),
            P(("grp", "seq"), ("head", "hold"), None),
        ),
        out_specs=(
            P(("grp", "seq"), ("head", "hold"), None),
            P(("grp", "seq"), ("head", "hold"), None),
        ),
        check_vma=False,
    )
```

```python
import functools
import math

import jax
import jax.numpy as jnp
from jax import lax
from jax.experimental import pallas as pl
from jax.experimental.pallas import tpu as pltpu
from jax.sharding import PartitionSpec as P


CH = 256
theta_base = 500000.0
lowest = -1e30
HIDDEN_BOUND = 6.0
WEIGHT_BOUND = 0.0625


def tables(positions, head_width):
    half = head_width // 2
    frequency = theta_base ** (
        -(jnp.arange(half, dtype=jnp.float32) * 2.0) / head_width
    )
    angles = positions.astype(jnp.float32)[:, None] * frequency[None, :]
    cosine, sine = jnp.cos(angles), jnp.sin(angles)
    return jnp.concatenate([cosine, cosine], -1), jnp.concatenate([-sine, sine], -1)


def attend_kernel(
    span_len, pieces, group, head_width, factor,
    query_span, live, home, piece_at, *refs,
):
    raw_refs, (cos_ref, sin_ref, kv_ref, out_ref, q_s) = refs[:pieces], refs[pieces:]
    slot = pl.program_id(0)
    my_span = query_span[slot]
    piece = span_len // pieces

    @pl.when(live[slot] == 0)
    def _():
        out_ref[...] = jnp.zeros_like(out_ref)

    @pl.when(live[slot] != 0)
    def _():
        for b, raw_ref in enumerate(raw_refs):
            at = slice(b * piece, (b + 1) * piece)
            cosine, sine = cos_ref[at, :], sin_ref[at, :]
            for g in range(group):
                head = raw_ref[:, g * head_width:(g + 1) * head_width]
                turned = head * cosine + pltpu.roll(head, head_width // 2, 1) * sine
                start = g * span_len + b * piece
                q_s[start:start + piece, :] = turned.astype(jnp.bfloat16)

        def scores_of(start):
            return lax.dot_general(
                kv_ref[pl.ds(start, span_len), :head_width], q_s[...],
                (((1,), (1,)), ((), ())), preferred_element_type=jnp.float32,
            )

        def weigh(start, weights):
            return lax.dot_general(
                kv_ref[pl.ds(start, span_len), head_width:], weights.astype(jnp.bfloat16),
                (((0,), (0,)), ((), ())), preferred_element_type=jnp.float32,
            )

        start = pl.multiple_of(home[my_span] * span_len, span_len)
        key_at = lax.broadcasted_iota(jnp.int32, (span_len, span_len), 0)
        row_at = lax.broadcasted_iota(jnp.int32, (span_len, span_len), 1)
        seen = jnp.concatenate([key_at <= row_at] * group, 1)
        scores = jnp.where(seen, scores_of(start), lowest)
        top = scores.max(0, keepdims=True)
        weights = jnp.exp2((scores - top) * factor)
        weights = jnp.where(seen, weights, 0.0)
        total = weights.sum(0, keepdims=True)
        mixed = weigh(start, weights)

        def step(i, carried):
            top, total, mixed = carried
            start = pl.multiple_of(home[i] * span_len, span_len)
            scores = scores_of(start)
            new = jnp.maximum(top, scores.max(0, keepdims=True))
            weights = jnp.exp2((scores - new) * factor)
            shrink = jnp.exp2((top - new) * factor)
            return (
                new,
                total * shrink + weights.sum(0, keepdims=True),
                mixed * shrink + weigh(start, weights),
            )

        top, total, mixed = lax.fori_loop(0, my_span, step, (top, total, mixed))
        result = mixed / total
        for g in range(group):
            out_ref[:, g * head_width:(g + 1) * head_width] = (
                result[:, g * span_len:(g + 1) * span_len].T.astype(out_ref.dtype)
            )


def attend(query_span, live, home, piece_at, raw, cosine, sine, kv, head, head_width, span_len):
    rows, width = raw.shape
    group = width // head_width
    keys = kv.shape[0]
    slots = rows // span_len
    pieces = piece_at.shape[0] // slots
    piece = span_len // pieces

    def raw_spec(b):
        return pl.BlockSpec(
            (piece, width), lambda s, qs, lv, hm, at: (at[s * pieces + b], 0)
        )

    return pl.pallas_call(
        functools.partial(
            attend_kernel, span_len, pieces, group, head_width,
            head_width ** (-0.5) * math.log2(math.e),
        ),
        grid_spec=pltpu.PrefetchScalarGridSpec(
            num_scalar_prefetch=4,
            grid=(slots,),
            in_specs=[raw_spec(b) for b in range(pieces)] + [
                pl.BlockSpec((span_len, head_width), lambda s, *_: (s, 0)),
                pl.BlockSpec((span_len, head_width), lambda s, *_: (s, 0)),
                pl.BlockSpec((keys, 2 * head_width), lambda s, *_: (0, head)),
            ],
            out_specs=pl.BlockSpec((span_len, width), lambda s, *_: (s, 0)),
            scratch_shapes=[pltpu.VMEM((group * span_len, head_width), jnp.bfloat16)],
        ),
        out_shape=jax.ShapeDtypeStruct((rows, width), jnp.bfloat16),
        cost_estimate=pl.CostEstimate(
            flops=2 * rows * group * keys * head_width * 2,
            bytes_accessed=rows * width * 6 + keys * 2 * head_width * 2,
            transcendentals=rows * group * keys,
        ),
        name="attend",
    )(query_span, live, home, piece_at, *([raw] * pieces), cosine, sine, kv)


def homes(key_span):
    places = jnp.arange(key_span.shape[0], dtype=jnp.int32)
    return jnp.sum(
        jnp.where(key_span[None, :] == places[:, None], places[None, :], 0), 1
    )


def local_line(planes, xs, cores, meet_span, span_map, hidden, w_query, w_keyval, stored_kv):
    rows, features = hidden.shape
    span_count = span_map.shape[0]
    heads = w_query.shape[1]
    head_width = stored_kv.shape[2] // 2
    span_len = CH
    slots = rows // span_len
    part = features // planes
    piece = rows // (xs * cores)
    p, x, c = lax.axis_index("seq"), lax.axis_index("head"), lax.axis_index("hold")
    scale = 2.0 ** math.floor(
        math.log2(65504.0 / (features * HIDDEN_BOUND * WEIGHT_BOUND))
    )

    my_spans = lax.dynamic_slice_in_dim(span_map, p * slots, slots, 0)
    offsets = jnp.arange(span_len, dtype=jnp.int32)
    positions = (my_spans[:, None] * span_len + offsets[None, :]).reshape(-1)
    live = (my_spans < meet_span[0]) | (my_spans == span_count - 1)
    cosine, sine = tables(positions, head_width)

    mine = (x * cores + c) * piece

    def share(block, valid):
        got = [block]
        for i in range(1, xs):
            pairs = [
                (q * xs + a, q * xs + (a - i) % xs) for q in valid for a in range(xs)
            ]
            got.append(lax.ppermute(block, ("seq", "head"), pairs))
        half = jnp.concatenate(got, 0)
        out = [half]
        for i in range(1, cores):
            pairs = [
                (q * cores + a, q * cores + (a - i) % cores)
                for q in valid for a in range(cores)
            ]
            out.append(lax.ppermute(half, ("seq", "hold"), pairs))
        return jnp.concatenate(out, 0)

    from_right, from_left = {}, {}
    for k in range(planes - 1, 0, -1):
        for table, sign in ((from_right, 1), (from_left, -1)):
            target = jnp.mod(p - sign * k, planes)
            block = lax.dynamic_slice(hidden, (mine, target * part), (piece, part))
            pairs = [
                (q, q - sign * k) for q in range(planes) if 0 <= q - sign * k < planes
            ]
            table[k] = (lax.ppermute(block, "seq", pairs), [b for _, b in pairs])
    for k in range(planes - 1, 0, -1):
        from_right[k] = share(*from_right[k])
        from_left[k] = share(*from_left[k])
    own = lax.dynamic_slice(hidden, (0, p * part), (rows, part))

    def ordered(value):
        out = []
        for a in range(xs):
            for b in range(cores):
                at = (jnp.mod(b - c, cores) * xs + jnp.mod(a - x, xs)) * piece
                out.append(lax.dynamic_slice_in_dim(value, at, piece, 0))
        return jnp.concatenate(out, 0)

    def project(weights):
        def step(block, arrived):
            total = jnp.dot(block, weights, preferred_element_type=jnp.float32) * scale
            if arrived is not None:
                total = total + arrived.astype(jnp.float32)
            return total.astype(jnp.float16)

        right = left = None
        for k in range(planes - 1, 0, -1):
            send = step(from_right[k], right)
            right = lax.ppermute(send, "seq", [(q, q + 1) for q in range(planes - k)])
            send = step(from_left[k], left)
            left = lax.ppermute(send, "seq", [(q + 1, q) for q in range(k - 1, planes - 1)])
        total = jnp.dot(own, weights, preferred_element_type=jnp.float32)
        if planes > 1:
            others = ordered(right).astype(jnp.float32) + ordered(left).astype(jnp.float32)
            total = total + others * (1.0 / scale)
        return total

    keyval_raw = project(w_keyval.reshape(part, -1)).reshape(rows, heads, 2 * head_width)
    keys_raw = keyval_raw[..., :head_width]
    turned = (
        keys_raw * cosine[:, None, :]
        + jnp.roll(keys_raw, head_width // 2, -1) * sine[:, None, :]
    )
    recomputed = jnp.concatenate([turned, keyval_raw[..., head_width:]], -1).astype(jnp.bfloat16)
    computed_rows = jnp.repeat(live, span_len)
    kv_cache = jnp.where(computed_rows[:, None, None], recomputed, stored_kv)

    kv_own = kv_cache.reshape(rows, -1)
    right, left = kv_own, kv_own
    near_left, near_right = {}, {}
    for k in range(1, planes):
        right = lax.ppermute(right, "seq", [(q, q + 1) for q in range(k - 1, planes - 1)])
        left = lax.ppermute(left, "seq", [(q + 1, q) for q in range(planes - k)])
        near_left[k], near_right[k] = right, left
    kv_all = [kv_own]
    for k in range(1, planes):
        kv_all.append(jnp.where(p + k < planes, near_right[k], near_left[planes - k]))
    kv_all = jnp.concatenate(kv_all, 0)
    order = jnp.mod(p + jnp.arange(planes, dtype=jnp.int32), planes)
    key_span = span_map.reshape(planes, slots)[order].reshape(-1)

    home = homes(key_span)
    piece_at = jnp.arange(slots, dtype=jnp.int32)
    live_int = live.astype(jnp.int32)
    outs = []
    for h in range(heads):
        raw = project(w_query[:, h, :])
        outs.append(
            attend(my_spans, live_int, home, piece_at, raw, cosine, sine, kv_all, h, head_width, span_len)
        )
    attended = jnp.stack(outs, 1)
    return attended, kv_cache


def local_four(planes, xs, cores, meet_span, span_map, hidden, w_query, w_keyval, stored_kv):
    return four_body(planes, xs, cores, meet_span, span_map, hidden, w_query, w_keyval, stored_kv)


def four_body(planes, xs, cores, meet_span, span_map, hidden, w_query, w_keyval, stored_kv):
    rows, features = hidden.shape
    span_count = span_map.shape[0]
    heads, width = w_query.shape[1:]
    head_width = stored_kv.shape[2] // 2
    span_len = CH
    slots = rows // span_len
    part = features // planes
    piece = rows // (xs * cores)
    p, x, c = lax.axis_index("seq"), lax.axis_index("head"), lax.axis_index("hold")
    at_end = (p == 0) | (p == planes - 1)
    scale = 2.0 ** math.floor(
        math.log2(65504.0 / (features * HIDDEN_BOUND * WEIGHT_BOUND))
    )
    ends, inner = (0, 3), (1, 2)
    inward = [(0, 1), (3, 2)]
    outward = [(1, 0), (2, 3)]
    across = [(1, 2), (2, 1)]

    def send(value, pairs, axis="seq"):
        return lax.ppermute(value, axis, pairs)

    my_spans = lax.dynamic_slice_in_dim(span_map, p * slots, slots, 0)
    offsets = jnp.arange(span_len, dtype=jnp.int32)
    positions = (my_spans[:, None] * span_len + offsets[None, :]).reshape(-1)
    live = (my_spans < meet_span[0]) | (my_spans == span_count - 1)

    def piece_start(i, j):
        return (jnp.mod(x + i, xs) * cores + jnp.mod(c + j, cores)) * piece

    grid = [(i, j) for i in range(xs) for j in range(cores)]
    piece_at = jnp.stack(
        [jnp.mod(a - x, xs) * cores + jnp.mod(b - c, cores) for a, b in grid]
    ).astype(jnp.int32)

    def share_x(block, where):
        got = [block]
        for i in range(1, xs):
            pairs = [(q * xs + a, q * xs + (a - i) % xs) for q in where for a in range(xs)]
            got.append(send(block, pairs, ("seq", "head")))
        return jnp.concatenate(got, 0)

    def share_c(half, where):
        parts = [half]
        for j in range(1, cores):
            pairs = [
                (q * cores + a, q * cores + (a - j) % cores) for q in where for a in range(cores)
            ]
            parts.append(send(half, pairs, ("seq", "hold")))
        return jnp.concatenate(
            [parts[j][i * piece:(i + 1) * piece] for i, j in grid], 0
        )

    def slice_for(m):
        return lax.dynamic_slice(
            hidden, (piece_start(0, 0), jnp.bitwise_xor(p, m) * part), (piece, part)
        )

    for_far, for_near, for_mid = slice_for(3), slice_for(1), slice_for(2)
    far_end = send(for_far, [(0, 3), (3, 0)])
    near = send(for_near, [(q, q ^ 1) for q in range(planes)])
    mid_end = send(for_mid, [(1, 3), (2, 0)])
    mid_inner = send(for_mid, [(0, 2), (3, 1)])
    far_inner = send(for_far, across)

    cosine, sine = tables(positions, head_width)
    whole_keyval, whole_query = w_keyval.reshape(part, -1), w_query.reshape(part, -1)
    far_end, whole_keyval, whole_query, cosine, sine = lax.optimization_barrier(
        (far_end, whole_keyval, whole_query, cosine, sine)
    )
    far_end = share_c(share_x(far_end, ends), ends)
    near = share_c(share_x(near, range(planes)), range(planes))
    mid = jnp.where(at_end, mid_end, mid_inner)
    mid = share_c(share_x(mid, range(planes)), range(planes))
    far_inner = share_c(share_x(far_inner, inner), inner)
    own = jnp.concatenate(
        [lax.dynamic_slice(hidden, (piece_start(i, j), p * part), (piece, part)) for i, j in grid], 0
    )

    def project(weights):
        def product(block):
            total = jnp.dot(block, weights, preferred_element_type=jnp.float32)
            return (total * scale).astype(jnp.float16)

        def plus(a, b):
            return (a.astype(jnp.float32) + b.astype(jnp.float32)).astype(jnp.float16)

        mid_term = product(mid)
        near_term = product(near)
        got_far = send(product(far_end), inward)
        got_near = send(near_term, inward)
        got_mid = send(mid_term, inward)
        got_cross = send(plus(mid_term, got_far), across)
        got_pair = send(plus(product(far_inner), got_mid), across)
        got_out = send(plus(near_term, got_cross), outward)
        late_own, got_out = lax.optimization_barrier((own, got_out))
        others = (
            got_near.astype(jnp.float32) + got_pair.astype(jnp.float32)
            + got_out.astype(jnp.float32)
        )
        total = jnp.dot(late_own, weights, preferred_element_type=jnp.float32)
        return total + others * (1.0 / scale)

    keyval_raw = project(whole_keyval)
    keyval_raw = jnp.concatenate(
        [
            lax.dynamic_slice_in_dim(keyval_raw, piece_at[i] * piece, piece, 0)
            for i in range(xs * cores)
        ],
        0,
    )
    kv_parts = []
    for h in range(heads):
        keys_raw = keyval_raw[:, 2 * h * head_width:(2 * h + 1) * head_width]
        kv_parts.append(keys_raw * cosine + jnp.roll(keys_raw, head_width // 2, -1) * sine)
        kv_parts.append(keyval_raw[:, (2 * h + 1) * head_width:(2 * h + 2) * head_width])
    recomputed = jnp.concatenate(kv_parts, -1).astype(jnp.bfloat16)
    computed_rows = jnp.repeat(live, span_len)
    kv_own = jnp.where(computed_rows[:, None], recomputed, stored_kv.reshape(rows, -1))
    kv_cache = kv_own.reshape(stored_kv.shape)

    end_kv = send(kv_own, inward)
    cross_kv = send(kv_own, across)
    near_kv = send(kv_own, outward)
    far_kv = send(end_kv, across)
    rest_cross = send(cross_kv, outward)
    rest_far = send(far_kv, outward)
    first = jnp.where(at_end, near_kv, end_kv)
    second = jnp.where(at_end, rest_cross, far_kv)
    kv_all = jnp.concatenate(
        [kv_own, first, second, jnp.where(at_end, rest_far, cross_kv)], 0
    )
    order = jnp.bitwise_xor(p, jnp.arange(planes, dtype=jnp.int32))
    key_span = span_map.reshape(planes, slots)[order].reshape(-1)
    home = homes(key_span)

    live_int = live.astype(jnp.int32)
    outs = []
    for h in range(heads):
        raw = project(whole_query[:, h * width:(h + 1) * width])
        outs.append(
            attend(
                my_spans, live_int, home, piece_at, raw, cosine, sine, kv_all, h, head_width,
                span_len,
            )
        )
    attended = jnp.concatenate(outs, 1).reshape(rows, heads, width)
    return attended, kv_cache


def fits_four(planes, xs, rows, heads):
    return planes == 4 and (rows // xs) % CH == 0 and heads == 2


def local(planes, xs, cores, *args):
    four = fits_four(planes, xs, args[2].shape[0], args[3].shape[1])
    return (local_four if four else local_line)(planes, xs, cores, *args)


def solution(mesh):
    shape = dict(mesh.shape)
    return jax.shard_map(
        functools.partial(local, shape["seq"], shape["head"], shape["hold"]),
        mesh=mesh,
        in_specs=(
            P("grp"),
            P("grp"),
            P(("grp", "seq"), None),
            P("seq", ("head", "hold"), None),
            P("seq", ("head", "hold"), None),
            P(("grp", "seq"), ("head", "hold"), None),
        ),
        out_specs=(
            P(("grp", "seq"), ("head", "hold"), None),
            P(("grp", "seq"), ("head", "hold"), None),
        ),
        check_vma=False,
    )
```

```python
import functools
import math

import jax
import jax.numpy as jnp
from jax import lax
from jax.experimental import pallas as pl
from jax.experimental.pallas import tpu as pltpu
from jax.sharding import PartitionSpec as P


CH = 256
theta_base = 500000.0
lowest = -1e30
HIDDEN_BOUND = 6.0
WEIGHT_BOUND = 0.0625


def tables(positions, head_width):
    half = head_width // 2
    frequency = theta_base ** (
        -(jnp.arange(half, dtype=jnp.float32) * 2.0) / head_width
    )
    angles = positions.astype(jnp.float32)[:, None] * frequency[None, :]
    cosine, sine = jnp.cos(angles), jnp.sin(angles)
    return jnp.concatenate([cosine, cosine], -1), jnp.concatenate([-sine, sine], -1)


def attend_kernel(
    span_len, pieces, group, head_width, factor,
    query_span, live, home, piece_at, *refs,
):
    raw_refs, (cos_ref, sin_ref, kv_ref, out_ref, q_s) = refs[:pieces], refs[pieces:]
    slot = pl.program_id(0)
    my_span = query_span[slot]
    piece = span_len // pieces

    @pl.when(live[slot] == 0)
    def _():
        out_ref[...] = jnp.zeros_like(out_ref)

    @pl.when(live[slot] != 0)
    def _():
        for b, raw_ref in enumerate(raw_refs):
            at = slice(b * piece, (b + 1) * piece)
            cosine, sine = cos_ref[at, :], sin_ref[at, :]
            for g in range(group):
                head = raw_ref[:, g * head_width:(g + 1) * head_width]
                turned = head * cosine + pltpu.roll(head, head_width // 2, 1) * sine
                start = g * span_len + b * piece
                q_s[start:start + piece, :] = turned.astype(jnp.bfloat16)

        def scores_of(start):
            return lax.dot_general(
                kv_ref[pl.ds(start, span_len), :head_width], q_s[...],
                (((1,), (1,)), ((), ())), preferred_element_type=jnp.float32,
            )

        def weigh(start, weights):
            return lax.dot_general(
                kv_ref[pl.ds(start, span_len), head_width:], weights.astype(jnp.bfloat16),
                (((0,), (0,)), ((), ())), preferred_element_type=jnp.float32,
            )

        start = pl.multiple_of(home[my_span] * span_len, span_len)
        key_at = lax.broadcasted_iota(jnp.int32, (span_len, span_len), 0)
        row_at = lax.broadcasted_iota(jnp.int32, (span_len, span_len), 1)
        seen = jnp.concatenate([key_at <= row_at] * group, 1)
        scores = jnp.where(seen, scores_of(start), lowest)
        top = scores.max(0, keepdims=True)
        weights = jnp.exp2((scores - top) * factor)
        weights = jnp.where(seen, weights, 0.0)
        total = weights.sum(0, keepdims=True)
        mixed = weigh(start, weights)

        def step(i, carried):
            top, total, mixed = carried
            start = pl.multiple_of(home[i] * span_len, span_len)
            scores = scores_of(start)
            new = jnp.maximum(top, scores.max(0, keepdims=True))
            weights = jnp.exp2((scores - new) * factor)
            shrink = jnp.exp2((top - new) * factor)
            return (
                new,
                total * shrink + weights.sum(0, keepdims=True),
                mixed * shrink + weigh(start, weights),
            )

        top, total, mixed = lax.fori_loop(0, my_span, step, (top, total, mixed))
        result = mixed / total
        for g in range(group):
            out_ref[:, g * head_width:(g + 1) * head_width] = (
                result[:, g * span_len:(g + 1) * span_len].T.astype(out_ref.dtype)
            )


def attend(query_span, live, home, piece_at, raw, cosine, sine, kv, head, head_width, span_len):
    rows, width = raw.shape
    group = width // head_width
    keys = kv.shape[0]
    slots = rows // span_len
    pieces = piece_at.shape[0] // slots
    piece = span_len // pieces

    def raw_spec(b):
        return pl.BlockSpec(
            (piece, width), lambda s, qs, lv, hm, at: (at[s * pieces + b], 0)
        )

    return pl.pallas_call(
        functools.partial(
            attend_kernel, span_len, pieces, group, head_width,
            head_width ** (-0.5) * math.log2(math.e),
        ),
        grid_spec=pltpu.PrefetchScalarGridSpec(
            num_scalar_prefetch=4,
            grid=(slots,),
            in_specs=[raw_spec(b) for b in range(pieces)] + [
                pl.BlockSpec((span_len, head_width), lambda s, *_: (s, 0)),
                pl.BlockSpec((span_len, head_width), lambda s, *_: (s, 0)),
                pl.BlockSpec((keys, 2 * head_width), lambda s, *_: (0, head)),
            ],
            out_specs=pl.BlockSpec((span_len, width), lambda s, *_: (s, 0)),
            scratch_shapes=[pltpu.VMEM((group * span_len, head_width), jnp.bfloat16)],
        ),
        out_shape=jax.ShapeDtypeStruct((rows, width), jnp.bfloat16),
        cost_estimate=pl.CostEstimate(
            flops=2 * rows * group * keys * head_width * 2,
            bytes_accessed=rows * width * 6 + keys * 2 * head_width * 2,
            transcendentals=rows * group * keys,
        ),
        name="attend",
    )(query_span, live, home, piece_at, *([raw] * pieces), cosine, sine, kv)


def homes(key_span):
    places = jnp.arange(key_span.shape[0], dtype=jnp.int32)
    return jnp.sum(
        jnp.where(key_span[None, :] == places[:, None], places[None, :], 0), 1
    )


def local_line(planes, xs, cores, meet_span, span_map, hidden, w_query, w_keyval, stored_kv):
    rows, features = hidden.shape
    span_count = span_map.shape[0]
    heads = w_query.shape[1]
    head_width = stored_kv.shape[2] // 2
    span_len = CH
    slots = rows // span_len
    part = features // planes
    piece = rows // (xs * cores)
    p, x, c = lax.axis_index("seq"), lax.axis_index("head"), lax.axis_index("hold")
    scale = 2.0 ** math.floor(
        math.log2(65504.0 / (features * HIDDEN_BOUND * WEIGHT_BOUND))
    )

    my_spans = lax.dynamic_slice_in_dim(span_map, p * slots, slots, 0)
    offsets = jnp.arange(span_len, dtype=jnp.int32)
    positions = (my_spans[:, None] * span_len + offsets[None, :]).reshape(-1)
    live = (my_spans < meet_span[0]) | (my_spans == span_count - 1)
    cosine, sine = tables(positions, head_width)

    mine = (x * cores + c) * piece

    def share(block, valid):
        got = [block]
        for i in range(1, xs):
            pairs = [
                (q * xs + a, q * xs + (a - i) % xs) for q in valid for a in range(xs)
            ]
            got.append(lax.ppermute(block, ("seq", "head"), pairs))
        half = jnp.concatenate(got, 0)
        out = [half]
        for i in range(1, cores):
            pairs = [
                (q * cores + a, q * cores + (a - i) % cores)
                for q in valid for a in range(cores)
            ]
            out.append(lax.ppermute(half, ("seq", "hold"), pairs))
        return jnp.concatenate(out, 0)

    from_right, from_left = {}, {}
    for k in range(planes - 1, 0, -1):
        for table, sign in ((from_right, 1), (from_left, -1)):
            target = jnp.mod(p - sign * k, planes)
            block = lax.dynamic_slice(hidden, (mine, target * part), (piece, part))
            pairs = [
                (q, q - sign * k) for q in range(planes) if 0 <= q - sign * k < planes
            ]
            table[k] = (lax.ppermute(block, "seq", pairs), [b for _, b in pairs])
    for k in range(planes - 1, 0, -1):
        from_right[k] = share(*from_right[k])
        from_left[k] = share(*from_left[k])
    own = lax.dynamic_slice(hidden, (0, p * part), (rows, part))

    def ordered(value):
        out = []
        for a in range(xs):
            for b in range(cores):
                at = (jnp.mod(b - c, cores) * xs + jnp.mod(a - x, xs)) * piece
                out.append(lax.dynamic_slice_in_dim(value, at, piece, 0))
        return jnp.concatenate(out, 0)

    def project(weights):
        def step(block, arrived):
            total = jnp.dot(block, weights, preferred_element_type=jnp.float32) * scale
            if arrived is not None:
                total = total + arrived.astype(jnp.float32)
            return total.astype(jnp.float16)

        right = left = None
        for k in range(planes - 1, 0, -1):
            send = step(from_right[k], right)
            right = lax.ppermute(send, "seq", [(q, q + 1) for q in range(planes - k)])
            send = step(from_left[k], left)
            left = lax.ppermute(send, "seq", [(q + 1, q) for q in range(k - 1, planes - 1)])
        total = jnp.dot(own, weights, preferred_element_type=jnp.float32)
        if planes > 1:
            others = ordered(right).astype(jnp.float32) + ordered(left).astype(jnp.float32)
            total = total + others * (1.0 / scale)
        return total

    keyval_raw = project(w_keyval.reshape(part, -1)).reshape(rows, heads, 2 * head_width)
    keys_raw = keyval_raw[..., :head_width]
    turned = (
        keys_raw * cosine[:, None, :]
        + jnp.roll(keys_raw, head_width // 2, -1) * sine[:, None, :]
    )
    recomputed = jnp.concatenate([turned, keyval_raw[..., head_width:]], -1).astype(jnp.bfloat16)
    computed_rows = jnp.repeat(live, span_len)
    kv_cache = jnp.where(computed_rows[:, None, None], recomputed, stored_kv)

    kv_own = kv_cache.reshape(rows, -1)
    right, left = kv_own, kv_own
    near_left, near_right = {}, {}
    for k in range(1, planes):
        right = lax.ppermute(right, "seq", [(q, q + 1) for q in range(k - 1, planes - 1)])
        left = lax.ppermute(left, "seq", [(q + 1, q) for q in range(planes - k)])
        near_left[k], near_right[k] = right, left
    kv_all = [kv_own]
    for k in range(1, planes):
        kv_all.append(jnp.where(p + k < planes, near_right[k], near_left[planes - k]))
    kv_all = jnp.concatenate(kv_all, 0)
    order = jnp.mod(p + jnp.arange(planes, dtype=jnp.int32), planes)
    key_span = span_map.reshape(planes, slots)[order].reshape(-1)

    home = homes(key_span)
    piece_at = jnp.arange(slots, dtype=jnp.int32)
    live_int = live.astype(jnp.int32)
    outs = []
    for h in range(heads):
        raw = project(w_query[:, h, :])
        outs.append(
            attend(my_spans, live_int, home, piece_at, raw, cosine, sine, kv_all, h, head_width, span_len)
        )
    attended = jnp.stack(outs, 1)
    return attended, kv_cache


def local_four(planes, xs, cores, meet_span, span_map, hidden, w_query, w_keyval, stored_kv):
    return four_body(planes, xs, cores, meet_span, span_map, hidden, w_query, w_keyval, stored_kv)


def four_body(planes, xs, cores, meet_span, span_map, hidden, w_query, w_keyval, stored_kv):
    rows, features = hidden.shape
    span_count = span_map.shape[0]
    heads, width = w_query.shape[1:]
    head_width = stored_kv.shape[2] // 2
    span_len = CH
    slots = rows // span_len
    part = features // planes
    piece = rows // (xs * cores)
    p, x, c = lax.axis_index("seq"), lax.axis_index("head"), lax.axis_index("hold")
    at_end = (p == 0) | (p == planes - 1)
    scale = 2.0 ** math.floor(
        math.log2(65504.0 / (features * HIDDEN_BOUND * WEIGHT_BOUND))
    )
    ends, inner = (0, 3), (1, 2)
    inward = [(0, 1), (3, 2)]
    outward = [(1, 0), (2, 3)]
    across = [(1, 2), (2, 1)]

    def send(value, pairs, axis="seq"):
        return lax.ppermute(value, axis, pairs)

    my_spans = lax.dynamic_slice_in_dim(span_map, p * slots, slots, 0)
    offsets = jnp.arange(span_len, dtype=jnp.int32)
    positions = (my_spans[:, None] * span_len + offsets[None, :]).reshape(-1)
    live = (my_spans < meet_span[0]) | (my_spans == span_count - 1)

    def piece_start(i, j):
        return (jnp.mod(x + i, xs) * cores + jnp.mod(c + j, cores)) * piece

    grid = [(i, j) for i in range(xs) for j in range(cores)]
    piece_at = jnp.stack(
        [jnp.mod(a - x, xs) * cores + jnp.mod(b - c, cores) for a, b in grid]
    ).astype(jnp.int32)

    def around_x(block, where):
        got = []
        for i in range(1, xs):
            pairs = [(q * xs + a, q * xs + (a - i) % xs) for q in where for a in range(xs)]
            got.append(send(block, pairs, ("seq", "head")))
        return [block] + got

    def share_x(block, where):
        got = around_x(block, where)
        return jnp.concatenate(got, 0)

    def share_c(half, where):
        parts = [half]
        for j in range(1, cores):
            pairs = [
                (q * cores + a, q * cores + (a - j) % cores) for q in where for a in range(cores)
            ]
            parts.append(send(half, pairs, ("seq", "hold")))
        return jnp.concatenate(
            [parts[j][i * piece:(i + 1) * piece] for i, j in grid], 0
        )

    def slice_for(m):
        return lax.dynamic_slice(
            hidden, (piece_start(0, 0), jnp.bitwise_xor(p, m) * part), (piece, part)
        )

    for_far, for_near, for_mid = slice_for(3), slice_for(1), slice_for(2)
    far_end = send(for_far, [(0, 3), (3, 0)])
    near = send(for_near, [(q, q ^ 1) for q in range(planes)])
    mid_end = send(for_mid, [(1, 3), (2, 0)])
    mid_inner = send(for_mid, [(0, 2), (3, 1)])
    far_inner = send(for_far, across)

    own = jnp.concatenate(
        [lax.dynamic_slice(hidden, (piece_start(i, j), p * part), (piece, part)) for i, j in grid], 0
    )
    cosine, sine = tables(positions, head_width)
    whole_keyval, whole_query = w_keyval.reshape(part, -1), w_query.reshape(part, -1)
    far_end, own, whole_keyval, whole_query, cosine, sine = lax.optimization_barrier(
        (far_end, own, whole_keyval, whole_query, cosine, sine)
    )
    far_end = share_c(share_x(far_end, ends), ends)
    near = share_c(share_x(near, range(planes)), range(planes))
    mid_pairs = zip(around_x(mid_end, ends), around_x(mid_inner, inner))
    mid = jnp.concatenate([jnp.where(at_end, e, i) for e, i in mid_pairs], 0)
    mid = share_c(mid, range(planes))
    far_inner = share_c(share_x(far_inner, inner), inner)

    def project(weights):
        def product(block):
            total = jnp.dot(block, weights, preferred_element_type=jnp.float32)
            return (total * scale).astype(jnp.float16)

        def plus(a, b):
            return (a.astype(jnp.float32) + b.astype(jnp.float32)).astype(jnp.float16)

        mid_term = product(mid)
        near_term = product(near)
        got_far = send(product(far_end), inward)
        got_near = send(near_term, inward)
        got_mid = send(mid_term, inward)
        got_cross = send(plus(mid_term, got_far), across)
        pair_term = plus(product(far_inner), got_mid)
        got_pair = send(pair_term, across)
        got_out = send(plus(near_term, got_cross), outward)
        late_own, got_out = lax.optimization_barrier((own, got_out))
        others = (
            got_near.astype(jnp.float32) + got_pair.astype(jnp.float32)
            + got_out.astype(jnp.float32)
        )
        total = jnp.dot(late_own, weights, preferred_element_type=jnp.float32)
        return total + others * (1.0 / scale)

    keyval_raw = project(whole_keyval)
    keyval_raw = jnp.concatenate(
        [
            lax.dynamic_slice_in_dim(keyval_raw, piece_at[i] * piece, piece, 0)
            for i in range(xs * cores)
        ],
        0,
    )
    kv_parts = []
    for h in range(heads):
        keys_raw = keyval_raw[:, 2 * h * head_width:(2 * h + 1) * head_width]
        kv_parts.append(keys_raw * cosine + jnp.roll(keys_raw, head_width // 2, -1) * sine)
        kv_parts.append(keyval_raw[:, (2 * h + 1) * head_width:(2 * h + 2) * head_width])
    recomputed = jnp.concatenate(kv_parts, -1).astype(jnp.bfloat16)
    computed_rows = jnp.repeat(live, span_len)
    kv_own = jnp.where(computed_rows[:, None], recomputed, stored_kv.reshape(rows, -1))
    kv_cache = kv_own.reshape(stored_kv.shape)

    end_kv = send(kv_own, inward)
    cross_kv = send(kv_own, across)
    near_kv = send(kv_own, outward)
    far_kv = send(end_kv, across)
    rest_cross = send(cross_kv, outward)
    rest_far = send(far_kv, outward)
    first = jnp.where(at_end, near_kv, end_kv)
    second = jnp.where(at_end, rest_cross, far_kv)
    kv_all = jnp.concatenate(
        [kv_own, first, second, jnp.where(at_end, rest_far, cross_kv)], 0
    )
    order = jnp.bitwise_xor(p, jnp.arange(planes, dtype=jnp.int32))
    key_span = span_map.reshape(planes, slots)[order].reshape(-1)
    home = homes(key_span)

    live_int = live.astype(jnp.int32)
    outs = []
    for h in range(heads):
        raw = project(whole_query[:, h * width:(h + 1) * width])
        outs.append(
            attend(
                my_spans, live_int, home, piece_at, raw, cosine, sine, kv_all, h, head_width,
                span_len,
            )
        )
    attended = jnp.concatenate(outs, 1).reshape(rows, heads, width)
    return attended, kv_cache


def fits_four(planes, xs, rows, heads):
    return planes == 4 and (rows // xs) % CH == 0 and heads == 2


def local(planes, xs, cores, *args):
    four = fits_four(planes, xs, args[2].shape[0], args[3].shape[1])
    return (local_four if four else local_line)(planes, xs, cores, *args)


def solution(mesh):
    shape = dict(mesh.shape)
    return jax.shard_map(
        functools.partial(local, shape["seq"], shape["head"], shape["hold"]),
        mesh=mesh,
        in_specs=(
            P("grp"),
            P("grp"),
            P(("grp", "seq"), None),
            P("seq", ("head", "hold"), None),
            P("seq", ("head", "hold"), None),
            P(("grp", "seq"), ("head", "hold"), None),
        ),
        out_specs=(
            P(("grp", "seq"), ("head", "hold"), None),
            P(("grp", "seq"), ("head", "hold"), None),
        ),
        check_vma=False,
    )
```

```python
import functools
import math

import jax
import jax.numpy as jnp
from jax import lax
from jax.experimental import pallas as pl
from jax.experimental.pallas import tpu as pltpu
from jax.sharding import PartitionSpec as P


CH = 256
theta_base = 500000.0
lowest = -1e30
HIDDEN_BOUND = 6.0
WEIGHT_BOUND = 0.0625


def tables(positions, head_width):
    half = head_width // 2
    frequency = theta_base ** (
        -(jnp.arange(half, dtype=jnp.float32) * 2.0) / head_width
    )
    angles = positions.astype(jnp.float32)[:, None] * frequency[None, :]
    cosine, sine = jnp.cos(angles), jnp.sin(angles)
    return jnp.concatenate([cosine, cosine], -1), jnp.concatenate([-sine, sine], -1)


def attend_kernel(
    span_len, pieces, group, head_width, factor,
    query_span, live, home, piece_at, *refs,
):
    raw_refs, (cos_ref, sin_ref, kv_ref, out_ref, q_s, top_s, sum_s, mix_s) = (
        refs[:pieces], refs[pieces:],
    )
    slot = pl.program_id(1)
    my_span = query_span[slot]
    piece = span_len // pieces

    @pl.when(live[slot] == 0)
    def _():
        out_ref[...] = jnp.zeros_like(out_ref)

    @pl.when(live[slot] != 0)
    def _():
        for b, raw_ref in enumerate(raw_refs):
            at = slice(b * piece, (b + 1) * piece)
            cosine, sine = cos_ref[at, :], sin_ref[at, :]
            for g in range(group):
                head = raw_ref[:, g * head_width:(g + 1) * head_width]
                turned = head * cosine + pltpu.roll(head, head_width // 2, 1) * sine
                q_s[g, at, :] = turned.astype(jnp.bfloat16)

        def scores_of(start):
            keys = kv_ref[pl.ds(start, span_len), :head_width]
            return [
                lax.dot_general(
                    keys, q_s[g], (((1,), (1,)), ((), ())), preferred_element_type=jnp.float32
                )
                for g in range(group)
            ]

        def weigh(start, weights):
            return lax.dot_general(
                kv_ref[pl.ds(start, span_len), head_width:], weights.astype(jnp.bfloat16),
                (((0,), (0,)), ((), ())), preferred_element_type=jnp.float32,
            )

        start = pl.multiple_of(home[my_span] * span_len, span_len)
        key_at = lax.broadcasted_iota(jnp.int32, (span_len, span_len), 0)
        row_at = lax.broadcasted_iota(jnp.int32, (span_len, span_len), 1)
        seen = key_at <= row_at
        for g, scores in enumerate(scores_of(start)):
            scores = jnp.where(seen, scores, lowest)
            top = scores.max(0, keepdims=True)
            weights = jnp.where(seen, jnp.exp2((scores - top) * factor), 0.0)
            top_s[g] = top
            sum_s[g] = weights.sum(0, keepdims=True)
            mix_s[g] = weigh(start, weights)

        @pl.loop(0, my_span)
        def _(i):
            start = pl.multiple_of(home[i] * span_len, span_len)
            for g, scores in enumerate(scores_of(start)):
                top = top_s[g]
                new = jnp.maximum(top, scores.max(0, keepdims=True))
                weights = jnp.exp2((scores - new) * factor)
                shrink = jnp.exp2((top - new) * factor)
                top_s[g] = new
                sum_s[g] = sum_s[g] * shrink + weights.sum(0, keepdims=True)
                mix_s[g] = mix_s[g] * shrink + weigh(start, weights)

        for g in range(group):
            out_ref[:, g * head_width:(g + 1) * head_width] = (
                (mix_s[g] / sum_s[g]).T.astype(out_ref.dtype)
            )


def attend(query_span, live, home, piece_at, raw, cosine, sine, kv, heads, head_width, span_len):
    rows = raw.shape[0]
    width = raw.shape[1] // heads
    group = width // head_width
    keys = kv.shape[0]
    slots = rows // span_len
    pieces = piece_at.shape[0] // slots
    piece = span_len // pieces

    def raw_spec(b):
        return pl.BlockSpec(
            (piece, width), lambda h, s, qs, lv, hm, at: (at[s * pieces + b], h)
        )

    return pl.pallas_call(
        functools.partial(
            attend_kernel, span_len, pieces, group, head_width,
            head_width ** (-0.5) * math.log2(math.e),
        ),
        grid_spec=pltpu.PrefetchScalarGridSpec(
            num_scalar_prefetch=4,
            grid=(heads, slots),
            in_specs=[raw_spec(b) for b in range(pieces)] + [
                pl.BlockSpec((span_len, head_width), lambda h, s, *_: (s, 0)),
                pl.BlockSpec((span_len, head_width), lambda h, s, *_: (s, 0)),
                pl.BlockSpec((keys, 2 * head_width), lambda h, s, *_: (0, h)),
            ],
            out_specs=pl.BlockSpec((span_len, width), lambda h, s, *_: (s, h)),
            scratch_shapes=[
                pltpu.VMEM((group, span_len, head_width), jnp.bfloat16),
                pltpu.VMEM((group, 1, span_len), jnp.float32),
                pltpu.VMEM((group, 1, span_len), jnp.float32),
                pltpu.VMEM((group, head_width, span_len), jnp.float32),
            ],
        ),
        out_shape=jax.ShapeDtypeStruct(raw.shape, jnp.bfloat16),
        cost_estimate=pl.CostEstimate(
            flops=4 * rows * heads * group * keys * head_width,
            bytes_accessed=rows * heads * width * 6 + keys * heads * 2 * head_width * 2,
            transcendentals=rows * heads * group * keys,
        ),
        name="attend",
    )(query_span, live, home, piece_at, *([raw] * pieces), cosine, sine, kv)


def homes(key_span):
    places = jnp.arange(key_span.shape[0], dtype=jnp.int32)
    return jnp.sum(
        jnp.where(key_span[None, :] == places[:, None], places[None, :], 0), 1
    )


def local_line(planes, xs, cores, meet_span, span_map, hidden, w_query, w_keyval, stored_kv):
    rows, features = hidden.shape
    span_count = span_map.shape[0]
    heads = w_query.shape[1]
    head_width = stored_kv.shape[2] // 2
    span_len = CH
    slots = rows // span_len
    part = features // planes
    piece = rows // (xs * cores)
    p, x, c = lax.axis_index("seq"), lax.axis_index("head"), lax.axis_index("hold")
    scale = 2.0 ** math.floor(
        math.log2(65504.0 / (features * HIDDEN_BOUND * WEIGHT_BOUND))
    )

    my_spans = lax.dynamic_slice_in_dim(span_map, p * slots, slots, 0)
    offsets = jnp.arange(span_len, dtype=jnp.int32)
    positions = (my_spans[:, None] * span_len + offsets[None, :]).reshape(-1)
    live = (my_spans < meet_span[0]) | (my_spans == span_count - 1)
    cosine, sine = tables(positions, head_width)

    mine = (x * cores + c) * piece

    def share(block, valid):
        got = [block]
        for i in range(1, xs):
            pairs = [
                (q * xs + a, q * xs + (a - i) % xs) for q in valid for a in range(xs)
            ]
            got.append(lax.ppermute(block, ("seq", "head"), pairs))
        half = jnp.concatenate(got, 0)
        out = [half]
        for i in range(1, cores):
            pairs = [
                (q * cores + a, q * cores + (a - i) % cores)
                for q in valid for a in range(cores)
            ]
            out.append(lax.ppermute(half, ("seq", "hold"), pairs))
        return jnp.concatenate(out, 0)

    from_right, from_left = {}, {}
    for k in range(planes - 1, 0, -1):
        for table, sign in ((from_right, 1), (from_left, -1)):
            target = jnp.mod(p - sign * k, planes)
            block = lax.dynamic_slice(hidden, (mine, target * part), (piece, part))
            pairs = [
                (q, q - sign * k) for q in range(planes) if 0 <= q - sign * k < planes
            ]
            table[k] = (lax.ppermute(block, "seq", pairs), [b for _, b in pairs])
    for k in range(planes - 1, 0, -1):
        from_right[k] = share(*from_right[k])
        from_left[k] = share(*from_left[k])
    own = lax.dynamic_slice(hidden, (0, p * part), (rows, part))

    def ordered(value):
        out = []
        for a in range(xs):
            for b in range(cores):
                at = (jnp.mod(b - c, cores) * xs + jnp.mod(a - x, xs)) * piece
                out.append(lax.dynamic_slice_in_dim(value, at, piece, 0))
        return jnp.concatenate(out, 0)

    def project(weights):
        def step(block, arrived):
            total = jnp.dot(block, weights, preferred_element_type=jnp.float32) * scale
            if arrived is not None:
                total = total + arrived.astype(jnp.float32)
            return total.astype(jnp.float16)

        right = left = None
        for k in range(planes - 1, 0, -1):
            send = step(from_right[k], right)
            right = lax.ppermute(send, "seq", [(q, q + 1) for q in range(planes - k)])
            send = step(from_left[k], left)
            left = lax.ppermute(send, "seq", [(q + 1, q) for q in range(k - 1, planes - 1)])
        total = jnp.dot(own, weights, preferred_element_type=jnp.float32)
        if planes > 1:
            others = ordered(right).astype(jnp.float32) + ordered(left).astype(jnp.float32)
            total = total + others * (1.0 / scale)
        return total

    keyval_raw = project(w_keyval.reshape(part, -1)).reshape(rows, heads, 2 * head_width)
    keys_raw = keyval_raw[..., :head_width]
    turned = (
        keys_raw * cosine[:, None, :]
        + jnp.roll(keys_raw, head_width // 2, -1) * sine[:, None, :]
    )
    recomputed = jnp.concatenate([turned, keyval_raw[..., head_width:]], -1).astype(jnp.bfloat16)
    computed_rows = jnp.repeat(live, span_len)
    kv_cache = jnp.where(computed_rows[:, None, None], recomputed, stored_kv)

    kv_own = kv_cache.reshape(rows, -1)
    right, left = kv_own, kv_own
    near_left, near_right = {}, {}
    for k in range(1, planes):
        right = lax.ppermute(right, "seq", [(q, q + 1) for q in range(k - 1, planes - 1)])
        left = lax.ppermute(left, "seq", [(q + 1, q) for q in range(planes - k)])
        near_left[k], near_right[k] = right, left
    kv_all = [kv_own]
    for k in range(1, planes):
        kv_all.append(jnp.where(p + k < planes, near_right[k], near_left[planes - k]))
    kv_all = jnp.concatenate(kv_all, 0)
    order = jnp.mod(p + jnp.arange(planes, dtype=jnp.int32), planes)
    key_span = span_map.reshape(planes, slots)[order].reshape(-1)

    home = homes(key_span)
    piece_at = jnp.arange(slots, dtype=jnp.int32)
    raw = jnp.concatenate([project(w_query[:, h, :]) for h in range(heads)], 1)
    attended = attend(
        my_spans, live.astype(jnp.int32), home, piece_at, raw, cosine, sine, kv_all, heads,
        head_width, span_len,
    ).reshape(rows, heads, -1)
    return attended, kv_cache


def local_four(planes, xs, cores, meet_span, span_map, hidden, w_query, w_keyval, stored_kv):
    return four_body(planes, xs, cores, meet_span, span_map, hidden, w_query, w_keyval, stored_kv)


def four_body(planes, xs, cores, meet_span, span_map, hidden, w_query, w_keyval, stored_kv):
    rows, features = hidden.shape
    span_count = span_map.shape[0]
    heads, width = w_query.shape[1:]
    head_width = stored_kv.shape[2] // 2
    span_len = CH
    slots = rows // span_len
    part = features // planes
    piece = rows // (xs * cores)
    p, x, c = lax.axis_index("seq"), lax.axis_index("head"), lax.axis_index("hold")
    at_end = (p == 0) | (p == planes - 1)
    scale = 2.0 ** math.floor(
        math.log2(65504.0 / (features * HIDDEN_BOUND * WEIGHT_BOUND))
    )
    ends, inner = (0, 3), (1, 2)
    inward = [(0, 1), (3, 2)]
    outward = [(1, 0), (2, 3)]
    across = [(1, 2), (2, 1)]

    def send(value, pairs, axis="seq"):
        return lax.ppermute(value, axis, pairs)

    my_spans = lax.dynamic_slice_in_dim(span_map, p * slots, slots, 0)
    offsets = jnp.arange(span_len, dtype=jnp.int32)
    positions = (my_spans[:, None] * span_len + offsets[None, :]).reshape(-1)
    live = (my_spans < meet_span[0]) | (my_spans == span_count - 1)

    def piece_start(i, j):
        return (jnp.mod(x + i, xs) * cores + jnp.mod(c + j, cores)) * piece

    grid = [(i, j) for i in range(xs) for j in range(cores)]
    piece_at = jnp.stack(
        [jnp.mod(a - x, xs) * cores + jnp.mod(b - c, cores) for a, b in grid]
    ).astype(jnp.int32)

    def share_x(block, where):
        got = [block]
        for i in range(1, xs):
            pairs = [(q * xs + a, q * xs + (a - i) % xs) for q in where for a in range(xs)]
            got.append(send(block, pairs, ("seq", "head")))
        return jnp.concatenate(got, 0)

    def share_c(half, where):
        parts = [half]
        for j in range(1, cores):
            pairs = [
                (q * cores + a, q * cores + (a - j) % cores) for q in where for a in range(cores)
            ]
            parts.append(send(half, pairs, ("seq", "hold")))
        return jnp.concatenate(
            [parts[j][i * piece:(i + 1) * piece] for i, j in grid], 0
        )

    def slice_for(m):
        return lax.dynamic_slice(
            hidden, (piece_start(0, 0), jnp.bitwise_xor(p, m) * part), (piece, part)
        )

    for_far, for_near, for_mid = slice_for(3), slice_for(1), slice_for(2)
    far_end = send(for_far, [(0, 3), (3, 0)])
    near = send(for_near, [(q, q ^ 1) for q in range(planes)])
    mid_end = send(for_mid, [(1, 3), (2, 0)])
    mid_inner = send(for_mid, [(0, 2), (3, 1)])
    far_inner = send(for_far, across)

    own = jnp.concatenate(
        [lax.dynamic_slice(hidden, (piece_start(i, j), p * part), (piece, part)) for i, j in grid], 0
    )
    cosine, sine = tables(positions, head_width)
    whole_keyval, whole_query = w_keyval.reshape(part, -1), w_query.reshape(part, -1)
    far_end, own, whole_keyval, whole_query, cosine, sine = lax.optimization_barrier(
        (far_end, own, whole_keyval, whole_query, cosine, sine)
    )
    far_end = share_c(share_x(far_end, ends), ends)
    near = share_c(share_x(near, range(planes)), range(planes))
    mid = jnp.where(at_end, mid_end, mid_inner)
    mid = share_c(share_x(mid, range(planes)), range(planes))
    far_inner = share_c(share_x(far_inner, inner), inner)

    def project(weights):
        def product(block):
            total = jnp.dot(block, weights, preferred_element_type=jnp.float32)
            return (total * scale).astype(jnp.float16)

        def plus(a, b):
            return (a.astype(jnp.float32) + b.astype(jnp.float32)).astype(jnp.float16)

        mid_term = product(mid)
        near_term = product(near)
        got_far = send(product(far_end), inward)
        got_near = send(near_term, inward)
        got_mid = send(mid_term, inward)
        got_cross = send(plus(mid_term, got_far), across)
        pair_term = plus(product(far_inner), got_mid)
        got_pair = send(pair_term, across)
        got_out = send(plus(near_term, got_cross), outward)
        late_own, got_out = lax.optimization_barrier((own, got_out))
        others = (
            got_near.astype(jnp.float32) + got_pair.astype(jnp.float32)
            + got_out.astype(jnp.float32)
        )
        total = jnp.dot(late_own, weights, preferred_element_type=jnp.float32)
        return total + others * (1.0 / scale)

    keyval_raw = project(whole_keyval)
    keyval_raw = jnp.concatenate(
        [
            lax.dynamic_slice_in_dim(keyval_raw, piece_at[i] * piece, piece, 0)
            for i in range(xs * cores)
        ],
        0,
    )
    kv_parts = []
    for h in range(heads):
        keys_raw = keyval_raw[:, 2 * h * head_width:(2 * h + 1) * head_width]
        kv_parts.append(keys_raw * cosine + jnp.roll(keys_raw, head_width // 2, -1) * sine)
        kv_parts.append(keyval_raw[:, (2 * h + 1) * head_width:(2 * h + 2) * head_width])
    recomputed = jnp.concatenate(kv_parts, -1).astype(jnp.bfloat16)
    computed_rows = jnp.repeat(live, span_len)
    kv_own = jnp.where(computed_rows[:, None], recomputed, stored_kv.reshape(rows, -1))
    kv_cache = kv_own.reshape(stored_kv.shape)

    end_kv = send(kv_own, inward)
    cross_kv = send(kv_own, across)
    near_kv = send(kv_own, outward)
    far_kv = send(end_kv, across)
    rest_cross = send(cross_kv, outward)
    rest_far = send(far_kv, outward)
    first = jnp.where(at_end, near_kv, end_kv)
    second = jnp.where(at_end, rest_cross, far_kv)
    kv_all = jnp.concatenate(
        [kv_own, first, second, jnp.where(at_end, rest_far, cross_kv)], 0
    )
    order = jnp.bitwise_xor(p, jnp.arange(planes, dtype=jnp.int32))
    key_span = span_map.reshape(planes, slots)[order].reshape(-1)
    home = homes(key_span)

    raw = project(whole_query)
    attended = attend(
        my_spans, live.astype(jnp.int32), home, piece_at, raw, cosine, sine, kv_all, heads,
        head_width, span_len,
    )
    attended = attended.reshape(rows, heads, width)
    return attended, kv_cache


def fits_four(planes, xs, rows, heads):
    return planes == 4 and (rows // xs) % CH == 0 and heads == 2


def local(planes, xs, cores, *args):
    four = fits_four(planes, xs, args[2].shape[0], args[3].shape[1])
    return (local_four if four else local_line)(planes, xs, cores, *args)


def solution(mesh):
    shape = dict(mesh.shape)
    return jax.shard_map(
        functools.partial(local, shape["seq"], shape["head"], shape["hold"]),
        mesh=mesh,
        in_specs=(
            P("grp"),
            P("grp"),
            P(("grp", "seq"), None),
            P("seq", ("head", "hold"), None),
            P("seq", ("head", "hold"), None),
            P(("grp", "seq"), ("head", "hold"), None),
        ),
        out_specs=(
            P(("grp", "seq"), ("head", "hold"), None),
            P(("grp", "seq"), ("head", "hold"), None),
        ),
        check_vma=False,
    )
```

```python
import functools
import math

import jax
import jax.numpy as jnp
from jax import lax
from jax.experimental import pallas as pl
from jax.experimental.pallas import tpu as pltpu
from jax.sharding import PartitionSpec as P


CH = 256
theta_base = 500000.0
lowest = -1e30
HIDDEN_BOUND = 6.0
WEIGHT_BOUND = 0.0625


def tables(positions, head_width):
    half = head_width // 2
    frequency = theta_base ** (
        -(jnp.arange(half, dtype=jnp.float32) * 2.0) / head_width
    )
    angles = positions.astype(jnp.float32)[:, None] * frequency[None, :]
    cosine, sine = jnp.cos(angles), jnp.sin(angles)
    return jnp.concatenate([cosine, cosine], -1), jnp.concatenate([-sine, sine], -1)


def attend_kernel(
    span_len, pieces, group, head_width, factor,
    query_span, live, home, piece_at, *refs,
):
    raw_refs, (cos_ref, sin_ref, kv_ref, out_ref, q_s, top_s, sum_s, mix_s) = (
        refs[:pieces], refs[pieces:],
    )
    slot = pl.program_id(1)
    my_span = query_span[slot]
    piece = span_len // pieces

    @pl.when(live[slot] == 0)
    def _():
        out_ref[...] = jnp.zeros_like(out_ref)

    @pl.when(live[slot] != 0)
    def _():
        for b, raw_ref in enumerate(raw_refs):
            at = slice(b * piece, (b + 1) * piece)
            cosine, sine = cos_ref[at, :], sin_ref[at, :]
            for g in range(group):
                head = raw_ref[:, g * head_width:(g + 1) * head_width]
                turned = head * cosine + pltpu.roll(head, head_width // 2, 1) * sine
                q_s[g, at, :] = turned.astype(jnp.bfloat16)

        def scores_of(start):
            keys = kv_ref[pl.ds(start, span_len), :head_width]
            return [
                lax.dot_general(
                    keys, q_s[g], (((1,), (1,)), ((), ())), preferred_element_type=jnp.float32
                )
                for g in range(group)
            ]

        def weigh(start, weights):
            return lax.dot_general(
                kv_ref[pl.ds(start, span_len), head_width:], weights.astype(jnp.bfloat16),
                (((0,), (0,)), ((), ())), preferred_element_type=jnp.float32,
            )

        start = pl.multiple_of(home[my_span] * span_len, span_len)
        key_at = lax.broadcasted_iota(jnp.int32, (span_len, span_len), 0)
        row_at = lax.broadcasted_iota(jnp.int32, (span_len, span_len), 1)
        seen = key_at <= row_at
        for g, scores in enumerate(scores_of(start)):
            scores = jnp.where(seen, scores, lowest)
            top = scores.max(0, keepdims=True)
            weights = jnp.where(seen, jnp.exp2((scores - top) * factor), 0.0)
            top_s[g] = top
            sum_s[g] = weights.sum(0, keepdims=True)
            mix_s[g] = weigh(start, weights)

        @pl.loop(0, my_span)
        def _(i):
            start = pl.multiple_of(home[i] * span_len, span_len)
            for g, scores in enumerate(scores_of(start)):
                top = top_s[g]
                new = jnp.maximum(top, scores.max(0, keepdims=True))
                weights = jnp.exp2((scores - new) * factor)
                shrink = jnp.exp2((top - new) * factor)
                top_s[g] = new
                sum_s[g] = sum_s[g] * shrink + weights.sum(0, keepdims=True)
                mix_s[g] = mix_s[g] * shrink + weigh(start, weights)

        for g in range(group):
            out_ref[:, g * head_width:(g + 1) * head_width] = (
                (mix_s[g] / sum_s[g]).T.astype(out_ref.dtype)
            )


def attend(
    query_span, live, home, piece_at, raw, cosine, sine, kv, first, heads, head_width, span_len
):
    rows = raw.shape[0]
    width = raw.shape[1] // heads
    group = width // head_width
    keys = kv.shape[0]
    slots = rows // span_len
    pieces = piece_at.shape[0] // slots
    piece = span_len // pieces

    def raw_spec(b):
        return pl.BlockSpec(
            (piece, width), lambda h, s, qs, lv, hm, at: (at[s * pieces + b], h)
        )

    return pl.pallas_call(
        functools.partial(
            attend_kernel, span_len, pieces, group, head_width,
            head_width ** (-0.5) * math.log2(math.e),
        ),
        grid_spec=pltpu.PrefetchScalarGridSpec(
            num_scalar_prefetch=4,
            grid=(heads, slots),
            in_specs=[raw_spec(b) for b in range(pieces)] + [
                pl.BlockSpec((span_len, head_width), lambda h, s, *_: (s, 0)),
                pl.BlockSpec((span_len, head_width), lambda h, s, *_: (s, 0)),
                pl.BlockSpec((keys, 2 * head_width), lambda h, s, *_: (0, first + h)),
            ],
            out_specs=pl.BlockSpec((span_len, width), lambda h, s, *_: (s, h)),
            scratch_shapes=[
                pltpu.VMEM((group, span_len, head_width), jnp.bfloat16),
                pltpu.VMEM((group, 1, span_len), jnp.float32),
                pltpu.VMEM((group, 1, span_len), jnp.float32),
                pltpu.VMEM((group, head_width, span_len), jnp.float32),
            ],
        ),
        out_shape=jax.ShapeDtypeStruct(raw.shape, jnp.bfloat16),
        cost_estimate=pl.CostEstimate(
            flops=4 * rows * heads * group * keys * head_width,
            bytes_accessed=rows * heads * width * 6 + keys * heads * 2 * head_width * 2,
            transcendentals=rows * heads * group * keys,
        ),
        name="attend",
    )(query_span, live, home, piece_at, *([raw] * pieces), cosine, sine, kv)


def homes(key_span):
    places = jnp.arange(key_span.shape[0], dtype=jnp.int32)
    return jnp.sum(
        jnp.where(key_span[None, :] == places[:, None], places[None, :], 0), 1
    )


def local_line(planes, xs, cores, meet_span, span_map, hidden, w_query, w_keyval, stored_kv):
    rows, features = hidden.shape
    span_count = span_map.shape[0]
    heads = w_query.shape[1]
    head_width = stored_kv.shape[2] // 2
    span_len = CH
    slots = rows // span_len
    part = features // planes
    piece = rows // (xs * cores)
    p, x, c = lax.axis_index("seq"), lax.axis_index("head"), lax.axis_index("hold")
    scale = 2.0 ** math.floor(
        math.log2(65504.0 / (features * HIDDEN_BOUND * WEIGHT_BOUND))
    )

    my_spans = lax.dynamic_slice_in_dim(span_map, p * slots, slots, 0)
    offsets = jnp.arange(span_len, dtype=jnp.int32)
    positions = (my_spans[:, None] * span_len + offsets[None, :]).reshape(-1)
    live = (my_spans < meet_span[0]) | (my_spans == span_count - 1)
    cosine, sine = tables(positions, head_width)

    mine = (x * cores + c) * piece

    def share(block, valid):
        got = [block]
        for i in range(1, xs):
            pairs = [
                (q * xs + a, q * xs + (a - i) % xs) for q in valid for a in range(xs)
            ]
            got.append(lax.ppermute(block, ("seq", "head"), pairs))
        half = jnp.concatenate(got, 0)
        out = [half]
        for i in range(1, cores):
            pairs = [
                (q * cores + a, q * cores + (a - i) % cores)
                for q in valid for a in range(cores)
            ]
            out.append(lax.ppermute(half, ("seq", "hold"), pairs))
        return jnp.concatenate(out, 0)

    from_right, from_left = {}, {}
    for k in range(planes - 1, 0, -1):
        for table, sign in ((from_right, 1), (from_left, -1)):
            target = jnp.mod(p - sign * k, planes)
            block = lax.dynamic_slice(hidden, (mine, target * part), (piece, part))
            pairs = [
                (q, q - sign * k) for q in range(planes) if 0 <= q - sign * k < planes
            ]
            table[k] = (lax.ppermute(block, "seq", pairs), [b for _, b in pairs])
    for k in range(planes - 1, 0, -1):
        from_right[k] = share(*from_right[k])
        from_left[k] = share(*from_left[k])
    own = lax.dynamic_slice(hidden, (0, p * part), (rows, part))

    def ordered(value):
        out = []
        for a in range(xs):
            for b in range(cores):
                at = (jnp.mod(b - c, cores) * xs + jnp.mod(a - x, xs)) * piece
                out.append(lax.dynamic_slice_in_dim(value, at, piece, 0))
        return jnp.concatenate(out, 0)

    def project(weights):
        def step(block, arrived):
            total = jnp.dot(block, weights, preferred_element_type=jnp.float32) * scale
            if arrived is not None:
                total = total + arrived.astype(jnp.float32)
            return total.astype(jnp.float16)

        right = left = None
        for k in range(planes - 1, 0, -1):
            send = step(from_right[k], right)
            right = lax.ppermute(send, "seq", [(q, q + 1) for q in range(planes - k)])
            send = step(from_left[k], left)
            left = lax.ppermute(send, "seq", [(q + 1, q) for q in range(k - 1, planes - 1)])
        total = jnp.dot(own, weights, preferred_element_type=jnp.float32)
        if planes > 1:
            others = ordered(right).astype(jnp.float32) + ordered(left).astype(jnp.float32)
            total = total + others * (1.0 / scale)
        return total

    keyval_raw = project(w_keyval.reshape(part, -1)).reshape(rows, heads, 2 * head_width)
    keys_raw = keyval_raw[..., :head_width]
    turned = (
        keys_raw * cosine[:, None, :]
        + jnp.roll(keys_raw, head_width // 2, -1) * sine[:, None, :]
    )
    recomputed = jnp.concatenate([turned, keyval_raw[..., head_width:]], -1).astype(jnp.bfloat16)
    computed_rows = jnp.repeat(live, span_len)
    kv_cache = jnp.where(computed_rows[:, None, None], recomputed, stored_kv)

    kv_own = kv_cache.reshape(rows, -1)
    right, left = kv_own, kv_own
    near_left, near_right = {}, {}
    for k in range(1, planes):
        right = lax.ppermute(right, "seq", [(q, q + 1) for q in range(k - 1, planes - 1)])
        left = lax.ppermute(left, "seq", [(q + 1, q) for q in range(planes - k)])
        near_left[k], near_right[k] = right, left
    kv_all = [kv_own]
    for k in range(1, planes):
        kv_all.append(jnp.where(p + k < planes, near_right[k], near_left[planes - k]))
    kv_all = jnp.concatenate(kv_all, 0)
    order = jnp.mod(p + jnp.arange(planes, dtype=jnp.int32), planes)
    key_span = span_map.reshape(planes, slots)[order].reshape(-1)

    home = homes(key_span)
    piece_at = jnp.arange(slots, dtype=jnp.int32)
    raw = jnp.concatenate([project(w_query[:, h, :]) for h in range(heads)], 1)
    attended = attend(
        my_spans, live.astype(jnp.int32), home, piece_at, raw, cosine, sine, kv_all, 0, heads,
        head_width, span_len,
    ).reshape(rows, heads, -1)
    return attended, kv_cache


def local_four(planes, xs, cores, meet_span, span_map, hidden, w_query, w_keyval, stored_kv):
    return four_body(planes, xs, cores, meet_span, span_map, hidden, w_query, w_keyval, stored_kv)


def four_body(planes, xs, cores, meet_span, span_map, hidden, w_query, w_keyval, stored_kv):
    rows, features = hidden.shape
    span_count = span_map.shape[0]
    heads, width = w_query.shape[1:]
    head_width = stored_kv.shape[2] // 2
    span_len = CH
    slots = rows // span_len
    part = features // planes
    piece = rows // (xs * cores)
    p, x, c = lax.axis_index("seq"), lax.axis_index("head"), lax.axis_index("hold")
    at_end = (p == 0) | (p == planes - 1)
    scale = 2.0 ** math.floor(
        math.log2(65504.0 / (features * HIDDEN_BOUND * WEIGHT_BOUND))
    )
    ends, inner = (0, 3), (1, 2)
    inward = [(0, 1), (3, 2)]
    outward = [(1, 0), (2, 3)]
    across = [(1, 2), (2, 1)]

    def send(value, pairs, axis="seq"):
        return lax.ppermute(value, axis, pairs)

    my_spans = lax.dynamic_slice_in_dim(span_map, p * slots, slots, 0)
    offsets = jnp.arange(span_len, dtype=jnp.int32)
    positions = (my_spans[:, None] * span_len + offsets[None, :]).reshape(-1)
    live = (my_spans < meet_span[0]) | (my_spans == span_count - 1)

    def piece_start(i, j):
        return (jnp.mod(x + i, xs) * cores + jnp.mod(c + j, cores)) * piece

    grid = [(i, j) for i in range(xs) for j in range(cores)]
    piece_at = jnp.stack(
        [jnp.mod(a - x, xs) * cores + jnp.mod(b - c, cores) for a, b in grid]
    ).astype(jnp.int32)

    def share_x(block, where):
        got = [block]
        for i in range(1, xs):
            pairs = [(q * xs + a, q * xs + (a - i) % xs) for q in where for a in range(xs)]
            got.append(send(block, pairs, ("seq", "head")))
        return jnp.concatenate(got, 0)

    def share_c(half, where):
        parts = [half]
        for j in range(1, cores):
            pairs = [
                (q * cores + a, q * cores + (a - j) % cores) for q in where for a in range(cores)
            ]
            parts.append(send(half, pairs, ("seq", "hold")))
        return jnp.concatenate(
            [parts[j][i * piece:(i + 1) * piece] for i, j in grid], 0
        )

    def slice_for(m):
        return lax.dynamic_slice(
            hidden, (piece_start(0, 0), jnp.bitwise_xor(p, m) * part), (piece, part)
        )

    for_far, for_near, for_mid = slice_for(3), slice_for(1), slice_for(2)
    far_end = send(for_far, [(0, 3), (3, 0)])
    near = send(for_near, [(q, q ^ 1) for q in range(planes)])
    mid_end = send(for_mid, [(1, 3), (2, 0)])
    mid_inner = send(for_mid, [(0, 2), (3, 1)])
    far_inner = send(for_far, across)

    own = jnp.concatenate(
        [lax.dynamic_slice(hidden, (piece_start(i, j), p * part), (piece, part)) for i, j in grid], 0
    )
    cosine, sine = tables(positions, head_width)
    whole_keyval, whole_query = w_keyval.reshape(part, -1), w_query.reshape(part, -1)
    far_end, own, whole_keyval, whole_query, cosine, sine = lax.optimization_barrier(
        (far_end, own, whole_keyval, whole_query, cosine, sine)
    )
    far_end = share_c(share_x(far_end, ends), ends)
    near = share_c(share_x(near, range(planes)), range(planes))
    mid = jnp.where(at_end, mid_end, mid_inner)
    mid = share_c(share_x(mid, range(planes)), range(planes))
    far_inner = share_c(share_x(far_inner, inner), inner)

    def project(weights, splits):
        def product(block, columns=weights):
            total = jnp.dot(block, columns, preferred_element_type=jnp.float32)
            return (total * scale).astype(jnp.float16)

        def plus(a, b):
            return (a.astype(jnp.float32) + b.astype(jnp.float32)).astype(jnp.float16)

        mid_term = product(mid)
        near_term = product(near)
        got_far = send(product(far_end), inward)
        got_near = send(near_term, inward)
        got_mid = send(mid_term, inward)
        got_cross = send(plus(mid_term, got_far), across)
        got_out = send(plus(near_term, got_cross), outward)
        late_own, got_late = lax.optimization_barrier((own, got_out))
        totals = []
        step = weights.shape[1] // splits
        for i in range(splits):
            at = slice(i * step, (i + 1) * step)
            pair_term = plus(product(far_inner, weights[:, at]), got_mid[:, at])
            got_pair = send(pair_term, across)
            others = (
                got_near[:, at].astype(jnp.float32) + got_pair.astype(jnp.float32)
                + got_late[:, at].astype(jnp.float32)
            )
            total = jnp.dot(late_own, weights[:, at], preferred_element_type=jnp.float32)
            totals.append(total + others * (1.0 / scale))
        return totals

    keyval_raw, = project(whole_keyval, 1)
    keyval_raw = jnp.concatenate(
        [
            lax.dynamic_slice_in_dim(keyval_raw, piece_at[i] * piece, piece, 0)
            for i in range(xs * cores)
        ],
        0,
    )
    kv_parts = []
    for h in range(heads):
        keys_raw = keyval_raw[:, 2 * h * head_width:(2 * h + 1) * head_width]
        kv_parts.append(keys_raw * cosine + jnp.roll(keys_raw, head_width // 2, -1) * sine)
        kv_parts.append(keyval_raw[:, (2 * h + 1) * head_width:(2 * h + 2) * head_width])
    recomputed = jnp.concatenate(kv_parts, -1).astype(jnp.bfloat16)
    computed_rows = jnp.repeat(live, span_len)
    kv_own = jnp.where(computed_rows[:, None], recomputed, stored_kv.reshape(rows, -1))
    kv_cache = kv_own.reshape(stored_kv.shape)

    end_kv = send(kv_own, inward)
    cross_kv = send(kv_own, across)
    near_kv = send(kv_own, outward)
    far_kv = send(end_kv, across)
    rest_cross = send(cross_kv, outward)
    rest_far = send(far_kv, outward)
    first = jnp.where(at_end, near_kv, end_kv)
    second = jnp.where(at_end, rest_cross, far_kv)
    kv_all = jnp.concatenate(
        [kv_own, first, second, jnp.where(at_end, rest_far, cross_kv)], 0
    )
    order = jnp.bitwise_xor(p, jnp.arange(planes, dtype=jnp.int32))
    key_span = span_map.reshape(planes, slots)[order].reshape(-1)
    home = homes(key_span)

    live_int = live.astype(jnp.int32)
    outs = []
    for h, raw in enumerate(project(whole_query, heads)):
        outs.append(
            attend(
                my_spans, live_int, home, piece_at, raw, cosine, sine, kv_all, h, 1,
                head_width, span_len,
            )
        )
    attended = jnp.concatenate(outs, 1).reshape(rows, heads, width)
    return attended, kv_cache


def fits_four(planes, xs, rows, heads):
    return planes == 4 and (rows // xs) % CH == 0 and heads == 2


def local(planes, xs, cores, *args):
    four = fits_four(planes, xs, args[2].shape[0], args[3].shape[1])
    return (local_four if four else local_line)(planes, xs, cores, *args)


def solution(mesh):
    shape = dict(mesh.shape)
    return jax.shard_map(
        functools.partial(local, shape["seq"], shape["head"], shape["hold"]),
        mesh=mesh,
        in_specs=(
            P("grp"),
            P("grp"),
            P(("grp", "seq"), None),
            P("seq", ("head", "hold"), None),
            P("seq", ("head", "hold"), None),
            P(("grp", "seq"), ("head", "hold"), None),
        ),
        out_specs=(
            P(("grp", "seq"), ("head", "hold"), None),
            P(("grp", "seq"), ("head", "hold"), None),
        ),
        check_vma=False,
    )
```

```python
import functools
import math

import jax
import jax.numpy as jnp
from jax import lax
from jax.experimental import pallas as pl
from jax.experimental.pallas import tpu as pltpu
from jax.sharding import PartitionSpec as P


CH = 256
theta_base = 500000.0
lowest = -1e30
HIDDEN_BOUND = 6.0
WEIGHT_BOUND = 0.0625


def tables(positions, head_width):
    half = head_width // 2
    frequency = theta_base ** (
        -(jnp.arange(half, dtype=jnp.float32) * 2.0) / head_width
    )
    angles = positions.astype(jnp.float32)[:, None] * frequency[None, :]
    cosine, sine = jnp.cos(angles), jnp.sin(angles)
    return jnp.concatenate([cosine, cosine], -1), jnp.concatenate([-sine, sine], -1)


def attend_kernel(
    span_len, pieces, group, head_width, factor,
    query_span, live, home, piece_at, *refs,
):
    raw_refs, (cos_ref, sin_ref, kv_ref, out_ref, q_s, top_s, sum_s, mix_s) = (
        refs[:pieces], refs[pieces:],
    )
    slot = pl.program_id(1)
    my_span = query_span[slot]
    piece = span_len // pieces

    @pl.when(live[slot] == 0)
    def _():
        out_ref[...] = jnp.zeros_like(out_ref)

    @pl.when(live[slot] != 0)
    def _():
        for b, raw_ref in enumerate(raw_refs):
            at = slice(b * piece, (b + 1) * piece)
            cosine, sine = cos_ref[at, :], sin_ref[at, :]
            for g in range(group):
                head = raw_ref[:, g * head_width:(g + 1) * head_width]
                turned = head * cosine + pltpu.roll(head, head_width // 2, 1) * sine
                q_s[g, at, :] = turned.astype(jnp.bfloat16)

        def scores_of(start):
            keys = kv_ref[pl.ds(start, span_len), :head_width]
            return [
                lax.dot_general(
                    keys, q_s[g], (((1,), (1,)), ((), ())), preferred_element_type=jnp.float32
                )
                for g in range(group)
            ]

        def weigh(start, weights):
            return lax.dot_general(
                kv_ref[pl.ds(start, span_len), head_width:], weights.astype(jnp.bfloat16),
                (((0,), (0,)), ((), ())), preferred_element_type=jnp.float32,
            )

        start = pl.multiple_of(home[my_span] * span_len, span_len)
        key_at = lax.broadcasted_iota(jnp.int32, (span_len, span_len), 0)
        row_at = lax.broadcasted_iota(jnp.int32, (span_len, span_len), 1)
        seen = key_at <= row_at
        for g, scores in enumerate(scores_of(start)):
            scores = jnp.where(seen, scores, lowest)
            top = scores.max(0, keepdims=True)
            weights = jnp.where(seen, jnp.exp2((scores - top) * factor), 0.0)
            top_s[g] = top
            sum_s[g] = weights.sum(0, keepdims=True)
            mix_s[g] = weigh(start, weights)

        @pl.loop(0, my_span)
        def _(i):
            start = pl.multiple_of(home[i] * span_len, span_len)
            for g, scores in enumerate(scores_of(start)):
                top = top_s[g]
                new = jnp.maximum(top, scores.max(0, keepdims=True))
                weights = jnp.exp2((scores - new) * factor)
                shrink = jnp.exp2((top - new) * factor)
                top_s[g] = new
                sum_s[g] = sum_s[g] * shrink + weights.sum(0, keepdims=True)
                mix_s[g] = mix_s[g] * shrink + weigh(start, weights)

        for g in range(group):
            out_ref[:, g * head_width:(g + 1) * head_width] = (
                (mix_s[g] / sum_s[g]).T.astype(out_ref.dtype)
            )


def attend(
    query_span, live, home, piece_at, raw, cosine, sine, kv, first, heads, head_width, span_len
):
    rows = raw.shape[0]
    width = raw.shape[1] // heads
    group = width // head_width
    keys = kv.shape[0]
    slots = rows // span_len
    pieces = piece_at.shape[0] // slots
    piece = span_len // pieces

    def raw_spec(b):
        return pl.BlockSpec(
            (piece, width), lambda h, s, qs, lv, hm, at: (at[s * pieces + b], h)
        )

    return pl.pallas_call(
        functools.partial(
            attend_kernel, span_len, pieces, group, head_width,
            head_width ** (-0.5) * math.log2(math.e),
        ),
        grid_spec=pltpu.PrefetchScalarGridSpec(
            num_scalar_prefetch=4,
            grid=(heads, slots),
            in_specs=[raw_spec(b) for b in range(pieces)] + [
                pl.BlockSpec((span_len, head_width), lambda h, s, *_: (s, 0)),
                pl.BlockSpec((span_len, head_width), lambda h, s, *_: (s, 0)),
                pl.BlockSpec((keys, 2 * head_width), lambda h, s, *_: (0, first + h)),
            ],
            out_specs=pl.BlockSpec((span_len, width), lambda h, s, *_: (s, h)),
            scratch_shapes=[
                pltpu.VMEM((group, span_len, head_width), jnp.bfloat16),
                pltpu.VMEM((group, 1, span_len), jnp.float32),
                pltpu.VMEM((group, 1, span_len), jnp.float32),
                pltpu.VMEM((group, head_width, span_len), jnp.float32),
            ],
        ),
        out_shape=jax.ShapeDtypeStruct(raw.shape, jnp.bfloat16),
        cost_estimate=pl.CostEstimate(
            flops=4 * rows * heads * group * keys * head_width,
            bytes_accessed=rows * heads * width * 6 + keys * heads * 2 * head_width * 2,
            transcendentals=rows * heads * group * keys,
        ),
        name="attend",
    )(query_span, live, home, piece_at, *([raw] * pieces), cosine, sine, kv)


def homes(key_span):
    places = jnp.arange(key_span.shape[0], dtype=jnp.int32)
    return jnp.sum(
        jnp.where(key_span[None, :] == places[:, None], places[None, :], 0), 1
    )


def local_line(planes, xs, cores, meet_span, span_map, hidden, w_query, w_keyval, stored_kv):
    rows, features = hidden.shape
    span_count = span_map.shape[0]
    heads = w_query.shape[1]
    head_width = stored_kv.shape[2] // 2
    span_len = CH
    slots = rows // span_len
    part = features // planes
    piece = rows // (xs * cores)
    p, x, c = lax.axis_index("seq"), lax.axis_index("head"), lax.axis_index("hold")
    scale = 2.0 ** math.floor(
        math.log2(65504.0 / (features * HIDDEN_BOUND * WEIGHT_BOUND))
    )

    my_spans = lax.dynamic_slice_in_dim(span_map, p * slots, slots, 0)
    offsets = jnp.arange(span_len, dtype=jnp.int32)
    positions = (my_spans[:, None] * span_len + offsets[None, :]).reshape(-1)
    live = (my_spans < meet_span[0]) | (my_spans == span_count - 1)
    cosine, sine = tables(positions, head_width)

    mine = (x * cores + c) * piece

    def share(block, valid):
        got = [block]
        for i in range(1, xs):
            pairs = [
                (q * xs + a, q * xs + (a - i) % xs) for q in valid for a in range(xs)
            ]
            got.append(lax.ppermute(block, ("seq", "head"), pairs))
        half = jnp.concatenate(got, 0)
        out = [half]
        for i in range(1, cores):
            pairs = [
                (q * cores + a, q * cores + (a - i) % cores)
                for q in valid for a in range(cores)
            ]
            out.append(lax.ppermute(half, ("seq", "hold"), pairs))
        return jnp.concatenate(out, 0)

    from_right, from_left = {}, {}
    for k in range(planes - 1, 0, -1):
        for table, sign in ((from_right, 1), (from_left, -1)):
            target = jnp.mod(p - sign * k, planes)
            block = lax.dynamic_slice(hidden, (mine, target * part), (piece, part))
            pairs = [
                (q, q - sign * k) for q in range(planes) if 0 <= q - sign * k < planes
            ]
            table[k] = (lax.ppermute(block, "seq", pairs), [b for _, b in pairs])
    for k in range(planes - 1, 0, -1):
        from_right[k] = share(*from_right[k])
        from_left[k] = share(*from_left[k])
    own = lax.dynamic_slice(hidden, (0, p * part), (rows, part))

    def ordered(value):
        out = []
        for a in range(xs):
            for b in range(cores):
                at = (jnp.mod(b - c, cores) * xs + jnp.mod(a - x, xs)) * piece
                out.append(lax.dynamic_slice_in_dim(value, at, piece, 0))
        return jnp.concatenate(out, 0)

    def project(weights):
        def step(block, arrived):
            total = jnp.dot(block, weights, preferred_element_type=jnp.float32) * scale
            if arrived is not None:
                total = total + arrived.astype(jnp.float32)
            return total.astype(jnp.float16)

        right = left = None
        for k in range(planes - 1, 0, -1):
            send = step(from_right[k], right)
            right = lax.ppermute(send, "seq", [(q, q + 1) for q in range(planes - k)])
            send = step(from_left[k], left)
            left = lax.ppermute(send, "seq", [(q + 1, q) for q in range(k - 1, planes - 1)])
        total = jnp.dot(own, weights, preferred_element_type=jnp.float32)
        if planes > 1:
            others = ordered(right).astype(jnp.float32) + ordered(left).astype(jnp.float32)
            total = total + others * (1.0 / scale)
        return total

    keyval_raw = project(w_keyval.reshape(part, -1)).reshape(rows, heads, 2 * head_width)
    keys_raw = keyval_raw[..., :head_width]
    turned = (
        keys_raw * cosine[:, None, :]
        + jnp.roll(keys_raw, head_width // 2, -1) * sine[:, None, :]
    )
    recomputed = jnp.concatenate([turned, keyval_raw[..., head_width:]], -1).astype(jnp.bfloat16)
    computed_rows = jnp.repeat(live, span_len)
    kv_cache = jnp.where(computed_rows[:, None, None], recomputed, stored_kv)

    kv_own = kv_cache.reshape(rows, -1)
    right, left = kv_own, kv_own
    near_left, near_right = {}, {}
    for k in range(1, planes):
        right = lax.ppermute(right, "seq", [(q, q + 1) for q in range(k - 1, planes - 1)])
        left = lax.ppermute(left, "seq", [(q + 1, q) for q in range(planes - k)])
        near_left[k], near_right[k] = right, left
    kv_all = [kv_own]
    for k in range(1, planes):
        kv_all.append(jnp.where(p + k < planes, near_right[k], near_left[planes - k]))
    kv_all = jnp.concatenate(kv_all, 0)
    order = jnp.mod(p + jnp.arange(planes, dtype=jnp.int32), planes)
    key_span = span_map.reshape(planes, slots)[order].reshape(-1)

    home = homes(key_span)
    piece_at = jnp.arange(slots, dtype=jnp.int32)
    raw = jnp.concatenate([project(w_query[:, h, :]) for h in range(heads)], 1)
    attended = attend(
        my_spans, live.astype(jnp.int32), home, piece_at, raw, cosine, sine, kv_all, 0, heads,
        head_width, span_len,
    ).reshape(rows, heads, -1)
    return attended, kv_cache


def local_four(planes, xs, cores, meet_span, span_map, hidden, w_query, w_keyval, stored_kv):
    return four_body(planes, xs, cores, meet_span, span_map, hidden, w_query, w_keyval, stored_kv)


def four_body(planes, xs, cores, meet_span, span_map, hidden, w_query, w_keyval, stored_kv):
    rows, features = hidden.shape
    span_count = span_map.shape[0]
    heads, width = w_query.shape[1:]
    head_width = stored_kv.shape[2] // 2
    span_len = CH
    slots = rows // span_len
    part = features // planes
    piece = rows // (xs * cores)
    p, x, c = lax.axis_index("seq"), lax.axis_index("head"), lax.axis_index("hold")
    at_end = (p == 0) | (p == planes - 1)
    scale = 2.0 ** math.floor(
        math.log2(65504.0 / (features * HIDDEN_BOUND * WEIGHT_BOUND))
    )
    ends, inner = (0, 3), (1, 2)
    inward = [(0, 1), (3, 2)]
    outward = [(1, 0), (2, 3)]
    across = [(1, 2), (2, 1)]

    def send(value, pairs, axis="seq"):
        return lax.ppermute(value, axis, pairs)

    my_spans = lax.dynamic_slice_in_dim(span_map, p * slots, slots, 0)
    offsets = jnp.arange(span_len, dtype=jnp.int32)
    positions = (my_spans[:, None] * span_len + offsets[None, :]).reshape(-1)
    live = (my_spans < meet_span[0]) | (my_spans == span_count - 1)

    def piece_start(i, j):
        return (jnp.mod(x + i, xs) * cores + jnp.mod(c + j, cores)) * piece

    grid = [(i, j) for i in range(xs) for j in range(cores)]
    piece_at = jnp.stack(
        [jnp.mod(a - x, xs) * cores + jnp.mod(b - c, cores) for a, b in grid]
    ).astype(jnp.int32)

    def share_x(block, where):
        got = [block]
        for i in range(1, xs):
            pairs = [(q * xs + a, q * xs + (a - i) % xs) for q in where for a in range(xs)]
            got.append(send(block, pairs, ("seq", "head")))
        return jnp.concatenate(got, 0)

    def share_c(half, where):
        parts = [half]
        for j in range(1, cores):
            pairs = [
                (q * cores + a, q * cores + (a - j) % cores) for q in where for a in range(cores)
            ]
            parts.append(send(half, pairs, ("seq", "hold")))
        return jnp.concatenate(
            [parts[j][i * piece:(i + 1) * piece] for i, j in grid], 0
        )

    def slice_for(m):
        return lax.dynamic_slice(
            hidden, (piece_start(0, 0), jnp.bitwise_xor(p, m) * part), (piece, part)
        )

    for_far, for_near, for_mid = slice_for(3), slice_for(1), slice_for(2)
    far_end = send(for_far, [(0, 3), (3, 0)])
    near = send(for_near, [(q, q ^ 1) for q in range(planes)])
    mid_end = send(for_mid, [(1, 3), (2, 0)])
    mid_inner = send(for_mid, [(0, 2), (3, 1)])
    far_inner = send(for_far, across)

    own = jnp.concatenate(
        [lax.dynamic_slice(hidden, (piece_start(i, j), p * part), (piece, part)) for i, j in grid], 0
    )
    order = jnp.bitwise_xor(p, jnp.arange(planes, dtype=jnp.int32))
    key_span = span_map.reshape(planes, slots)[order].reshape(-1)
    home = homes(key_span)
    stored_rows = stored_kv.reshape(rows, -1)
    cosine, sine = tables(positions, head_width)
    whole_keyval, whole_query = w_keyval.reshape(part, -1), w_query.reshape(part, -1)
    (
        far_end, own, whole_keyval, whole_query, cosine, sine, stored_rows, home
    ) = lax.optimization_barrier(
        (far_end, own, whole_keyval, whole_query, cosine, sine, stored_rows, home)
    )
    far_end = share_c(share_x(far_end, ends), ends)
    near = share_c(share_x(near, range(planes)), range(planes))
    mid = jnp.where(at_end, mid_end, mid_inner)
    mid = share_c(share_x(mid, range(planes)), range(planes))
    far_inner = share_c(share_x(far_inner, inner), inner)

    def project(weights, splits):
        def product(block, columns=weights):
            total = jnp.dot(block, columns, preferred_element_type=jnp.float32)
            return (total * scale).astype(jnp.float16)

        def plus(a, b):
            return (a.astype(jnp.float32) + b.astype(jnp.float32)).astype(jnp.float16)

        mid_term = product(mid)
        near_term = product(near)
        got_far = send(product(far_end), inward)
        got_near = send(near_term, inward)
        got_mid = send(mid_term, inward)
        got_cross = send(plus(mid_term, got_far), across)
        got_out = send(plus(near_term, got_cross), outward)
        totals = []
        step = weights.shape[1] // splits
        for i in range(splits):
            at = slice(i * step, (i + 1) * step)
            pair_term = plus(product(far_inner, weights[:, at]), got_mid[:, at])
            got_pair = send(pair_term, across)
            others = (
                got_near[:, at].astype(jnp.float32) + got_pair.astype(jnp.float32)
                + got_out[:, at].astype(jnp.float32)
            )
            total = jnp.dot(own, weights[:, at], preferred_element_type=jnp.float32)
            totals.append((lax.optimization_barrier(total), others * (1.0 / scale)))
        return totals, got_out

    computed_rows = jnp.repeat(live, span_len)

    def finish(raw):
        raw = jnp.concatenate(
            [
                lax.dynamic_slice_in_dim(raw, piece_at[i] * piece, piece, 0)
                for i in range(xs * cores)
            ],
            0,
        )
        parts = []
        for h in range(heads):
            keys = raw[:, 2 * h * head_width:(2 * h + 1) * head_width]
            parts.append(keys * cosine + jnp.roll(keys, head_width // 2, -1) * sine)
            parts.append(raw[:, (2 * h + 1) * head_width:(2 * h + 2) * head_width])
        recomputed = jnp.concatenate(parts, -1).astype(jnp.bfloat16)
        return jnp.where(computed_rows[:, None], recomputed, stored_rows)

    ((own_total, others),), got_out = project(whole_keyval, 1)
    end_raw = own_total + got_out.astype(jnp.float32) * (1.0 / scale)
    end_own = finish(end_raw)
    own_total, end_own = lax.optimization_barrier((own_total, end_own))
    end_kv = send(end_own, inward)
    kv_own = finish(own_total + others)
    kv_cache = kv_own.reshape(stored_kv.shape)

    cross_kv = send(kv_own, across)
    near_kv = send(kv_own, outward)
    far_kv = send(end_kv, across)
    rest_cross = send(cross_kv, outward)
    rest_far = send(far_kv, outward)
    first = jnp.where(at_end, near_kv, end_kv)
    second = jnp.where(at_end, rest_cross, far_kv)
    kv_all = jnp.concatenate(
        [kv_own, first, second, jnp.where(at_end, rest_far, cross_kv)], 0
    )
    live_int = live.astype(jnp.int32)
    outs = []
    for h, (own_total, others) in enumerate(project(whole_query, heads)[0]):
        if h:
            own_total, raw = lax.optimization_barrier((own_total, raw))
        raw = own_total + others
        outs.append(
            attend(
                my_spans, live_int, home, piece_at, raw, cosine, sine, kv_all, h, 1,
                head_width, span_len,
            )
        )
    attended = jnp.concatenate(outs, 1).reshape(rows, heads, width)
    return attended, kv_cache


def fits_four(planes, xs, rows, heads):
    return planes == 4 and (rows // xs) % CH == 0 and heads == 2


def local(planes, xs, cores, *args):
    four = fits_four(planes, xs, args[2].shape[0], args[3].shape[1])
    return (local_four if four else local_line)(planes, xs, cores, *args)


def solution(mesh):
    shape = dict(mesh.shape)
    return jax.shard_map(
        functools.partial(local, shape["seq"], shape["head"], shape["hold"]),
        mesh=mesh,
        in_specs=(
            P("grp"),
            P("grp"),
            P(("grp", "seq"), None),
            P("seq", ("head", "hold"), None),
            P("seq", ("head", "hold"), None),
            P(("grp", "seq"), ("head", "hold"), None),
        ),
        out_specs=(
            P(("grp", "seq"), ("head", "hold"), None),
            P(("grp", "seq"), ("head", "hold"), None),
        ),
        check_vma=False,
    )
```

```python
import functools
import math

import jax
import jax.numpy as jnp
from jax import lax
from jax.experimental import pallas as pl
from jax.experimental.pallas import tpu as pltpu
from jax.sharding import PartitionSpec as P


CH = 256
theta_base = 500000.0
lowest = -1e30
HIDDEN_BOUND = 6.0
WEIGHT_BOUND = 0.0625


def tables(positions, head_width):
    half = head_width // 2
    frequency = theta_base ** (
        -(jnp.arange(half, dtype=jnp.float32) * 2.0) / head_width
    )
    angles = positions.astype(jnp.float32)[:, None] * frequency[None, :]
    cosine, sine = jnp.cos(angles), jnp.sin(angles)
    return jnp.concatenate([cosine, cosine], -1), jnp.concatenate([-sine, sine], -1)


def attend_kernel(
    span_len, pieces, group, head_width, factor,
    query_span, live, home, piece_at, *refs,
):
    raw_refs = refs[:pieces]
    cos_ref, sin_ref, kv_ref = refs[pieces:pieces + 3]
    out_ref, q_s, top_s, sum_s, mix_s = refs[-5:]
    slot = pl.program_id(1)
    my_span = query_span[slot]
    piece = span_len // pieces

    @pl.when(live[slot] == 0)
    def _():
        out_ref[...] = jnp.zeros_like(out_ref)

    @pl.when(live[slot] != 0)
    def _():
        for b, raw_ref in enumerate(raw_refs):
            at = slice(b * piece, (b + 1) * piece)
            cosine, sine = cos_ref[at, :], sin_ref[at, :]
            for g in range(group):
                head = raw_ref[:, g * head_width:(g + 1) * head_width]
                turned = head * cosine + pltpu.roll(head, head_width // 2, 1) * sine
                q_s[g, at, :] = turned.astype(jnp.bfloat16)

        def scores_of(start):
            keys = kv_ref[pl.ds(start, span_len), :head_width]
            return [
                lax.dot_general(
                    keys, q_s[g], (((1,), (1,)), ((), ())), preferred_element_type=jnp.float32
                )
                for g in range(group)
            ]

        def weigh(start, weights):
            return lax.dot_general(
                kv_ref[pl.ds(start, span_len), head_width:], weights.astype(jnp.bfloat16),
                (((0,), (0,)), ((), ())), preferred_element_type=jnp.float32,
            )

        start = pl.multiple_of(home[my_span] * span_len, span_len)
        key_at = lax.broadcasted_iota(jnp.int32, (span_len, span_len), 0)
        row_at = lax.broadcasted_iota(jnp.int32, (span_len, span_len), 1)
        seen = key_at <= row_at
        for g, scores in enumerate(scores_of(start)):
            scores = jnp.where(seen, scores, lowest)
            top = scores.max(0, keepdims=True)
            weights = jnp.where(seen, jnp.exp2((scores - top) * factor), 0.0)
            top_s[g] = top
            sum_s[g] = weights.sum(0, keepdims=True)
            mix_s[g] = weigh(start, weights)

        @pl.loop(0, my_span)
        def _(i):
            start = pl.multiple_of(home[i] * span_len, span_len)
            for g, scores in enumerate(scores_of(start)):
                top = top_s[g]
                new = jnp.maximum(top, scores.max(0, keepdims=True))
                weights = jnp.exp2((scores - new) * factor)
                shrink = jnp.exp2((top - new) * factor)
                top_s[g] = new
                sum_s[g] = sum_s[g] * shrink + weights.sum(0, keepdims=True)
                mix_s[g] = mix_s[g] * shrink + weigh(start, weights)

        for g in range(group):
            out_ref[:, g * head_width:(g + 1) * head_width] = (
                (mix_s[g] / sum_s[g]).T.astype(out_ref.dtype)
            )


def attend(
    query_span, live, home, piece_at, raw, cosine, sine, kv, first, heads, head_width, span_len,
    into=None,
):
    rows = raw.shape[0]
    width = raw.shape[1] // heads
    group = width // head_width
    keys = kv.shape[0]
    slots = rows // span_len
    pieces = piece_at.shape[0] // slots
    piece = span_len // pieces
    held = [] if into is None else [into]

    def raw_spec(b):
        return pl.BlockSpec(
            (piece, width), lambda h, s, qs, lv, hm, at: (at[s * pieces + b], h)
        )

    return pl.pallas_call(
        functools.partial(
            attend_kernel, span_len, pieces, group, head_width,
            head_width ** (-0.5) * math.log2(math.e),
        ),
        grid_spec=pltpu.PrefetchScalarGridSpec(
            num_scalar_prefetch=4,
            grid=(heads, slots),
            in_specs=[raw_spec(b) for b in range(pieces)] + [
                pl.BlockSpec((span_len, head_width), lambda h, s, *_: (s, 0)),
                pl.BlockSpec((span_len, head_width), lambda h, s, *_: (s, 0)),
                pl.BlockSpec((keys, 2 * head_width), lambda h, s, *_: (0, first + h)),
            ] + [pl.BlockSpec(memory_space=pl.ANY)] * len(held),
            out_specs=pl.BlockSpec((span_len, width), lambda h, s, *_: (s, first + h)),
            scratch_shapes=[
                pltpu.VMEM((group, span_len, head_width), jnp.bfloat16),
                pltpu.VMEM((group, 1, span_len), jnp.float32),
                pltpu.VMEM((group, 1, span_len), jnp.float32),
                pltpu.VMEM((group, head_width, span_len), jnp.float32),
            ],
        ),
        out_shape=jax.ShapeDtypeStruct(
            (rows, kv.shape[1] // (2 * head_width) * width), jnp.bfloat16
        ),
        input_output_aliases={4 + pieces + 3: 0} if held else {},
        cost_estimate=pl.CostEstimate(
            flops=4 * rows * heads * group * keys * head_width,
            bytes_accessed=rows * heads * width * 6 + keys * heads * 2 * head_width * 2,
            transcendentals=rows * heads * group * keys,
        ),
        name="attend",
    )(query_span, live, home, piece_at, *([raw] * pieces), cosine, sine, kv, *held)


def homes(key_span):
    places = jnp.arange(key_span.shape[0], dtype=jnp.int32)
    return jnp.sum(
        jnp.where(key_span[None, :] == places[:, None], places[None, :], 0), 1
    )


def local_line(planes, xs, cores, meet_span, span_map, hidden, w_query, w_keyval, stored_kv):
    rows, features = hidden.shape
    span_count = span_map.shape[0]
    heads = w_query.shape[1]
    head_width = stored_kv.shape[2] // 2
    span_len = CH
    slots = rows // span_len
    part = features // planes
    piece = rows // (xs * cores)
    p, x, c = lax.axis_index("seq"), lax.axis_index("head"), lax.axis_index("hold")
    scale = 2.0 ** math.floor(
        math.log2(65504.0 / (features * HIDDEN_BOUND * WEIGHT_BOUND))
    )

    my_spans = lax.dynamic_slice_in_dim(span_map, p * slots, slots, 0)
    offsets = jnp.arange(span_len, dtype=jnp.int32)
    positions = (my_spans[:, None] * span_len + offsets[None, :]).reshape(-1)
    live = (my_spans < meet_span[0]) | (my_spans == span_count - 1)
    cosine, sine = tables(positions, head_width)

    mine = (x * cores + c) * piece

    def share(block, valid):
        got = [block]
        for i in range(1, xs):
            pairs = [
                (q * xs + a, q * xs + (a - i) % xs) for q in valid for a in range(xs)
            ]
            got.append(lax.ppermute(block, ("seq", "head"), pairs))
        half = jnp.concatenate(got, 0)
        out = [half]
        for i in range(1, cores):
            pairs = [
                (q * cores + a, q * cores + (a - i) % cores)
                for q in valid for a in range(cores)
            ]
            out.append(lax.ppermute(half, ("seq", "hold"), pairs))
        return jnp.concatenate(out, 0)

    from_right, from_left = {}, {}
    for k in range(planes - 1, 0, -1):
        for table, sign in ((from_right, 1), (from_left, -1)):
            target = jnp.mod(p - sign * k, planes)
            block = lax.dynamic_slice(hidden, (mine, target * part), (piece, part))
            pairs = [
                (q, q - sign * k) for q in range(planes) if 0 <= q - sign * k < planes
            ]
            table[k] = (lax.ppermute(block, "seq", pairs), [b for _, b in pairs])
    for k in range(planes - 1, 0, -1):
        from_right[k] = share(*from_right[k])
        from_left[k] = share(*from_left[k])
    own = lax.dynamic_slice(hidden, (0, p * part), (rows, part))

    def ordered(value):
        out = []
        for a in range(xs):
            for b in range(cores):
                at = (jnp.mod(b - c, cores) * xs + jnp.mod(a - x, xs)) * piece
                out.append(lax.dynamic_slice_in_dim(value, at, piece, 0))
        return jnp.concatenate(out, 0)

    def project(weights):
        def step(block, arrived):
            total = jnp.dot(block, weights, preferred_element_type=jnp.float32) * scale
            if arrived is not None:
                total = total + arrived.astype(jnp.float32)
            return total.astype(jnp.float16)

        right = left = None
        for k in range(planes - 1, 0, -1):
            send = step(from_right[k], right)
            right = lax.ppermute(send, "seq", [(q, q + 1) for q in range(planes - k)])
            send = step(from_left[k], left)
            left = lax.ppermute(send, "seq", [(q + 1, q) for q in range(k - 1, planes - 1)])
        total = jnp.dot(own, weights, preferred_element_type=jnp.float32)
        if planes > 1:
            others = ordered(right).astype(jnp.float32) + ordered(left).astype(jnp.float32)
            total = total + others * (1.0 / scale)
        return total

    keyval_raw = project(w_keyval.reshape(part, -1)).reshape(rows, heads, 2 * head_width)
    keys_raw = keyval_raw[..., :head_width]
    turned = (
        keys_raw * cosine[:, None, :]
        + jnp.roll(keys_raw, head_width // 2, -1) * sine[:, None, :]
    )
    recomputed = jnp.concatenate([turned, keyval_raw[..., head_width:]], -1).astype(jnp.bfloat16)
    computed_rows = jnp.repeat(live, span_len)
    kv_cache = jnp.where(computed_rows[:, None, None], recomputed, stored_kv)

    kv_own = kv_cache.reshape(rows, -1)
    right, left = kv_own, kv_own
    near_left, near_right = {}, {}
    for k in range(1, planes):
        right = lax.ppermute(right, "seq", [(q, q + 1) for q in range(k - 1, planes - 1)])
        left = lax.ppermute(left, "seq", [(q + 1, q) for q in range(planes - k)])
        near_left[k], near_right[k] = right, left
    kv_all = [kv_own]
    for k in range(1, planes):
        kv_all.append(jnp.where(p + k < planes, near_right[k], near_left[planes - k]))
    kv_all = jnp.concatenate(kv_all, 0)
    order = jnp.mod(p + jnp.arange(planes, dtype=jnp.int32), planes)
    key_span = span_map.reshape(planes, slots)[order].reshape(-1)

    home = homes(key_span)
    piece_at = jnp.arange(slots, dtype=jnp.int32)
    raw = jnp.concatenate([project(w_query[:, h, :]) for h in range(heads)], 1)
    attended = attend(
        my_spans, live.astype(jnp.int32), home, piece_at, raw, cosine, sine, kv_all, 0, heads,
        head_width, span_len,
    ).reshape(rows, heads, -1)
    return attended, kv_cache


def local_four(planes, xs, cores, meet_span, span_map, hidden, w_query, w_keyval, stored_kv):
    return four_body(planes, xs, cores, meet_span, span_map, hidden, w_query, w_keyval, stored_kv)


def four_body(planes, xs, cores, meet_span, span_map, hidden, w_query, w_keyval, stored_kv):
    rows, features = hidden.shape
    span_count = span_map.shape[0]
    heads, width = w_query.shape[1:]
    head_width = stored_kv.shape[2] // 2
    span_len = CH
    slots = rows // span_len
    part = features // planes
    piece = rows // (xs * cores)
    p, x, c = lax.axis_index("seq"), lax.axis_index("head"), lax.axis_index("hold")
    at_end = (p == 0) | (p == planes - 1)
    scale = 2.0 ** math.floor(
        math.log2(65504.0 / (features * HIDDEN_BOUND * WEIGHT_BOUND))
    )
    ends, inner = (0, 3), (1, 2)
    inward = [(0, 1), (3, 2)]
    outward = [(1, 0), (2, 3)]
    across = [(1, 2), (2, 1)]

    def send(value, pairs, axis="seq"):
        return lax.ppermute(value, axis, pairs)

    my_spans = lax.dynamic_slice_in_dim(span_map, p * slots, slots, 0)
    offsets = jnp.arange(span_len, dtype=jnp.int32)
    positions = (my_spans[:, None] * span_len + offsets[None, :]).reshape(-1)
    live = (my_spans < meet_span[0]) | (my_spans == span_count - 1)

    def piece_start(i, j):
        return (jnp.mod(x + i, xs) * cores + jnp.mod(c + j, cores)) * piece

    grid = [(i, j) for i in range(xs) for j in range(cores)]
    piece_at = jnp.stack(
        [jnp.mod(a - x, xs) * cores + jnp.mod(b - c, cores) for a, b in grid]
    ).astype(jnp.int32)

    def share_x(block, where):
        got = [block]
        for i in range(1, xs):
            pairs = [(q * xs + a, q * xs + (a - i) % xs) for q in where for a in range(xs)]
            got.append(send(block, pairs, ("seq", "head")))
        return jnp.concatenate(got, 0)

    def share_c(half, where):
        parts = [half]
        for j in range(1, cores):
            pairs = [
                (q * cores + a, q * cores + (a - j) % cores) for q in where for a in range(cores)
            ]
            parts.append(send(half, pairs, ("seq", "hold")))
        return jnp.concatenate(
            [parts[j][i * piece:(i + 1) * piece] for i, j in grid], 0
        )

    def slice_for(m, plane):
        return lax.dynamic_slice(
            hidden, (piece_start(0, 0), jnp.bitwise_xor(plane, m) * part), (piece, part)
        )

    for_far, later = lax.optimization_barrier((slice_for(3, p), p))
    for_near, for_mid = slice_for(1, later), slice_for(2, later)
    far_end = send(for_far, [(0, 3), (3, 0)])
    near = send(for_near, [(q, q ^ 1) for q in range(planes)])
    mid_end = send(for_mid, [(1, 3), (2, 0)])
    mid_inner = send(for_mid, [(0, 2), (3, 1)])
    far_inner = send(for_far, across)

    own = jnp.concatenate(
        [lax.dynamic_slice(hidden, (piece_start(i, j), p * part), (piece, part)) for i, j in grid], 0
    )
    order = jnp.bitwise_xor(p, jnp.arange(planes, dtype=jnp.int32))
    key_span = span_map.reshape(planes, slots)[order].reshape(-1)
    home = homes(key_span)
    stored_rows = stored_kv.reshape(rows, -1)
    cosine, sine = tables(positions, head_width)
    whole_keyval, whole_query = w_keyval.reshape(part, -1), w_query.reshape(part, -1)
    far_end, whole_keyval, cosine, sine, stored_rows, home = lax.optimization_barrier(
        (far_end, whole_keyval, cosine, sine, stored_rows, home)
    )
    far_half = share_x(far_end, ends)
    far_half, own, whole_query = lax.optimization_barrier((far_half, own, whole_query))
    far_end = share_c(far_half, ends)
    near = share_c(share_x(near, range(planes)), range(planes))
    mid = jnp.where(at_end, mid_end, mid_inner)
    mid = share_c(share_x(mid, range(planes)), range(planes))
    far_inner = share_c(share_x(far_inner, inner), inner)

    def project(weights, splits):
        def product(block, columns=weights):
            total = jnp.dot(block, columns, preferred_element_type=jnp.float32)
            return (total * scale).astype(jnp.float16)

        def plus(a, b):
            return (a.astype(jnp.float32) + b.astype(jnp.float32)).astype(jnp.float16)

        mid_term = product(mid)
        near_term = product(near)
        got_far = send(product(far_end), inward)
        got_near = send(near_term, inward)
        got_mid = send(mid_term, inward)
        got_cross = send(plus(mid_term, got_far), across)
        got_out = send(plus(near_term, got_cross), outward)
        totals = []
        step = weights.shape[1] // splits
        for i in range(splits):
            at = slice(i * step, (i + 1) * step)
            pair_term = plus(product(far_inner, weights[:, at]), got_mid[:, at])
            got_pair = send(pair_term, across)
            others = (
                got_near[:, at].astype(jnp.float32) + got_pair.astype(jnp.float32)
                + got_out[:, at].astype(jnp.float32)
            )
            total = jnp.dot(own, weights[:, at], preferred_element_type=jnp.float32)
            totals.append((lax.optimization_barrier(total), others * (1.0 / scale)))
        return totals, got_out

    computed_rows = jnp.repeat(live, span_len)

    def finish(raw):
        raw = jnp.concatenate(
            [
                lax.dynamic_slice_in_dim(raw, piece_at[i] * piece, piece, 0)
                for i in range(xs * cores)
            ],
            0,
        )
        parts = []
        for h in range(heads):
            keys = raw[:, 2 * h * head_width:(2 * h + 1) * head_width]
            parts.append(keys * cosine + jnp.roll(keys, head_width // 2, -1) * sine)
            parts.append(raw[:, (2 * h + 1) * head_width:(2 * h + 2) * head_width])
        recomputed = jnp.concatenate(parts, -1).astype(jnp.bfloat16)
        return jnp.where(computed_rows[:, None], recomputed, stored_rows)

    ((own_total, others),), got_out = project(whole_keyval, 1)
    end_raw = own_total + got_out.astype(jnp.float32) * (1.0 / scale)
    end_own = finish(end_raw)
    own_total, end_own = lax.optimization_barrier((own_total, end_own))
    end_kv = send(end_own, inward)
    kv_own = finish(own_total + others)
    kv_cache = kv_own.reshape(stored_kv.shape)

    cross_kv = send(kv_own, across)
    near_kv = send(kv_own, outward)
    far_kv = send(end_kv, across)
    rest_cross = send(cross_kv, outward)
    rest_far = send(far_kv, outward)
    first = jnp.where(at_end, near_kv, end_kv)
    second = jnp.where(at_end, rest_cross, far_kv)
    kv_all = jnp.concatenate(
        [kv_own, first, second, jnp.where(at_end, rest_far, cross_kv)], 0
    )
    live_int = live.astype(jnp.int32)
    attended = None
    for h, (own_total, others) in enumerate(project(whole_query, heads)[0]):
        if h:
            own_total, raw = lax.optimization_barrier((own_total, raw))
        raw = own_total + others
        attended = attend(
            my_spans, live_int, home, piece_at, raw, cosine, sine, kv_all, h, 1,
            head_width, span_len, attended,
        )
    attended = attended.reshape(rows, heads, width)
    return attended, kv_cache


def fits_four(planes, xs, rows, heads):
    return planes == 4 and (rows // xs) % CH == 0 and heads == 2


def local(planes, xs, cores, *args):
    four = fits_four(planes, xs, args[2].shape[0], args[3].shape[1])
    return (local_four if four else local_line)(planes, xs, cores, *args)


def solution(mesh):
    shape = dict(mesh.shape)
    return jax.shard_map(
        functools.partial(local, shape["seq"], shape["head"], shape["hold"]),
        mesh=mesh,
        in_specs=(
            P("grp"),
            P("grp"),
            P(("grp", "seq"), None),
            P("seq", ("head", "hold"), None),
            P("seq", ("head", "hold"), None),
            P(("grp", "seq"), ("head", "hold"), None),
        ),
        out_specs=(
            P(("grp", "seq"), ("head", "hold"), None),
            P(("grp", "seq"), ("head", "hold"), None),
        ),
        check_vma=False,
    )
```

```python
import functools
import math

import jax
import jax.numpy as jnp
from jax import lax
from jax.experimental import pallas as pl
from jax.experimental.pallas import tpu as pltpu
from jax.sharding import PartitionSpec as P


CH = 256
theta_base = 500000.0
lowest = -1e30
HIDDEN_BOUND = 6.0
WEIGHT_BOUND = 0.0625


def tables(positions, head_width):
    half = head_width // 2
    frequency = theta_base ** (
        -(jnp.arange(half, dtype=jnp.float32) * 2.0) / head_width
    )
    angles = positions.astype(jnp.float32)[:, None] * frequency[None, :]
    cosine, sine = jnp.cos(angles), jnp.sin(angles)
    return jnp.concatenate([cosine, cosine], -1), jnp.concatenate([-sine, sine], -1)


def attend_kernel(
    span_len, pieces, group, head_width, factor,
    query_span, live, home, piece_at, *refs,
):
    raw_refs = refs[:pieces]
    cos_ref, sin_ref, kv_ref = refs[pieces:pieces + 3]
    out_ref, q_s, top_s, sum_s, mix_s = refs[-5:]
    slot = pl.program_id(1)
    my_span = query_span[slot]
    piece = span_len // pieces

    @pl.when(live[slot] == 0)
    def _():
        out_ref[...] = jnp.zeros_like(out_ref)

    @pl.when(live[slot] != 0)
    def _():
        for b, raw_ref in enumerate(raw_refs):
            at = slice(b * piece, (b + 1) * piece)
            cosine, sine = cos_ref[at, :], sin_ref[at, :]
            for g in range(group):
                head = raw_ref[:, g * head_width:(g + 1) * head_width]
                turned = head * cosine + pltpu.roll(head, head_width // 2, 1) * sine
                q_s[g, at, :] = turned.astype(jnp.bfloat16)

        def scores_of(start):
            keys = kv_ref[pl.ds(start, span_len), :head_width]
            return [
                lax.dot_general(
                    keys, q_s[g], (((1,), (1,)), ((), ())), preferred_element_type=jnp.float32
                )
                for g in range(group)
            ]

        def weigh(start, weights):
            return lax.dot_general(
                kv_ref[pl.ds(start, span_len), head_width:], weights.astype(jnp.bfloat16),
                (((0,), (0,)), ((), ())), preferred_element_type=jnp.float32,
            )

        start = pl.multiple_of(home[my_span] * span_len, span_len)
        key_at = lax.broadcasted_iota(jnp.int32, (span_len, span_len), 0)
        row_at = lax.broadcasted_iota(jnp.int32, (span_len, span_len), 1)
        seen = key_at <= row_at
        for g, scores in enumerate(scores_of(start)):
            scores = jnp.where(seen, scores, lowest)
            top = scores.max(0, keepdims=True)
            weights = jnp.where(seen, jnp.exp2((scores - top) * factor), 0.0)
            top_s[g] = top
            sum_s[g] = weights.sum(0, keepdims=True)
            mix_s[g] = weigh(start, weights)

        @pl.loop(0, my_span)
        def _(i):
            start = pl.multiple_of(home[i] * span_len, span_len)
            for g, scores in enumerate(scores_of(start)):
                top = top_s[g]
                new = jnp.maximum(top, scores.max(0, keepdims=True))
                weights = jnp.exp2((scores - new) * factor)
                shrink = jnp.exp2((top - new) * factor)
                top_s[g] = new
                sum_s[g] = sum_s[g] * shrink + weights.sum(0, keepdims=True)
                mix_s[g] = mix_s[g] * shrink + weigh(start, weights)

        for g in range(group):
            out_ref[:, g * head_width:(g + 1) * head_width] = (
                (mix_s[g] / sum_s[g]).T.astype(out_ref.dtype)
            )


def attend(
    query_span, live, home, piece_at, raw, cosine, sine, kv, first, heads, head_width, span_len,
    into=None,
):
    rows = raw.shape[0]
    width = raw.shape[1] // heads
    group = width // head_width
    keys = kv.shape[0]
    slots = rows // span_len
    pieces = piece_at.shape[0] // slots
    piece = span_len // pieces
    held = [] if into is None else [into]

    def raw_spec(b):
        return pl.BlockSpec(
            (piece, width), lambda h, s, qs, lv, hm, at: (at[s * pieces + b], h)
        )

    return pl.pallas_call(
        functools.partial(
            attend_kernel, span_len, pieces, group, head_width,
            head_width ** (-0.5) * math.log2(math.e),
        ),
        grid_spec=pltpu.PrefetchScalarGridSpec(
            num_scalar_prefetch=4,
            grid=(heads, slots),
            in_specs=[raw_spec(b) for b in range(pieces)] + [
                pl.BlockSpec((span_len, head_width), lambda h, s, *_: (s, 0)),
                pl.BlockSpec((span_len, head_width), lambda h, s, *_: (s, 0)),
                pl.BlockSpec((keys, 2 * head_width), lambda h, s, *_: (0, first + h)),
            ] + [pl.BlockSpec(memory_space=pl.ANY)] * len(held),
            out_specs=pl.BlockSpec((span_len, width), lambda h, s, *_: (s, first + h)),
            scratch_shapes=[
                pltpu.VMEM((group, span_len, head_width), jnp.bfloat16),
                pltpu.VMEM((group, 1, span_len), jnp.float32),
                pltpu.VMEM((group, 1, span_len), jnp.float32),
                pltpu.VMEM((group, head_width, span_len), jnp.float32),
            ],
        ),
        out_shape=jax.ShapeDtypeStruct(
            (rows, kv.shape[1] // (2 * head_width) * width), jnp.bfloat16
        ),
        input_output_aliases={4 + pieces + 3: 0} if held else {},
        cost_estimate=pl.CostEstimate(
            flops=4 * rows * heads * group * keys * head_width,
            bytes_accessed=rows * heads * width * 6 + keys * heads * 2 * head_width * 2,
            transcendentals=rows * heads * group * keys,
        ),
        name="attend",
    )(query_span, live, home, piece_at, *([raw] * pieces), cosine, sine, kv, *held)


def homes(key_span):
    places = jnp.arange(key_span.shape[0], dtype=jnp.int32)
    return jnp.sum(
        jnp.where(key_span[None, :] == places[:, None], places[None, :], 0), 1
    )


def local_line(planes, xs, cores, meet_span, span_map, hidden, w_query, w_keyval, stored_kv):
    rows, features = hidden.shape
    span_count = span_map.shape[0]
    heads = w_query.shape[1]
    head_width = stored_kv.shape[2] // 2
    span_len = CH
    slots = rows // span_len
    part = features // planes
    piece = rows // (xs * cores)
    p, x, c = lax.axis_index("seq"), lax.axis_index("head"), lax.axis_index("hold")
    scale = 2.0 ** math.floor(
        math.log2(65504.0 / (features * HIDDEN_BOUND * WEIGHT_BOUND))
    )

    my_spans = lax.dynamic_slice_in_dim(span_map, p * slots, slots, 0)
    offsets = jnp.arange(span_len, dtype=jnp.int32)
    positions = (my_spans[:, None] * span_len + offsets[None, :]).reshape(-1)
    live = (my_spans < meet_span[0]) | (my_spans == span_count - 1)
    cosine, sine = tables(positions, head_width)

    mine = (x * cores + c) * piece

    def share(block, valid):
        got = [block]
        for i in range(1, xs):
            pairs = [
                (q * xs + a, q * xs + (a - i) % xs) for q in valid for a in range(xs)
            ]
            got.append(lax.ppermute(block, ("seq", "head"), pairs))
        half = jnp.concatenate(got, 0)
        out = [half]
        for i in range(1, cores):
            pairs = [
                (q * cores + a, q * cores + (a - i) % cores)
                for q in valid for a in range(cores)
            ]
            out.append(lax.ppermute(half, ("seq", "hold"), pairs))
        return jnp.concatenate(out, 0)

    from_right, from_left = {}, {}
    for k in range(planes - 1, 0, -1):
        for table, sign in ((from_right, 1), (from_left, -1)):
            target = jnp.mod(p - sign * k, planes)
            block = lax.dynamic_slice(hidden, (mine, target * part), (piece, part))
            pairs = [
                (q, q - sign * k) for q in range(planes) if 0 <= q - sign * k < planes
            ]
            table[k] = (lax.ppermute(block, "seq", pairs), [b for _, b in pairs])
    for k in range(planes - 1, 0, -1):
        from_right[k] = share(*from_right[k])
        from_left[k] = share(*from_left[k])
    own = lax.dynamic_slice(hidden, (0, p * part), (rows, part))

    def ordered(value):
        out = []
        for a in range(xs):
            for b in range(cores):
                at = (jnp.mod(b - c, cores) * xs + jnp.mod(a - x, xs)) * piece
                out.append(lax.dynamic_slice_in_dim(value, at, piece, 0))
        return jnp.concatenate(out, 0)

    def project(weights):
        def step(block, arrived):
            total = jnp.dot(block, weights, preferred_element_type=jnp.float32) * scale
            if arrived is not None:
                total = total + arrived.astype(jnp.float32)
            return total.astype(jnp.float16)

        right = left = None
        for k in range(planes - 1, 0, -1):
            send = step(from_right[k], right)
            right = lax.ppermute(send, "seq", [(q, q + 1) for q in range(planes - k)])
            send = step(from_left[k], left)
            left = lax.ppermute(send, "seq", [(q + 1, q) for q in range(k - 1, planes - 1)])
        total = jnp.dot(own, weights, preferred_element_type=jnp.float32)
        if planes > 1:
            others = ordered(right).astype(jnp.float32) + ordered(left).astype(jnp.float32)
            total = total + others * (1.0 / scale)
        return total

    keyval_raw = project(w_keyval.reshape(part, -1)).reshape(rows, heads, 2 * head_width)
    keys_raw = keyval_raw[..., :head_width]
    turned = (
        keys_raw * cosine[:, None, :]
        + jnp.roll(keys_raw, head_width // 2, -1) * sine[:, None, :]
    )
    recomputed = jnp.concatenate([turned, keyval_raw[..., head_width:]], -1).astype(jnp.bfloat16)
    computed_rows = jnp.repeat(live, span_len)
    kv_cache = jnp.where(computed_rows[:, None, None], recomputed, stored_kv)

    kv_own = kv_cache.reshape(rows, -1)
    right, left = kv_own, kv_own
    near_left, near_right = {}, {}
    for k in range(1, planes):
        right = lax.ppermute(right, "seq", [(q, q + 1) for q in range(k - 1, planes - 1)])
        left = lax.ppermute(left, "seq", [(q + 1, q) for q in range(planes - k)])
        near_left[k], near_right[k] = right, left
    kv_all = [kv_own]
    for k in range(1, planes):
        kv_all.append(jnp.where(p + k < planes, near_right[k], near_left[planes - k]))
    kv_all = jnp.concatenate(kv_all, 0)
    order = jnp.mod(p + jnp.arange(planes, dtype=jnp.int32), planes)
    key_span = span_map.reshape(planes, slots)[order].reshape(-1)

    home = homes(key_span)
    piece_at = jnp.arange(slots, dtype=jnp.int32)
    raw = jnp.concatenate([project(w_query[:, h, :]) for h in range(heads)], 1)
    attended = attend(
        my_spans, live.astype(jnp.int32), home, piece_at, raw, cosine, sine, kv_all, 0, heads,
        head_width, span_len,
    ).reshape(rows, heads, -1)
    return attended, kv_cache


def local_four(planes, xs, cores, meet_span, span_map, hidden, w_query, w_keyval, stored_kv):
    return four_body(planes, xs, cores, meet_span, span_map, hidden, w_query, w_keyval, stored_kv)


def four_body(planes, xs, cores, meet_span, span_map, hidden, w_query, w_keyval, stored_kv):
    rows, features = hidden.shape
    span_count = span_map.shape[0]
    heads, width = w_query.shape[1:]
    head_width = stored_kv.shape[2] // 2
    span_len = CH
    slots = rows // span_len
    part = features // planes
    piece = rows // (xs * cores)
    p, x, c = lax.axis_index("seq"), lax.axis_index("head"), lax.axis_index("hold")
    at_end = (p == 0) | (p == planes - 1)
    scale = 2.0 ** math.floor(
        math.log2(65504.0 / (features * HIDDEN_BOUND * WEIGHT_BOUND))
    )
    ends, inner = (0, 3), (1, 2)
    inward = [(0, 1), (3, 2)]
    outward = [(1, 0), (2, 3)]
    across = [(1, 2), (2, 1)]

    def send(value, pairs, axis="seq"):
        return lax.ppermute(value, axis, pairs)

    my_spans = lax.dynamic_slice_in_dim(span_map, p * slots, slots, 0)
    offsets = jnp.arange(span_len, dtype=jnp.int32)
    positions = (my_spans[:, None] * span_len + offsets[None, :]).reshape(-1)
    live = (my_spans < meet_span[0]) | (my_spans == span_count - 1)

    def piece_start(i, j):
        return (jnp.mod(x + i, xs) * cores + jnp.mod(c + j, cores)) * piece

    grid = [(i, j) for i in range(xs) for j in range(cores)]
    piece_at = jnp.stack(
        [jnp.mod(a - x, xs) * cores + jnp.mod(b - c, cores) for a, b in grid]
    ).astype(jnp.int32)

    def share_x(block, where):
        got = [block]
        for i in range(1, xs):
            pairs = [(q * xs + a, q * xs + (a - i) % xs) for q in where for a in range(xs)]
            got.append(send(block, pairs, ("seq", "head")))
        return jnp.concatenate(got, 0)

    def share_c(half, where):
        parts = [half]
        for j in range(1, cores):
            pairs = [
                (q * cores + a, q * cores + (a - j) % cores) for q in where for a in range(cores)
            ]
            parts.append(send(half, pairs, ("seq", "hold")))
        return jnp.concatenate(
            [parts[j][i * piece:(i + 1) * piece] for i, j in grid], 0
        )

    def slice_for(m, plane):
        return lax.dynamic_slice(
            hidden, (piece_start(0, 0), jnp.bitwise_xor(plane, m) * part), (piece, part)
        )

    for_far, later = lax.optimization_barrier((slice_for(3, p), p))
    for_near, for_mid = slice_for(1, later), slice_for(2, later)
    far_end = send(for_far, [(0, 3), (3, 0)])
    near = send(for_near, [(q, q ^ 1) for q in range(planes)])
    mid_end = send(for_mid, [(1, 3), (2, 0)])
    mid_inner = send(for_mid, [(0, 2), (3, 1)])
    far_inner = send(for_far, across)

    own = jnp.concatenate(
        [lax.dynamic_slice(hidden, (piece_start(i, j), p * part), (piece, part)) for i, j in grid], 0
    )
    order = jnp.bitwise_xor(p, jnp.arange(planes, dtype=jnp.int32))
    key_span = span_map.reshape(planes, slots)[order].reshape(-1)
    home = homes(key_span)
    stored_rows = stored_kv.reshape(rows, -1)
    cosine, sine = tables(positions, head_width)
    whole_keyval = w_keyval.reshape(part, -1)
    far_end, whole_keyval, cosine, sine, stored_rows, home = lax.optimization_barrier(
        (far_end, whole_keyval, cosine, sine, stored_rows, home)
    )
    far_half = share_x(far_end, ends)
    late_query, own = lax.optimization_barrier((w_query, own))
    far_half, whole_query = lax.optimization_barrier((far_half, late_query.reshape(part, -1)))
    far_end = share_c(far_half, ends)
    near = share_c(share_x(near, range(planes)), range(planes))
    mid = jnp.where(at_end, mid_end, mid_inner)
    mid = share_c(share_x(mid, range(planes)), range(planes))
    far_inner = share_c(share_x(far_inner, inner), inner)

    def project(weights, splits):
        def product(block, columns=weights):
            total = jnp.dot(block, columns, preferred_element_type=jnp.float32)
            return (total * scale).astype(jnp.float16)

        def plus(a, b):
            return (a.astype(jnp.float32) + b.astype(jnp.float32)).astype(jnp.float16)

        mid_term = product(mid)
        near_term = product(near)
        got_far = send(product(far_end), inward)
        got_near = send(near_term, inward)
        got_mid = send(mid_term, inward)
        got_cross = send(plus(mid_term, got_far), across)
        got_out = send(plus(near_term, got_cross), outward)
        totals = []
        step = weights.shape[1] // splits
        for i in range(splits):
            at = slice(i * step, (i + 1) * step)
            pair_term = plus(product(far_inner, weights[:, at]), got_mid[:, at])
            got_pair = send(pair_term, across)
            others = (
                got_near[:, at].astype(jnp.float32) + got_pair.astype(jnp.float32)
                + got_out[:, at].astype(jnp.float32)
            )
            total = jnp.dot(own, weights[:, at], preferred_element_type=jnp.float32)
            totals.append((lax.optimization_barrier(total), others * (1.0 / scale)))
        return totals, got_out

    computed_rows = jnp.repeat(live, span_len)

    def finish(raw):
        raw = jnp.concatenate(
            [
                lax.dynamic_slice_in_dim(raw, piece_at[i] * piece, piece, 0)
                for i in range(xs * cores)
            ],
            0,
        )
        parts = []
        for h in range(heads):
            keys = raw[:, 2 * h * head_width:(2 * h + 1) * head_width]
            parts.append(keys * cosine + jnp.roll(keys, head_width // 2, -1) * sine)
            parts.append(raw[:, (2 * h + 1) * head_width:(2 * h + 2) * head_width])
        recomputed = jnp.concatenate(parts, -1).astype(jnp.bfloat16)
        return jnp.where(computed_rows[:, None], recomputed, stored_rows)

    ((own_total, others),), got_out = project(whole_keyval, 1)
    end_raw = own_total + got_out.astype(jnp.float32) * (1.0 / scale)
    end_own = finish(end_raw)
    own_total, end_own = lax.optimization_barrier((own_total, end_own))
    end_kv = send(end_own, inward)
    kv_own = finish(own_total + others)
    kv_cache = kv_own.reshape(stored_kv.shape)

    cross_kv = send(kv_own, across)
    near_kv = send(kv_own, outward)
    far_kv = send(end_kv, across)
    rest_cross = send(cross_kv, outward)
    rest_far = send(far_kv, outward)
    first = jnp.where(at_end, near_kv, end_kv)
    second = jnp.where(at_end, rest_cross, far_kv)
    kv_all = jnp.concatenate(
        [kv_own, first, second, jnp.where(at_end, rest_far, cross_kv)], 0
    )
    live_int = live.astype(jnp.int32)
    attended = None
    for h, (own_total, others) in enumerate(project(whole_query, heads)[0]):
        if h:
            own_total, raw = lax.optimization_barrier((own_total, raw))
        raw = own_total + others
        attended = attend(
            my_spans, live_int, home, piece_at, raw, cosine, sine, kv_all, h, 1,
            head_width, span_len, attended,
        )
    attended = attended.reshape(rows, heads, width)
    return attended, kv_cache


def fits_four(planes, xs, rows, heads):
    return planes == 4 and (rows // xs) % CH == 0 and heads == 2


def local(planes, xs, cores, *args):
    four = fits_four(planes, xs, args[2].shape[0], args[3].shape[1])
    return (local_four if four else local_line)(planes, xs, cores, *args)


def solution(mesh):
    shape = dict(mesh.shape)
    return jax.shard_map(
        functools.partial(local, shape["seq"], shape["head"], shape["hold"]),
        mesh=mesh,
        in_specs=(
            P("grp"),
            P("grp"),
            P(("grp", "seq"), None),
            P("seq", ("head", "hold"), None),
            P("seq", ("head", "hold"), None),
            P(("grp", "seq"), ("head", "hold"), None),
        ),
        out_specs=(
            P(("grp", "seq"), ("head", "hold"), None),
            P(("grp", "seq"), ("head", "hold"), None),
        ),
        check_vma=False,
    )
```

```python
import functools
import math

import jax
import jax.numpy as jnp
from jax import lax
from jax.experimental import pallas as pl
from jax.experimental.pallas import tpu as pltpu
from jax.sharding import PartitionSpec as P


CH = 256
theta_base = 500000.0
lowest = -1e30
HIDDEN_BOUND = 6.0
WEIGHT_BOUND = 0.0625


def tables(positions, head_width):
    half = head_width // 2
    frequency = theta_base ** (
        -(jnp.arange(half, dtype=jnp.float32) * 2.0) / head_width
    )
    angles = positions.astype(jnp.float32)[:, None] * frequency[None, :]
    cosine, sine = jnp.cos(angles), jnp.sin(angles)
    return jnp.concatenate([cosine, cosine], -1), jnp.concatenate([-sine, sine], -1)


def attend_kernel(
    span_len, pieces, group, head_width, factor,
    query_span, live, home, piece_at, *refs,
):
    raw_refs = refs[:pieces]
    cos_ref, sin_ref, kv_ref = refs[pieces:pieces + 3]
    out_ref, q_s, top_s, sum_s, mix_s = refs[-5:]
    slot = pl.program_id(1)
    my_span = query_span[slot]
    piece = span_len // pieces

    @pl.when(live[slot] == 0)
    def _():
        out_ref[...] = jnp.zeros_like(out_ref)

    @pl.when(live[slot] != 0)
    def _():
        for b, raw_ref in enumerate(raw_refs):
            at = slice(b * piece, (b + 1) * piece)
            cosine, sine = cos_ref[at, :], sin_ref[at, :]
            for g in range(group):
                head = raw_ref[:, g * head_width:(g + 1) * head_width]
                turned = head * cosine + pltpu.roll(head, head_width // 2, 1) * sine
                q_s[g, at, :] = turned.astype(jnp.bfloat16)

        def scores_of(start):
            keys = kv_ref[pl.ds(start, span_len), :head_width]
            return [
                lax.dot_general(
                    keys, q_s[g], (((1,), (1,)), ((), ())), preferred_element_type=jnp.float32
                )
                for g in range(group)
            ]

        def weigh(start, weights):
            return lax.dot_general(
                kv_ref[pl.ds(start, span_len), head_width:], weights.astype(jnp.bfloat16),
                (((0,), (0,)), ((), ())), preferred_element_type=jnp.float32,
            )

        start = pl.multiple_of(home[my_span] * span_len, span_len)
        key_at = lax.broadcasted_iota(jnp.int32, (span_len, span_len), 0)
        row_at = lax.broadcasted_iota(jnp.int32, (span_len, span_len), 1)
        seen = key_at <= row_at
        for g, scores in enumerate(scores_of(start)):
            scores = jnp.where(seen, scores, lowest)
            top = scores.max(0, keepdims=True)
            weights = jnp.where(seen, jnp.exp2((scores - top) * factor), 0.0)
            top_s[g] = top
            sum_s[g] = weights.sum(0, keepdims=True)
            mix_s[g] = weigh(start, weights)

        @pl.loop(0, my_span)
        def _(i):
            start = pl.multiple_of(home[i] * span_len, span_len)
            for g, scores in enumerate(scores_of(start)):
                top = top_s[g]
                new = jnp.maximum(top, scores.max(0, keepdims=True))
                weights = jnp.exp2((scores - new) * factor)
                shrink = jnp.exp2((top - new) * factor)
                top_s[g] = new
                sum_s[g] = sum_s[g] * shrink + weights.sum(0, keepdims=True)
                mix_s[g] = mix_s[g] * shrink + weigh(start, weights)

        for g in range(group):
            out_ref[:, g * head_width:(g + 1) * head_width] = (
                (mix_s[g] / sum_s[g]).T.astype(out_ref.dtype)
            )


def attend(
    query_span, live, home, piece_at, raw, cosine, sine, kv, first, heads, head_width, span_len,
    into=None,
):
    rows = raw.shape[0]
    width = raw.shape[1] // heads
    group = width // head_width
    keys = kv.shape[0]
    slots = rows // span_len
    pieces = piece_at.shape[0] // slots
    piece = span_len // pieces
    held = [] if into is None else [into]

    def raw_spec(b):
        return pl.BlockSpec(
            (piece, width), lambda h, s, qs, lv, hm, at: (at[s * pieces + b], h)
        )

    return pl.pallas_call(
        functools.partial(
            attend_kernel, span_len, pieces, group, head_width,
            head_width ** (-0.5) * math.log2(math.e),
        ),
        grid_spec=pltpu.PrefetchScalarGridSpec(
            num_scalar_prefetch=4,
            grid=(heads, slots),
            in_specs=[raw_spec(b) for b in range(pieces)] + [
                pl.BlockSpec((span_len, head_width), lambda h, s, *_: (s, 0)),
                pl.BlockSpec((span_len, head_width), lambda h, s, *_: (s, 0)),
                pl.BlockSpec((keys, 2 * head_width), lambda h, s, *_: (0, first + h)),
            ] + [pl.BlockSpec(memory_space=pl.ANY)] * len(held),
            out_specs=pl.BlockSpec((span_len, width), lambda h, s, *_: (s, first + h)),
            scratch_shapes=[
                pltpu.VMEM((group, span_len, head_width), jnp.bfloat16),
                pltpu.VMEM((group, 1, span_len), jnp.float32),
                pltpu.VMEM((group, 1, span_len), jnp.float32),
                pltpu.VMEM((group, head_width, span_len), jnp.float32),
            ],
        ),
        out_shape=jax.ShapeDtypeStruct(
            (rows, kv.shape[1] // (2 * head_width) * width), jnp.bfloat16
        ),
        input_output_aliases={4 + pieces + 3: 0} if held else {},
        cost_estimate=pl.CostEstimate(
            flops=4 * rows * heads * group * keys * head_width,
            bytes_accessed=rows * heads * width * 6 + keys * heads * 2 * head_width * 2,
            transcendentals=rows * heads * group * keys,
        ),
        name="attend",
    )(query_span, live, home, piece_at, *([raw] * pieces), cosine, sine, kv, *held)


def homes(key_span):
    places = jnp.arange(key_span.shape[0], dtype=jnp.int32)
    return jnp.sum(
        jnp.where(key_span[None, :] == places[:, None], places[None, :], 0), 1
    )


def local_line(planes, xs, cores, meet_span, span_map, hidden, w_query, w_keyval, stored_kv):
    rows, features = hidden.shape
    span_count = span_map.shape[0]
    heads = w_query.shape[1]
    head_width = stored_kv.shape[2] // 2
    span_len = CH
    slots = rows // span_len
    part = features // planes
    piece = rows // (xs * cores)
    p, x, c = lax.axis_index("seq"), lax.axis_index("head"), lax.axis_index("hold")
    scale = 2.0 ** math.floor(
        math.log2(65504.0 / (features * HIDDEN_BOUND * WEIGHT_BOUND))
    )

    my_spans = lax.dynamic_slice_in_dim(span_map, p * slots, slots, 0)
    offsets = jnp.arange(span_len, dtype=jnp.int32)
    positions = (my_spans[:, None] * span_len + offsets[None, :]).reshape(-1)
    live = (my_spans < meet_span[0]) | (my_spans == span_count - 1)
    cosine, sine = tables(positions, head_width)

    mine = (x * cores + c) * piece

    def share(block, valid):
        got = [block]
        for i in range(1, xs):
            pairs = [
                (q * xs + a, q * xs + (a - i) % xs) for q in valid for a in range(xs)
            ]
            got.append(lax.ppermute(block, ("seq", "head"), pairs))
        half = jnp.concatenate(got, 0)
        out = [half]
        for i in range(1, cores):
            pairs = [
                (q * cores + a, q * cores + (a - i) % cores)
                for q in valid for a in range(cores)
            ]
            out.append(lax.ppermute(half, ("seq", "hold"), pairs))
        return jnp.concatenate(out, 0)

    from_right, from_left = {}, {}
    for k in range(planes - 1, 0, -1):
        for table, sign in ((from_right, 1), (from_left, -1)):
            target = jnp.mod(p - sign * k, planes)
            block = lax.dynamic_slice(hidden, (mine, target * part), (piece, part))
            pairs = [
                (q, q - sign * k) for q in range(planes) if 0 <= q - sign * k < planes
            ]
            table[k] = (lax.ppermute(block, "seq", pairs), [b for _, b in pairs])
    for k in range(planes - 1, 0, -1):
        from_right[k] = share(*from_right[k])
        from_left[k] = share(*from_left[k])
    own = lax.dynamic_slice(hidden, (0, p * part), (rows, part))

    def ordered(value):
        out = []
        for a in range(xs):
            for b in range(cores):
                at = (jnp.mod(b - c, cores) * xs + jnp.mod(a - x, xs)) * piece
                out.append(lax.dynamic_slice_in_dim(value, at, piece, 0))
        return jnp.concatenate(out, 0)

    def project(weights):
        def step(block, arrived):
            total = jnp.dot(block, weights, preferred_element_type=jnp.float32) * scale
            if arrived is not None:
                total = total + arrived.astype(jnp.float32)
            return total.astype(jnp.float16)

        right = left = None
        for k in range(planes - 1, 0, -1):
            send = step(from_right[k], right)
            right = lax.ppermute(send, "seq", [(q, q + 1) for q in range(planes - k)])
            send = step(from_left[k], left)
            left = lax.ppermute(send, "seq", [(q + 1, q) for q in range(k - 1, planes - 1)])
        total = jnp.dot(own, weights, preferred_element_type=jnp.float32)
        if planes > 1:
            others = ordered(right).astype(jnp.float32) + ordered(left).astype(jnp.float32)
            total = total + others * (1.0 / scale)
        return total

    keyval_raw = project(w_keyval.reshape(part, -1)).reshape(rows, heads, 2 * head_width)
    keys_raw = keyval_raw[..., :head_width]
    turned = (
        keys_raw * cosine[:, None, :]
        + jnp.roll(keys_raw, head_width // 2, -1) * sine[:, None, :]
    )
    recomputed = jnp.concatenate([turned, keyval_raw[..., head_width:]], -1).astype(jnp.bfloat16)
    computed_rows = jnp.repeat(live, span_len)
    kv_cache = jnp.where(computed_rows[:, None, None], recomputed, stored_kv)

    kv_own = kv_cache.reshape(rows, -1)
    right, left = kv_own, kv_own
    near_left, near_right = {}, {}
    for k in range(1, planes):
        right = lax.ppermute(right, "seq", [(q, q + 1) for q in range(k - 1, planes - 1)])
        left = lax.ppermute(left, "seq", [(q + 1, q) for q in range(planes - k)])
        near_left[k], near_right[k] = right, left
    kv_all = [kv_own]
    for k in range(1, planes):
        kv_all.append(jnp.where(p + k < planes, near_right[k], near_left[planes - k]))
    kv_all = jnp.concatenate(kv_all, 0)
    order = jnp.mod(p + jnp.arange(planes, dtype=jnp.int32), planes)
    key_span = span_map.reshape(planes, slots)[order].reshape(-1)

    home = homes(key_span)
    piece_at = jnp.arange(slots, dtype=jnp.int32)
    raw = jnp.concatenate([project(w_query[:, h, :]) for h in range(heads)], 1)
    attended = attend(
        my_spans, live.astype(jnp.int32), home, piece_at, raw, cosine, sine, kv_all, 0, heads,
        head_width, span_len,
    ).reshape(rows, heads, -1)
    return attended, kv_cache


def local_four(planes, xs, cores, meet_span, span_map, hidden, w_query, w_keyval, stored_kv):
    return four_body(planes, xs, cores, meet_span, span_map, hidden, w_query, w_keyval, stored_kv)


def four_body(planes, xs, cores, meet_span, span_map, hidden, w_query, w_keyval, stored_kv):
    rows, features = hidden.shape
    span_count = span_map.shape[0]
    heads, width = w_query.shape[1:]
    head_width = stored_kv.shape[2] // 2
    span_len = CH
    slots = rows // span_len
    part = features // planes
    piece = rows // (xs * cores)
    p, x, c = lax.axis_index("seq"), lax.axis_index("head"), lax.axis_index("hold")
    at_end = (p == 0) | (p == planes - 1)
    scale = 2.0 ** math.floor(
        math.log2(65504.0 / (features * HIDDEN_BOUND * WEIGHT_BOUND))
    )
    ends, inner = (0, 3), (1, 2)
    inward = [(0, 1), (3, 2)]
    outward = [(1, 0), (2, 3)]
    across = [(1, 2), (2, 1)]

    def send(value, pairs, axis="seq"):
        return lax.ppermute(value, axis, pairs)

    my_spans = lax.dynamic_slice_in_dim(span_map, p * slots, slots, 0)
    offsets = jnp.arange(span_len, dtype=jnp.int32)
    positions = (my_spans[:, None] * span_len + offsets[None, :]).reshape(-1)
    live = (my_spans < meet_span[0]) | (my_spans == span_count - 1)

    def piece_start(i, j):
        return (jnp.mod(x + i, xs) * cores + jnp.mod(c + j, cores)) * piece

    grid = [(i, j) for i in range(xs) for j in range(cores)]
    piece_at = jnp.stack(
        [jnp.mod(a - x, xs) * cores + jnp.mod(b - c, cores) for a, b in grid]
    ).astype(jnp.int32)

    def share_x(block, where):
        got = [block]
        for i in range(1, xs):
            pairs = [(q * xs + a, q * xs + (a - i) % xs) for q in where for a in range(xs)]
            got.append(send(block, pairs, ("seq", "head")))
        return jnp.concatenate(got, 0)

    def share_c(half, where):
        parts = [half]
        for j in range(1, cores):
            pairs = [
                (q * cores + a, q * cores + (a - j) % cores) for q in where for a in range(cores)
            ]
            parts.append(send(half, pairs, ("seq", "hold")))
        return jnp.concatenate(
            [parts[j][i * piece:(i + 1) * piece] for i, j in grid], 0
        )

    def slice_for(m, plane):
        return lax.dynamic_slice(
            hidden, (piece_start(0, 0), jnp.bitwise_xor(plane, m) * part), (piece, part)
        )

    for_far, later = lax.optimization_barrier((slice_for(3, p), p))
    for_near, for_mid = slice_for(1, later), slice_for(2, later)
    far_end = send(for_far, [(0, 3), (3, 0)])
    near = send(for_near, [(q, q ^ 1) for q in range(planes)])
    mid_end = send(for_mid, [(1, 3), (2, 0)])
    mid_inner = send(for_mid, [(0, 2), (3, 1)])
    far_inner = send(for_far, across)

    own = jnp.concatenate(
        [lax.dynamic_slice(hidden, (piece_start(i, j), p * part), (piece, part)) for i, j in grid], 0
    )
    order = jnp.bitwise_xor(p, jnp.arange(planes, dtype=jnp.int32))
    key_span = span_map.reshape(planes, slots)[order].reshape(-1)
    home = homes(key_span)
    stored_rows = stored_kv.reshape(rows, -1)
    cosine, sine = tables(positions, head_width)
    whole_keyval = w_keyval.reshape(part, -1)
    far_end, whole_keyval, cosine, sine, stored_rows, home = lax.optimization_barrier(
        (far_end, whole_keyval, cosine, sine, stored_rows, home)
    )
    far_half = share_x(far_end, ends)
    late_query, own = lax.optimization_barrier((w_query, own))
    far_half, whole_query = lax.optimization_barrier((far_half, late_query.reshape(part, -1)))
    far_end = share_c(far_half, ends)
    near = share_c(share_x(near, range(planes)), range(planes))
    mid = jnp.where(at_end, mid_end, mid_inner)
    mid = share_c(share_x(mid, range(planes)), range(planes))
    far_inner = share_c(share_x(far_inner, inner), inner)

    def project(weights, splits):
        def product(block, columns=weights):
            total = jnp.dot(block, columns, preferred_element_type=jnp.float32)
            return (total * scale).astype(jnp.float16)

        def plus(a, b):
            return (a.astype(jnp.float32) + b.astype(jnp.float32)).astype(jnp.float16)

        mid_term = product(mid)
        near_term = product(near)
        got_far = send(product(far_end), inward)
        got_near = send(near_term, inward)
        got_mid = send(mid_term, inward)
        got_cross = send(plus(mid_term, got_far), across)
        totals, got_outs = [], []
        step = weights.shape[1] // splits
        for i in range(splits):
            at = slice(i * step, (i + 1) * step)
            if i:
                near_term, got_cross, pair_term = lax.optimization_barrier(
                    (near_term, got_cross, pair_term)
                )
            got_out = send(plus(near_term[:, at], got_cross[:, at]), outward)
            got_outs.append(got_out)
            pair_term = plus(product(far_inner, weights[:, at]), got_mid[:, at])
            got_pair = send(pair_term, across)
            others = (
                got_near[:, at].astype(jnp.float32) + got_pair.astype(jnp.float32)
                + got_out.astype(jnp.float32)
            )
            total = jnp.dot(own, weights[:, at], preferred_element_type=jnp.float32)
            totals.append((lax.optimization_barrier(total), others * (1.0 / scale)))
        return totals, got_outs

    computed_rows = jnp.repeat(live, span_len)

    def finish(raw):
        raw = jnp.concatenate(
            [
                lax.dynamic_slice_in_dim(raw, piece_at[i] * piece, piece, 0)
                for i in range(xs * cores)
            ],
            0,
        )
        parts = []
        for h in range(heads):
            keys = raw[:, 2 * h * head_width:(2 * h + 1) * head_width]
            parts.append(keys * cosine + jnp.roll(keys, head_width // 2, -1) * sine)
            parts.append(raw[:, (2 * h + 1) * head_width:(2 * h + 2) * head_width])
        recomputed = jnp.concatenate(parts, -1).astype(jnp.bfloat16)
        return jnp.where(computed_rows[:, None], recomputed, stored_rows)

    ((own_total, others),), (got_out,) = project(whole_keyval, 1)
    end_raw = own_total + got_out.astype(jnp.float32) * (1.0 / scale)
    end_own = finish(end_raw)
    own_total, end_own = lax.optimization_barrier((own_total, end_own))
    end_kv = send(end_own, inward)
    kv_own = finish(own_total + others)
    kv_cache = kv_own.reshape(stored_kv.shape)

    cross_kv = send(kv_own, across)
    near_kv = send(kv_own, outward)
    far_kv = send(end_kv, across)
    rest_cross = send(cross_kv, outward)
    rest_far = send(far_kv, outward)
    first = jnp.where(at_end, near_kv, end_kv)
    second = jnp.where(at_end, rest_cross, far_kv)
    kv_all = jnp.concatenate(
        [kv_own, first, second, jnp.where(at_end, rest_far, cross_kv)], 0
    )
    live_int = live.astype(jnp.int32)
    attended = None
    for h, (own_total, others) in enumerate(project(whole_query, heads)[0]):
        if h:
            own_total, raw = lax.optimization_barrier((own_total, raw))
        raw = own_total + others
        attended = attend(
            my_spans, live_int, home, piece_at, raw, cosine, sine, kv_all, h, 1,
            head_width, span_len, attended,
        )
    attended = attended.reshape(rows, heads, width)
    return attended, kv_cache


def fits_four(planes, xs, rows, heads):
    return planes == 4 and (rows // xs) % CH == 0 and heads == 2


def local(planes, xs, cores, *args):
    four = fits_four(planes, xs, args[2].shape[0], args[3].shape[1])
    return (local_four if four else local_line)(planes, xs, cores, *args)


def solution(mesh):
    shape = dict(mesh.shape)
    return jax.shard_map(
        functools.partial(local, shape["seq"], shape["head"], shape["hold"]),
        mesh=mesh,
        in_specs=(
            P("grp"),
            P("grp"),
            P(("grp", "seq"), None),
            P("seq", ("head", "hold"), None),
            P("seq", ("head", "hold"), None),
            P(("grp", "seq"), ("head", "hold"), None),
        ),
        out_specs=(
            P(("grp", "seq"), ("head", "hold"), None),
            P(("grp", "seq"), ("head", "hold"), None),
        ),
        check_vma=False,
    )
```
